512 devices in a mesh: bg: 128 (over y, z, core), sp: 4 (over x).
Axes of the slice: x: 4, y: 8, z: 8, core: 2. Of those that a mesh axis runs over, the one named last changes fastest.
Arguments:
- covariates: bfloat16 [65536, 256], P(('bg', 'sp')), may hold values from -6 to 6
- first_weight: bfloat16 [8, 128, 128], replicated, may hold values from -0.5 to 0.5
- first_bias: float32 [1024], replicated, may hold values from -3 to 3
- first_index: int32 [8], replicated, may hold values from 0 to 1
- second_weight: bfloat16 [8, 128, 128], replicated, may hold values from -0.5 to 0.5
- second_bias: float32 [1024], replicated, may hold values from -3 to 3
- second_index: int32 [8], replicated, may hold values from 0 to 7
- head_weight: bfloat16 [80, 64, 128], P('sp'), may hold values from -150 to 150
- clade_block: int32 [80], P('sp'), may hold values from 0 to 15
- presence: int32 [10240, 16], P('sp'), may hold values from 0 to 65535, as said below
Outputs:
- species_loss: float32 [10240], P('sp')
- head_grad: float32 [80, 64, 128], P('sp')
- first_grad: float32 [8, 128, 128], replicated
- first_bias_grad: float32 [1024], replicated
- second_grad: float32 [8, 128, 128], replicated
- second_bias_grad: float32 [1024], replicated
The draws below stay inside these ranges and needn't reach their ends.
Inputs may be any that keep to these rules, and one draw needn't show every extreme that they name: `presence`: the records of one species lie within 128 consecutive cells; cells may repeat.
All inputs are finite; a program needn't handle non-finite values.
Results may differ from the reference program's by a relative error of at most 0.014.
Values may be sent and summed in bfloat16 or wider, within the bound.
No kernel may reach another device: no remote copies, remote signals or barrier semaphores. Data moves between devices by JAX's collectives and lax.ppermute only.
A program may use at most 64 MiB of HBM per device.

```python
import math
import jax
import jax.numpy as jnp
from jax import lax

COVAR = 256
WIDTH = 1024
TILE = 128
SLAB = 64
SPBLOCK = 128
SPEC_DEV = 2560
PRES = 16
TRUNK_DEV = 128
CELLS = 65536
SPECIES = 10240
N_SP = 4


def draw_head_weight(key, part):
    first_key, second_key = jax.random.split(key, 2)
    shape = (SPECIES // SPBLOCK, SLAB, SPBLOCK)
    values = jnp.clip(jax.random.normal(first_key, shape, jnp.float32), -6.0, 6.0)
    log_scale = jax.random.uniform(second_key, (SPECIES // SPBLOCK, 1, SPBLOCK), jnp.float32, math.log(0.5), math.log(5.0))
    scale = jnp.exp(log_scale)
    return (values * scale / math.sqrt(SLAB)).astype(jnp.bfloat16)


def draw_presence(key, part):
    center_key, offset_key = jax.random.split(jax.random.fold_in(key, 7), 2)
    centers = jax.random.randint(center_key, (SPECIES, 1), 0, CELLS - TRUNK_DEV + 1, dtype=jnp.int32)
    offsets = jax.random.randint(offset_key, (SPECIES, PRES), 0, TRUNK_DEV, dtype=jnp.int32)
    centers = centers.at[0, 0].set(0).at[1, 0].set(CELLS - TRUNK_DEV)
    offsets = offsets.at[0, 0].set(0).at[1, 0].set(TRUNK_DEV - 1)
    return (centers + offsets).astype(jnp.int32)


def touch_ends(result, own_key, least, largest):
    longest = result.shape.index(max(result.shape))
    spots = []
    for shift in (0, 1):
        where = [jax.random.randint(jax.random.fold_in(own_key, axis), (), 0, length) for axis, length in enumerate(result.shape)]
        where[longest] = (where[longest] + shift) % result.shape[longest]
        spots.append(tuple(where))
    return result.at[spots[0]].set(least).at[spots[1]].set(largest)


def shard_levels(stream_key, shape, cuts, smallest, largest):
    gain, own = 1.0, jax.random.fold_in(stream_key, 6)
    for position, shards_of in cuts:
        draws = jnp.exp(jax.random.uniform(jax.random.fold_in(own, position), (shards_of,), jnp.float32, smallest / len(cuts), largest / len(cuts)))
        gain = gain * jnp.repeat(draws, shape[position] // shards_of).reshape([-1 if axis == position else 1 for axis in range(len(shape))])
    return gain


def centred(stream_key, dims, scale, limit, cuts=(), kind=jnp.bfloat16):
    values = scale * jax.random.normal(stream_key, dims, jnp.float32)
    if cuts:
        values = values * shard_levels(stream_key, dims, cuts, -0.22, 0.18)
    return jnp.clip(values, -limit, limit).astype(kind)


def setup_inputs(seed: int = 0) -> dict:
    streams_of = jax.random.split(jax.random.key(seed), 11)
    return {
        "covariates": centred(streams_of[0], (CELLS, COVAR), 1.0, 6.0, ((0, 512),)),
        "first_weight": centred(streams_of[1], (WIDTH // TILE, TILE, TILE), TILE ** -0.5, 0.5),
        "first_bias": centred(streams_of[2], (WIDTH,), 0.5, 3.0, (), jnp.float32),
        "first_index": touch_ends(jax.random.randint(streams_of[3], (WIDTH // TILE,), 0, COVAR // TILE), jax.random.fold_in(streams_of[3], 1), 0, (COVAR // TILE) - 1).astype(jnp.int32),
        "second_weight": centred(streams_of[4], (WIDTH // TILE, TILE, TILE), TILE ** -0.5, 0.5),
        "second_bias": centred(streams_of[5], (WIDTH,), 0.5, 3.0, (), jnp.float32),
        "second_index": touch_ends(jax.random.randint(streams_of[6], (WIDTH // TILE,), 0, WIDTH // TILE), jax.random.fold_in(streams_of[6], 1), 0, (WIDTH // TILE) - 1).astype(jnp.int32),
        "head_weight": draw_head_weight(jax.random.fold_in(streams_of[10], 71), 0),
        "clade_block": touch_ends(jax.random.randint(streams_of[8], (SPECIES // SPBLOCK,), 0, WIDTH // SLAB), jax.random.fold_in(streams_of[8], 1), 0, (WIDTH // SLAB) - 1).astype(jnp.int32),
        "presence": draw_presence(jax.random.fold_in(streams_of[10], 71), 0),
    }


def silu_slope(values):
    sigma = jax.nn.sigmoid(values)
    return sigma * (1.0 + values * (1.0 - sigma))


def trunk_forward(covariates, first_weight, first_bias, first_index, second_weight, second_bias, second_index):
    row_count = covariates.shape[0]
    blocks = first_weight.shape[0]
    tile_size = first_weight.shape[1]
    inputs = jnp.take(covariates.reshape(row_count, -1, tile_size), first_index, axis=1)
    first_pre = jnp.einsum("rot,oti->roi", inputs.astype(jnp.float32), first_weight.astype(jnp.float32), precision=lax.Precision.HIGHEST) + first_bias.reshape(blocks, tile_size)
    first_act = jax.nn.silu(first_pre).astype(jnp.bfloat16)
    middle = jnp.take(first_act, second_index, axis=1)
    second_pre = jnp.einsum("rot,oti->roi", middle.astype(jnp.float32), second_weight.astype(jnp.float32), precision=lax.Precision.HIGHEST) + second_bias.reshape(blocks, tile_size)
    features = jax.nn.silu(second_pre).astype(jnp.bfloat16).reshape(row_count, blocks * tile_size)
    return inputs, first_pre, middle, second_pre, features


def trunk_backward(feature_grad, inputs, first_pre, middle, second_pre, second_weight, second_index):
    row_count, blocks, tile_size = first_pre.shape
    second_dz = (feature_grad.reshape(row_count, blocks, tile_size) * silu_slope(second_pre)).astype(jnp.bfloat16)
    second_grad = jnp.einsum("rot,roi->oti", middle.astype(jnp.float32), second_dz.astype(jnp.float32), precision=lax.Precision.HIGHEST)
    second_bias_grad = jnp.sum(second_dz.astype(jnp.float32), axis=0).reshape(-1)
    spread = jnp.einsum("roi,oti->rot", second_dz.astype(jnp.float32), second_weight.astype(jnp.float32), precision=lax.Precision.HIGHEST)
    onehot = (second_index[:, None] == jnp.arange(blocks, dtype=jnp.int32)[None, :]).astype(jnp.float32)
    first_act_grad = jnp.einsum("rot,op->rpt", spread, onehot, precision=lax.Precision.HIGHEST)
    first_dz = (first_act_grad * silu_slope(first_pre)).astype(jnp.bfloat16)
    first_grad = jnp.einsum("rot,roi->oti", inputs.astype(jnp.float32), first_dz.astype(jnp.float32), precision=lax.Precision.HIGHEST)
    first_bias_grad = jnp.sum(first_dz.astype(jnp.float32), axis=0).reshape(-1)
    return first_grad, first_bias_grad, second_grad, second_bias_grad


def reference(covariates, first_weight, first_bias, first_index, second_weight, second_bias, second_index, head_weight, clade_block, presence):
    inputs, first_pre, middle, second_pre, features = trunk_forward(covariates, first_weight, first_bias, first_index, second_weight, second_bias, second_index)
    group_blocks = SPEC_DEV // SPBLOCK
    columns = jnp.broadcast_to(jnp.arange(SPBLOCK, dtype=jnp.int32)[:, None], (SPBLOCK, PRES))

    def block_step(accumulated, block):
        column_start = clade_block[block] * SLAB
        feature_slab = lax.dynamic_slice_in_dim(features, column_start, SLAB, 1)
        weights = head_weight[block].astype(jnp.float32)
        logits = jnp.dot(feature_slab.astype(jnp.float32), weights, precision=lax.Precision.HIGHEST)
        highest = jnp.max(logits, axis=0)
        partition = jnp.sum(jnp.exp(logits - highest[None, :]), axis=0)
        records = lax.dynamic_slice_in_dim(presence, block * SPBLOCK, SPBLOCK, 0)
        hits = jnp.zeros((CELLS, SPBLOCK), jnp.float32).at[records, columns].add(1.0)
        presence_sum = jnp.sum(hits * logits, axis=0)
        species_loss = highest + jnp.log(partition) - math.log(CELLS) - presence_sum / PRES
        weight_cells = (jnp.exp(logits - highest[None, :]) / partition[None, :] - hits / PRES).astype(jnp.bfloat16)
        block_grad = jnp.einsum("cf,cs->fs", feature_slab.astype(jnp.float32), weight_cells.astype(jnp.float32), precision=lax.Precision.HIGHEST)
        feature_back = jnp.einsum("cs,fs->cf", weight_cells.astype(jnp.float32), weights, precision=lax.Precision.HIGHEST)
        current = lax.dynamic_slice_in_dim(accumulated, column_start, SLAB, 1)
        accumulated = lax.dynamic_update_slice_in_dim(accumulated, current + feature_back, column_start, 1)
        return accumulated, (species_loss, block_grad)

    feature_grad = jnp.zeros((CELLS, WIDTH), jnp.float32)
    loss_parts = []
    grad_parts = []
    for group in range(N_SP):
        block_ids = jnp.arange(group * group_blocks, (group + 1) * group_blocks, dtype=jnp.int32)
        group_back, (species_loss, block_grad) = lax.scan(block_step, jnp.zeros((CELLS, WIDTH), jnp.float32), block_ids)
        rounded = lax.optimization_barrier(group_back.astype(jnp.bfloat16))
        feature_grad = feature_grad + rounded.astype(jnp.float32)
        loss_parts.append(species_loss.reshape(-1))
        grad_parts.append(block_grad)
    first_grad, first_bias_grad, second_grad, second_bias_grad = trunk_backward(feature_grad, inputs, first_pre, middle, second_pre, second_weight, second_index)
    return (jnp.concatenate(loss_parts, axis=0), jnp.concatenate(grad_parts, axis=0), first_grad, first_bias_grad, second_grad, second_bias_grad)
```

```python
import math

import jax
import jax.numpy as jnp
from jax import lax
from jax.experimental import pallas as pl
from jax.experimental.pallas import tpu as pltpu
from jax.sharding import Mesh, PartitionSpec as P

BF16 = jnp.bfloat16
F32 = jnp.float32
CHUNK = 128
LINK = BF16
VMEM = pl.BlockSpec(memory_space=pltpu.VMEM)
SMEM = pl.BlockSpec(memory_space=pltpu.SMEM)
PARAMS = pltpu.CompilerParams(vmem_limit_bytes=56 << 20)


def dot(a, b):
    return jnp.dot(a, b, preferred_element_type=F32)


def dot_t(a, b):
    return lax.dot_general(a, b, (((1,), (1,)), ((), ())), preferred_element_type=F32)


def hits_of(presence_ref, lanes, first_row):
    rows = first_row + lax.broadcasted_iota(jnp.int32, (CHUNK, lanes.size), 0)
    hits = jnp.zeros((CHUNK, lanes.size), F32)
    for record in range(presence_ref.shape[0]):
        hits += jnp.where(rows == presence_ref[record : record + 1, lanes], 1.0, 0.0)
    return hits


def forward_kernel(
    first_index,
    second_index,
    clade,
    busy,
    place,
    covariates,
    first_weight,
    first_bias,
    second_weight,
    second_bias,
    head_weight,
    presence,
    shifted,
    high,
    local_lse,
    hit_sum,
    features,
    first_act,
    first_slope,
    second_slope,
    wide_weight,
    logits,
):
    blocks, cells, tile = features.shape
    block_count, slab, _ = head_weight.shape
    first_cell = place[0]

    def layer(pre, act_ref, slope_ref, o):
        sigma = 1.0 / (1.0 + jnp.exp(-pre))
        act_ref[o] = (pre * sigma).astype(BF16)
        slope_ref[o] = sigma * (1.0 + pre * (1.0 - sigma))

    for o in range(blocks):
        columns = pl.ds(pl.multiple_of(first_index[o] * tile, tile), tile)
        pre = dot(covariates[:, columns], first_weight[o]) + first_bias[o : o + 1, :]
        layer(pre, first_act, first_slope, o)
    for o in range(blocks):
        pre = dot(first_act[second_index[o]], second_weight[o]) + second_bias[o : o + 1, :]
        layer(pre, features, second_slope, o)

    hit_sum[...] = jnp.zeros_like(hit_sum)
    wide_weight[...] = jnp.zeros_like(wide_weight)

    def step(b, carry):
        spot = clade[b]
        half = pl.ds(pl.multiple_of((spot % 2) * slab, slab), slab)
        lanes = pl.ds(pl.multiple_of(b * tile, tile), tile)
        row = pl.ds(b, 1)
        wide_weight[b, half, :] = head_weight[b]
        logits[...] = dot(features[spot // 2], wide_weight[b])
        top = jnp.max(logits[...], axis=0, keepdims=True)
        terms = jnp.exp(logits[...] - top)
        shifted[b] = terms
        high[row, :] = top
        local_lse[row, :] = top + jnp.log(jnp.sum(terms, axis=0, keepdims=True))
        for k in range(cells // CHUNK):

            @pl.when(busy[b * (cells // CHUNK) + k] > 0)
            def _():
                hits = hits_of(presence, lanes, first_cell + k * CHUNK)
                part = hits * logits[k * CHUNK : (k + 1) * CHUNK, :]
                hit_sum[row, :] += jnp.sum(part, axis=0, keepdims=True)

        return carry

    lax.fori_loop(0, block_count, step, 0)


def backward_kernel(
    first_index,
    second_index,
    clade,
    busy,
    place,
    covariates,
    second_weight,
    presence,
    shifted,
    high,
    lse,
    hit_sum,
    features,
    first_act,
    first_slope,
    second_slope,
    wide_weight,
    keep,
    send,
    packed,
    features_t,
    first_act_t,
    covariates_t,
    weight_cells,
    slab_grad,
    group_back,
    act_grad,
):
    blocks, cells, tile = features.shape
    block_count = wide_weight.shape[0]
    slab = tile // 2
    records = presence.shape[0]
    first_cell = place[0]
    parts = packed.shape[0]
    head_rows = block_count * slab // parts
    piece = math.gcd(slab, head_rows)

    for o in range(blocks):
        features_t[o] = features[o].T
        first_act_t[o] = first_act[o].T
    for o in range(covariates.shape[1] // tile):
        covariates_t[o] = covariates[:, o * tile : (o + 1) * tile].T
    group_back[...] = jnp.zeros_like(group_back)
    act_grad[...] = jnp.zeros_like(act_grad)

    def step(b, carry):
        spot = clade[b]
        lanes = pl.ds(pl.multiple_of(b * tile, tile), tile)
        row = pl.ds(b, 1)
        scale = jnp.exp(high[row, :] - lse[row, :])
        weight_cells[...] = (shifted[b] * scale).astype(BF16)
        for k in range(cells // CHUNK):

            @pl.when(busy[b * (cells // CHUNK) + k] > 0)
            def _():
                hits = hits_of(presence, lanes, first_cell + k * CHUNK)
                rows = slice(k * CHUNK, (k + 1) * CHUNK)
                weights = shifted[b, rows, :] * scale - hits * (1.0 / records)
                weight_cells[rows, :] = weights.astype(BF16)

        slab_grad[...] = dot(features_t[spot // 2], weight_cells[...])
        for j in range(slab // piece):
            q = b * (slab // piece) + j
            source = pl.ds(pl.multiple_of((spot % 2) * slab + j * piece, piece), piece)
            target = pl.ds(pl.multiple_of(tile + (q % (head_rows // piece)) * piece, piece), piece)
            packed[q // (head_rows // piece), target, :] = slab_grad[source, :]
        group_back[spot // 2] += dot_t(weight_cells[...], wide_weight[b])
        return carry

    lax.fori_loop(0, block_count, step, 0)

    bias_row = tile + head_rows
    packed[:, bias_row:, :] = jnp.zeros((parts, packed.shape[1] - bias_row, tile), F32)
    for o in range(blocks):
        dz = (group_back[o] * second_slope[o]).astype(BF16)
        packed[blocks + o, :tile, :] = dot(first_act_t[second_index[o]], dz)
        packed[blocks + o, bias_row : bias_row + 1, :] = jnp.sum(
            dz.astype(F32), axis=0, keepdims=True
        )
        act_grad[second_index[o]] += dot_t(dz, second_weight[o])
    for o in range(blocks):
        dz = (act_grad[o] * first_slope[o]).astype(BF16)
        packed[o, :tile, :] = dot(covariates_t[first_index[o]], dz)
        packed[o, bias_row : bias_row + 1, :] = jnp.sum(dz.astype(F32), axis=0, keepdims=True)
    for b in range(block_count):
        spot = bias_row + 1 + b % 2
        packed[b // 2, spot : spot + 1, :] = hit_sum[b : b + 1, :]

    core = place[1]
    for o in range(blocks):
        keep[o] = packed[core * blocks + o]
        send[o] = packed[(1 - core) * blocks + o]


def spread(value, axis, size):
    return lax.all_to_all(jnp.broadcast_to(value[None], (size, *value.shape)), axis, 0, 0)


def join(parts):
    top = jnp.max(parts, axis=0)
    return top + jnp.log(jnp.sum(jnp.exp(parts - top), axis=0))


def body(
    covariates,
    first_weight,
    first_bias,
    first_index,
    second_weight,
    second_bias,
    second_index,
    head_weight,
    clade_block,
    presence,
):
    ny, nz, nx = lax.axis_size("y"), lax.axis_size("z"), lax.axis_size("x")
    core, mine = lax.axis_index("c"), lax.axis_index("x")
    swap = [(0, 1), (1, 0)]
    blocks, tile, _ = first_weight.shape
    block_count, slab, species = head_weight.shape
    records = presence.shape[1]
    own_cells, width = covariates.shape
    cells = own_cells * nx
    first_cell = ((lax.axis_index("y") * nz + lax.axis_index("z")) * 2 + core) * cells
    total_cells = ny * nz * 2 * cells

    presence_t = presence.T
    chunk_of = lax.shift_right_arithmetic(presence_t - first_cell, int(math.log2(CHUNK)))
    chunk_of = chunk_of.reshape(records, block_count, species)
    busy = jnp.stack(
        [jnp.any(chunk_of == k, axis=(0, 2)) for k in range(cells // CHUNK)], axis=1
    )
    busy = busy.astype(jnp.int32).reshape(-1)
    place = jnp.stack([first_cell, core]).astype(jnp.int32)
    scalars = (first_index, second_index, clade_block, busy, place)

    all_covariates = spread(covariates, "x", nx).reshape(cells, width)
    by_block = (blocks, cells, tile)
    shape = jax.ShapeDtypeStruct
    shifted, high, local_lse, hit_sum, features, first_act, first_slope, second_slope, wide = (
        pl.pallas_call(
            forward_kernel,
            name="forward",
            out_shape=(
                shape((block_count, cells, species), F32),
                shape((block_count, species), F32),
                shape((block_count, species), F32),
                shape((block_count, species), F32),
                shape(by_block, BF16),
                shape(by_block, BF16),
                shape(by_block, F32),
                shape(by_block, F32),
                shape((block_count, tile, species), BF16),
            ),
            in_specs=[SMEM] * 5 + [VMEM] * 7,
            out_specs=[VMEM] * 9,
            scratch_shapes=[pltpu.VMEM((cells, species), F32)],
            compiler_params=PARAMS,
        )(
            *scalars,
            all_covariates,
            first_weight,
            first_bias.reshape(blocks, tile),
            second_weight,
            second_bias.reshape(blocks, tile),
            head_weight,
            presence_t,
        )
    )

    lse = join(jnp.stack([local_lse, lax.ppermute(local_lse, "c", swap)]))
    lse = join(spread(lse, "y", ny))
    lse = join(spread(lse, "z", nz))

    parts = 2 * ny
    head_rows = block_count * slab // parts
    part_rows = -(-(tile + head_rows + 3) // 8) * 8
    keep, send = pl.pallas_call(
        backward_kernel,
        name="backward",
        out_shape=(
            shape((ny, part_rows, tile), F32),
            shape((ny, part_rows, tile), F32),
        ),
        in_specs=[SMEM] * 5 + [VMEM] * 12,
        out_specs=[VMEM] * 2,
        scratch_shapes=[
            pltpu.VMEM((parts, part_rows, tile), F32),
            pltpu.VMEM((blocks, tile, cells), BF16),
            pltpu.VMEM((blocks, tile, cells), BF16),
            pltpu.VMEM((width // tile, tile, cells), BF16),
            pltpu.VMEM((cells, species), BF16),
            pltpu.VMEM((tile, species), F32),
            pltpu.VMEM(by_block, F32),
            pltpu.VMEM(by_block, F32),
        ],
        compiler_params=PARAMS,
    )(
        *scalars,
        all_covariates,
        second_weight,
        presence_t,
        shifted,
        high,
        lse,
        hit_sum,
        features,
        first_act,
        first_slope,
        second_slope,
        wide,
    )

    total = keep + lax.ppermute(send, "c", swap)
    rounded = lax.reduce_precision(total, 8, 7)
    rest = (total - rounded)[:, tile : tile + head_rows]
    total = jnp.concatenate([rounded.astype(LINK), rest.astype(LINK)], axis=1)
    total = jnp.sum(lax.all_to_all(total, "y", 0, 0).astype(F32), axis=0)
    total_head = (total[tile : tile + head_rows] + total[part_rows:]).astype(LINK)
    total = total[:part_rows].astype(LINK)
    trunk_cut, head_cut = tile // (nz * nx), head_rows // nz
    pieces = [
        total[:tile].reshape(nz, nx, trunk_cut, tile),
        jnp.broadcast_to(
            total_head.reshape(nz, 1, head_cut, tile),
            (nz, nx, head_cut, tile),
        ),
        jnp.broadcast_to(total[tile + head_rows :], (nz, nx, part_rows - tile - head_rows, tile)),
    ]
    cut = jnp.concatenate(pieces, axis=2)
    cut_rows = -(-cut.shape[2] // 8) * 8
    cut = jnp.pad(cut, ((0, 0), (0, 0), (0, cut_rows - cut.shape[2]), (0, 0)))
    cut = lax.all_to_all(cut.reshape(nz * nx, cut_rows, tile), ("z", "x"), 0, 0)
    cut = cut.reshape(nz, nx, cut_rows, tile).astype(F32)
    over_z = jnp.sum(lax.dynamic_index_in_dim(cut, mine, 1, False), axis=0)
    over_both = jnp.sum(cut, axis=(0, 1))
    bias_row = trunk_cut + head_cut
    bias = over_both[bias_row : bias_row + 1]
    hit_part = over_z[bias_row + 1 : bias_row + 3]

    done = jnp.concatenate([over_both[:trunk_cut], over_z[trunk_cut:bias_row]])
    done = jnp.pad(done, ((0, -bias_row % 8), (0, 0))).astype(LINK)
    done = spread(done, ("z", "x"), nz * nx).reshape(nz, nx, -1, tile)
    trunk = done[:, :, :trunk_cut].reshape(tile, tile)
    head = lax.dynamic_index_in_dim(done, mine, 1, False)[:, trunk_cut:bias_row]
    rows = jnp.concatenate(
        [trunk, head.reshape(head_rows, tile), bias.astype(LINK), hit_part.astype(LINK)]
    )
    rows = jnp.pad(rows, ((0, part_rows - rows.shape[0]), (0, 0)))
    rows = spread(rows, "y", ny)
    other = lax.ppermute(rows, "c", swap)
    low = jnp.where(core == 0, rows, other).astype(F32)
    upper = jnp.where(core == 0, other, rows).astype(F32)
    both = jnp.concatenate([low, upper])
    head_grad = both[:, tile : tile + head_rows].reshape(block_count, slab, species)
    hit_total = both[:, tile + head_rows + 1 : tile + head_rows + 3].reshape(parts * 2, tile)
    hit_total = hit_total[:block_count]
    species_loss = (lse - math.log(total_cells) - hit_total / records).reshape(-1)
    return (
        species_loss,
        head_grad,
        low[:, :tile],
        low[:, tile + head_rows].reshape(-1),
        upper[:, :tile],
        upper[:, tile + head_rows].reshape(-1),
    )


def solution(mesh):
    devices = mesh.devices.reshape(8, mesh.shape["bg"] // 16, 2, mesh.shape["sp"])
    torus = Mesh(devices, ("y", "z", "c", "x"))
    placed = (
        P(("y", "z", "c", "x"), None),
        P(),
        P(),
        P(),
        P(),
        P(),
        P(),
        P("x", None, None),
        P("x"),
        P("x", None),
    )
    return jax.shard_map(
        body,
        mesh=torus,
        in_specs=placed,
        out_specs=(P("x"), P("x", None, None), P(), P(), P(), P()),
        check_vma=False,
    )
```

```python
import functools
import math

import jax
import jax.numpy as jnp
from jax import lax
from jax.experimental import pallas as pl
from jax.experimental.pallas import tpu as pltpu
from jax.sharding import Mesh, PartitionSpec as P

BF16 = jnp.bfloat16
F32 = jnp.float32
CHUNK = 128
LINK = BF16
VMEM = pl.BlockSpec(memory_space=pltpu.VMEM)
SMEM = pl.BlockSpec(memory_space=pltpu.SMEM)
PARAMS = pltpu.CompilerParams(vmem_limit_bytes=56 << 20)


def dot(a, b):
    return jnp.dot(a, b, preferred_element_type=F32)


def dot_t(a, b):
    return lax.dot_general(a, b, (((1,), (1,)), ((), ())), preferred_element_type=F32)


def hits_of(presence_ref, lanes, first_row):
    rows = first_row + lax.broadcasted_iota(jnp.int32, (CHUNK, lanes.size), 0)
    hits = jnp.zeros((CHUNK, lanes.size), F32)
    for record in range(presence_ref.shape[0]):
        hits += jnp.where(rows == presence_ref[record : record + 1, lanes], 1.0, 0.0)
    return hits


def forward_kernel(
    first_index,
    second_index,
    clade,
    busy,
    place,
    covariates,
    first_weight,
    first_bias,
    second_weight,
    second_bias,
    head_weight,
    presence,
    shifted,
    high,
    local_lse,
    hit_sum,
    features,
    first_act,
    first_slope,
    second_slope,
    wide_weight,
    logits,
):
    blocks, cells, tile = features.shape
    block_count, slab, _ = head_weight.shape
    first_cell = place[0]

    def layer(pre, act_ref, slope_ref, o):
        sigma = 1.0 / (1.0 + jnp.exp(-pre))
        act_ref[o] = (pre * sigma).astype(BF16)
        slope_ref[o] = sigma * (1.0 + pre * (1.0 - sigma))

    for o in range(blocks):
        columns = pl.ds(pl.multiple_of(first_index[o] * tile, tile), tile)
        pre = dot(covariates[:, columns], first_weight[o]) + first_bias[o : o + 1, :]
        layer(pre, first_act, first_slope, o)
    for o in range(blocks):
        pre = dot(first_act[second_index[o]], second_weight[o]) + second_bias[o : o + 1, :]
        layer(pre, features, second_slope, o)

    hit_sum[...] = jnp.zeros_like(hit_sum)
    wide_weight[...] = jnp.zeros_like(wide_weight)

    def step(b, carry):
        spot = clade[b]
        half = pl.ds(pl.multiple_of((spot % 2) * slab, slab), slab)
        lanes = pl.ds(pl.multiple_of(b * tile, tile), tile)
        row = pl.ds(b, 1)
        wide_weight[b, half, :] = head_weight[b]
        logits[...] = dot(features[spot // 2], wide_weight[b])
        top = jnp.max(logits[...], axis=0, keepdims=True)
        terms = jnp.exp(logits[...] - top)
        shifted[b] = terms
        high[row, :] = top
        local_lse[row, :] = top + jnp.log(jnp.sum(terms, axis=0, keepdims=True))
        for k in range(cells // CHUNK):

            @pl.when(busy[b * (cells // CHUNK) + k] > 0)
            def _():
                hits = hits_of(presence, lanes, first_cell + k * CHUNK)
                part = hits * logits[k * CHUNK : (k + 1) * CHUNK, :]
                hit_sum[row, :] += jnp.sum(part, axis=0, keepdims=True)

        return carry

    lax.fori_loop(0, block_count, step, 0)


def backward_kernel(
    first_index,
    second_index,
    clade,
    busy,
    place,
    covariates,
    second_weight,
    presence,
    shifted,
    high,
    lse,
    hit_sum,
    features,
    first_act,
    first_slope,
    second_slope,
    wide_weight,
    trunk,
    keep,
    send,
    packed,
    bias,
    features_t,
    first_act_t,
    covariates_t,
    weight_cells,
    slab_grad,
    group_back,
    act_grad,
):
    blocks, cells, tile = features.shape
    block_count = wide_weight.shape[0]
    slab = tile // 2
    records = presence.shape[0]
    first_cell = place[0]
    group = block_count // 2
    core = place[1]

    for o in range(blocks):
        features_t[o] = features[o].T
        first_act_t[o] = first_act[o].T
    for o in range(covariates.shape[1] // tile):
        covariates_t[o] = covariates[:, o * tile : (o + 1) * tile].T
    group_back[...] = jnp.zeros_like(group_back)
    act_grad[...] = jnp.zeros_like(act_grad)

    def step(b, carry):
        spot = clade[b]
        lanes = pl.ds(pl.multiple_of(b * tile, tile), tile)
        row = pl.ds(b, 1)
        scale = jnp.exp(high[row, :] - lse[row, :])
        weight_cells[...] = (shifted[b] * scale).astype(BF16)
        for k in range(cells // CHUNK):

            @pl.when(busy[b * (cells // CHUNK) + k] > 0)
            def _():
                hits = hits_of(presence, lanes, first_cell + k * CHUNK)
                rows = slice(k * CHUNK, (k + 1) * CHUNK)
                weights = shifted[b, rows, :] * scale - hits * (1.0 / records)
                weight_cells[rows, :] = weights.astype(BF16)

        slab_grad[...] = dot(features_t[spot // 2], weight_cells[...])
        source = pl.ds(pl.multiple_of((spot % 2) * slab, slab), slab)
        target = pl.ds(pl.multiple_of((b % group) * slab, slab), slab)
        packed[b // group, target, :] = slab_grad[source, :]
        group_back[spot // 2] += dot_t(weight_cells[...], wide_weight[b])
        return carry

    lax.fori_loop(0, block_count, step, 0)

    bias[...] = jnp.zeros_like(bias)
    pair = blocks // (trunk.shape[0] // 2)

    def trunk_sums(o, layer, left, dz):
        part, at = layer * (trunk.shape[0] // 2) + o // pair, o % pair
        trunk[part, at * tile : (at + 1) * tile, :] = dot(left, dz).astype(LINK)
        bias[part, at : at + 1, :] = jnp.sum(dz.astype(F32), axis=0, keepdims=True)

    for o in range(blocks):
        dz = (group_back[o] * second_slope[o]).astype(BF16)
        trunk_sums(o, 1, first_act_t[second_index[o]], dz)
        act_grad[second_index[o]] += dot_t(dz, second_weight[o])
    for o in range(blocks):
        dz = (act_grad[o] * first_slope[o]).astype(BF16)
        trunk_sums(o, 0, covariates_t[first_index[o]], dz)
    for part in range(trunk.shape[0]):
        trunk[part, pair * tile :, :] = bias[part].astype(LINK)

    tail = group * slab
    for half in range(2):
        packed[half, tail:, :] = jnp.zeros((packed.shape[1] - tail, tile), F32)
        packed[half, tail : tail + group, :] = hit_sum[half * group : (half + 1) * group, :]
    keep[...] = packed[core]
    send[...] = packed[1 - core]


def finish_kernel(
    total_cells,
    records,
    place,
    trunk,
    own,
    other,
    lse,
    species_loss,
    head_grad,
    first_grad,
    first_bias_grad,
    second_grad,
    second_bias_grad,
    halves,
):
    core = place[1]
    blocks, tile, _ = first_grad.shape
    block_count, slab, _ = head_grad.shape
    group = block_count // 2
    halves[core] = own[...]
    halves[1 - core] = other[...]
    for b in range(block_count):
        rows = slice((b % group) * slab, (b % group + 1) * slab)
        head_grad[b] = halves[b // group, rows, :].astype(F32)
    tail = group * slab
    for half in range(2):
        rows = slice(half * group, (half + 1) * group)
        hit_mean = halves[half, tail:, :].astype(F32)[:group] * (1.0 / records)
        species_loss[rows, :] = lse[rows, :] - math.log(total_cells) - hit_mean
    half = trunk.shape[0] // 2
    pair = blocks // half
    for layer, (grad, bias_grad) in enumerate(
        ((first_grad, first_bias_grad), (second_grad, second_bias_grad))
    ):
        for part in range(half):
            for at in range(pair):
                rows = slice(at * tile, (at + 1) * tile)
                grad[part * pair + at] = trunk[layer * half + part, rows, :].astype(F32)
            bias = trunk[layer * half + part, pair * tile :, :].astype(F32)
            bias_grad[part * pair : (part + 1) * pair, :] = bias[:pair]


def spread(value, axis, size):
    return lax.all_to_all(jnp.broadcast_to(value[None], (size, *value.shape)), axis, 0, 0)


def join(parts):
    top = jnp.max(parts, axis=0)
    return top + jnp.log(jnp.sum(jnp.exp(parts - top), axis=0))


def body(
    covariates,
    first_weight,
    first_bias,
    first_index,
    second_weight,
    second_bias,
    second_index,
    head_weight,
    clade_block,
    presence,
):
    ny, nz, nx = lax.axis_size("y"), lax.axis_size("z"), lax.axis_size("x")
    core, mine = lax.axis_index("c"), lax.axis_index("x")
    swap = [(0, 1), (1, 0)]
    blocks, tile, _ = first_weight.shape
    block_count, slab, species = head_weight.shape
    records = presence.shape[1]
    own_cells, width = covariates.shape
    cells = own_cells * nx
    first_cell = ((lax.axis_index("y") * nz + lax.axis_index("z")) * 2 + core) * cells
    total_cells = ny * nz * 2 * cells

    presence_t = presence.T
    chunk_of = lax.shift_right_arithmetic(presence_t - first_cell, int(math.log2(CHUNK)))
    chunk_of = chunk_of.reshape(records, block_count, species)
    busy = jnp.stack(
        [jnp.any(chunk_of == k, axis=(0, 2)) for k in range(cells // CHUNK)], axis=1
    )
    busy = busy.astype(jnp.int32).reshape(-1)
    place = jnp.stack([first_cell, core]).astype(jnp.int32)
    scalars = (first_index, second_index, clade_block, busy, place)

    all_covariates = spread(covariates, "x", nx).reshape(cells, width)
    by_block = (blocks, cells, tile)
    shape = jax.ShapeDtypeStruct
    shifted, high, local_lse, hit_sum, features, first_act, first_slope, second_slope, wide = (
        pl.pallas_call(
            forward_kernel,
            name="forward",
            out_shape=(
                shape((block_count, cells, species), F32),
                shape((block_count, species), F32),
                shape((block_count, species), F32),
                shape((block_count, species), F32),
                shape(by_block, BF16),
                shape(by_block, BF16),
                shape(by_block, F32),
                shape(by_block, F32),
                shape((block_count, tile, species), BF16),
            ),
            in_specs=[SMEM] * 5 + [VMEM] * 7,
            out_specs=[VMEM] * 9,
            scratch_shapes=[pltpu.VMEM((cells, species), F32)],
            compiler_params=PARAMS,
        )(
            *scalars,
            all_covariates,
            first_weight,
            first_bias.reshape(blocks, tile),
            second_weight,
            second_bias.reshape(blocks, tile),
            head_weight,
            presence_t,
        )
    )

    lse = join(spread(local_lse, "y", ny))
    lse = join(spread(lse, ("z", "c"), nz * 2))

    pair = blocks // nx
    part_rows = pair * tile + 8
    group = block_count // 2
    head_rows = group * slab
    half_rows = head_rows + -(-group // 8) * 8
    trunk, keep, send = pl.pallas_call(
        backward_kernel,
        name="backward",
        out_shape=(
            shape((2 * nx, part_rows, tile), LINK),
            shape((half_rows, tile), F32),
            shape((half_rows, tile), F32),
        ),
        in_specs=[SMEM] * 5 + [VMEM] * 12,
        out_specs=[VMEM] * 3,
        scratch_shapes=[
            pltpu.VMEM((2, half_rows, tile), F32),
            pltpu.VMEM((2 * nx, 8, tile), F32),
            pltpu.VMEM((blocks, tile, cells), BF16),
            pltpu.VMEM((blocks, tile, cells), BF16),
            pltpu.VMEM((width // tile, tile, cells), BF16),
            pltpu.VMEM((cells, species), BF16),
            pltpu.VMEM((tile, species), F32),
            pltpu.VMEM(by_block, F32),
            pltpu.VMEM(by_block, F32),
        ],
        compiler_params=PARAMS,
    )(
        *scalars,
        all_covariates,
        second_weight,
        presence_t,
        shifted,
        high,
        lse,
        hit_sum,
        features,
        first_act,
        first_slope,
        second_slope,
        wide,
    )

    head = keep + lax.ppermute(send, "c", swap)
    trunk = jnp.sum(lax.all_to_all(trunk, ("c", "x"), 0, 0).astype(F32), axis=0)
    peers = ny * nz
    misc = jnp.concatenate([head[head_rows : head_rows + group], trunk[pair * tile :][:pair]])
    misc = jnp.pad(misc, ((0, peers - misc.shape[0]), (0, 0)))
    trunk_cut, head_cut = pair * tile // peers, head_rows // peers
    cut = jnp.concatenate(
        [
            trunk[: pair * tile].reshape(peers, trunk_cut, tile),
            head[:head_rows].reshape(peers, head_cut, tile),
            misc[:, None],
        ],
        axis=1,
    )
    cut = jnp.pad(cut, ((0, 0), (0, -cut.shape[1] % 8), (0, 0))).astype(LINK)
    cut = jnp.sum(lax.all_to_all(cut, ("y", "z"), 0, 0).astype(F32), axis=0).astype(LINK)

    cut = spread(cut, ("y", "z"), peers)
    misc = cut[:, trunk_cut + head_cut]
    head = jnp.concatenate(
        [
            cut[:, trunk_cut : trunk_cut + head_cut].reshape(head_rows, tile),
            jnp.pad(misc[:group], ((0, -group % 8), (0, 0))),
        ]
    )
    other_head = lax.ppermute(head, "c", swap)
    trunk = jnp.concatenate(
        [
            cut[:, :trunk_cut].reshape(pair * tile, tile),
            jnp.pad(misc[group : group + pair], ((0, -pair % 8), (0, 0))),
        ]
    )
    trunk = spread(trunk, ("c", "x"), 2 * nx)
    species_loss, head_grad, first_grad, first_bias_grad, second_grad, second_bias_grad = (
        pl.pallas_call(
            functools.partial(finish_kernel, total_cells, records),
            name="finish",
            out_shape=(
                shape((block_count, species), F32),
                shape(head_weight.shape, F32),
                shape(first_weight.shape, F32),
                shape((blocks, tile), F32),
                shape(second_weight.shape, F32),
                shape((blocks, tile), F32),
            ),
            in_specs=[SMEM] + [VMEM] * 4,
            out_specs=[VMEM] * 6,
            scratch_shapes=[pltpu.VMEM((2, half_rows, tile), LINK)],
            compiler_params=PARAMS,
        )(place, trunk, head, other_head, lse)
    )
    return (
        species_loss.reshape(-1),
        head_grad,
        first_grad,
        first_bias_grad.reshape(-1),
        second_grad,
        second_bias_grad.reshape(-1),
    )


def solution(mesh):
    devices = mesh.devices.reshape(8, mesh.shape["bg"] // 16, 2, mesh.shape["sp"])
    torus = Mesh(devices, ("y", "z", "c", "x"))
    placed = (
        P(("y", "z", "c", "x"), None),
        P(),
        P(),
        P(),
        P(),
        P(),
        P(),
        P("x", None, None),
        P("x"),
        P("x", None),
    )
    return jax.shard_map(
        body,
        mesh=torus,
        in_specs=placed,
        out_specs=(P("x"), P("x", None, None), P(), P(), P(), P()),
        check_vma=False,
    )
```

```python
import functools
import math

import jax
import jax.numpy as jnp
from jax import lax
from jax.experimental import pallas as pl
from jax.experimental.pallas import tpu as pltpu
from jax.sharding import Mesh, PartitionSpec as P

BF16 = jnp.bfloat16
F32 = jnp.float32
CHUNK = 128
GROUP = 10
LINK = BF16
VMEM = pl.BlockSpec(memory_space=pltpu.VMEM)
SMEM = pl.BlockSpec(memory_space=pltpu.SMEM)
PARAMS = pltpu.CompilerParams(vmem_limit_bytes=28 << 20)


def dot(a, b):
    return jnp.dot(a, b, preferred_element_type=F32)


def dot_t(a, b):
    return lax.dot_general(a, b, (((1,), (1,)), ((), ())), preferred_element_type=F32)


def hits_of(presence_ref, lanes, first_row):
    shape = (CHUNK // 16, 16, lanes.size)
    rows = 16 * lax.broadcasted_iota(jnp.int32, shape, 0) + lax.broadcasted_iota(jnp.int32, shape, 1)
    rows = rows.astype(F32).astype(BF16)
    local = jnp.clip(presence_ref[:, lanes] - first_row, -1, CHUNK).astype(F32)
    one, zero = jnp.ones(shape, BF16), jnp.zeros(shape, BF16)
    hits = zero
    for record in range(presence_ref.shape[0]):
        there = jnp.broadcast_to(local[record : record + 1], shape[1:]).astype(BF16)
        hits += jnp.where(rows == there[None], one, zero)
    return hits.reshape(CHUNK, lanes.size)


def each_busy(busy, block_count, chunks, act):
    def step(i, carry):
        @pl.when(busy[i] > 0)
        def _():
            b = i // chunks
            act(b, pl.multiple_of((i % chunks) * CHUNK, CHUNK))

        return carry

    lax.fori_loop(0, block_count * chunks, step, 0)


def forward_kernel(
    first_index,
    second_index,
    clade,
    busy,
    place,
    covariates,
    first_weight,
    first_bias,
    second_weight,
    second_bias,
    head_weight,
    presence,
    logits,
    hits,
    local_lse,
    hit_sum,
    features,
    first_act,
    first_slope,
    second_slope,
    wide_weight,
    tops,
):
    blocks, cells, tile = features.shape
    block_count, slab, _ = head_weight.shape
    first_cell = place[0]

    def layer(pre, act_ref, slope_ref, o):
        sigma = 1.0 / (1.0 + jnp.exp(-pre))
        act_ref[o] = (pre * sigma).astype(BF16)
        slope_ref[o] = sigma * (1.0 + pre * (1.0 - sigma))

    for o in range(blocks):
        columns = pl.ds(pl.multiple_of(first_index[o] * tile, tile), tile)
        pre = dot(covariates[:, columns], first_weight[o]) + first_bias[o : o + 1, :]
        layer(pre, first_act, first_slope, o)
    for o in range(blocks):
        pre = dot(first_act[second_index[o]], second_weight[o]) + second_bias[o : o + 1, :]
        layer(pre, features, second_slope, o)

    hit_sum[...] = jnp.zeros_like(hit_sum)
    wide_weight[...] = jnp.zeros_like(wide_weight)
    for b in range(block_count):
        half = pl.ds(pl.multiple_of((clade[b] % 2) * slab, slab), slab)
        wide_weight[b, half, :] = head_weight[b]

    def step(i, carry):
        for g in range(GROUP):
            b = i * GROUP + g
            part = dot(features[clade[b] // 2], wide_weight[b])
            logits[b] = part
            tops[g] = jnp.max(part.reshape(cells // 8, 8, -1), axis=0)
        for g in range(GROUP):
            b = i * GROUP + g
            top = jnp.max(tops[g], axis=0, keepdims=True)
            total = jnp.sum(jnp.exp(logits[b] - top), axis=0, keepdims=True)
            local_lse[pl.ds(b, 1), :] = top + jnp.log(total)
        return carry

    lax.fori_loop(0, block_count // GROUP, step, 0)

    def add_hits(b, start):
        lanes = pl.ds(pl.multiple_of(b * tile, tile), tile)
        rows = pl.ds(start, CHUNK)
        found = hits_of(presence, lanes, first_cell + start)
        hits[b, rows, :] = found
        part = found.astype(F32) * logits[b, rows, :]
        hit_sum[pl.ds(b, 1), :] += jnp.sum(part, axis=0, keepdims=True)

    each_busy(busy, block_count, cells // CHUNK, add_hits)


def backward_kernel(
    records,
    first_index,
    second_index,
    clade,
    busy,
    place,
    covariates,
    second_weight,
    logits,
    hits,
    lse,
    hit_sum,
    features,
    first_act,
    first_slope,
    second_slope,
    wide_weight,
    trunk,
    keep,
    send,
    packed,
    bias,
    features_t,
    first_act_t,
    covariates_t,
    weight_cells,
    slab_grad,
    group_back,
    act_grad,
):
    blocks, cells, tile = features.shape
    block_count = wide_weight.shape[0]
    slab = tile // 2
    group = block_count // 2
    core = place[1]

    for o in range(blocks):
        features_t[o] = features[o].T
        first_act_t[o] = first_act[o].T
    for o in range(covariates.shape[1] // tile):
        covariates_t[o] = covariates[:, o * tile : (o + 1) * tile].T
    group_back[...] = jnp.zeros_like(group_back)
    act_grad[...] = jnp.zeros_like(act_grad)

    def weigh(i, carry):
        for g in range(GROUP):
            b = i * GROUP + g
            weight_cells[b] = jnp.exp(logits[b] - lse[pl.ds(b, 1), :]).astype(BF16)
        return carry

    lax.fori_loop(0, block_count // GROUP, weigh, 0)

    def take_hits(b, start):
        rows = pl.ds(start, CHUNK)
        weights = jnp.exp(logits[b, rows, :] - lse[pl.ds(b, 1), :])
        weights -= hits[b, rows, :].astype(F32) * (1.0 / records)
        weight_cells[b, rows, :] = weights.astype(BF16)

    each_busy(busy, block_count, cells // CHUNK, take_hits)

    def step(i, carry):
        for g in range(GROUP):
            b = i * GROUP + g
            slab_grad[g] = dot(features_t[clade[b] // 2], weight_cells[b])
        for g in range(GROUP):
            b = i * GROUP + g
            spot = clade[b]
            source = pl.ds(pl.multiple_of((spot % 2) * slab, slab), slab)
            target = pl.ds(pl.multiple_of((b % group) * slab, slab), slab)
            packed[b // group, target, :] = slab_grad[g, source, :]
            group_back[spot // 2] += dot_t(weight_cells[b], wide_weight[b])
        return carry

    lax.fori_loop(0, block_count // GROUP, step, 0)

    bias[...] = jnp.zeros_like(bias)
    pair = blocks // (trunk.shape[0] // 2)

    def trunk_sums(o, layer, left, dz):
        part, at = layer * (trunk.shape[0] // 2) + o // pair, o % pair
        trunk[part, at * tile : (at + 1) * tile, :] = dot(left, dz).astype(LINK)
        bias[part, at : at + 1, :] = jnp.sum(dz.astype(F32), axis=0, keepdims=True)

    for o in range(blocks):
        dz = (group_back[o] * second_slope[o]).astype(BF16)
        trunk_sums(o, 1, first_act_t[second_index[o]], dz)
        act_grad[second_index[o]] += dot_t(dz, second_weight[o])
    for o in range(blocks):
        dz = (act_grad[o] * first_slope[o]).astype(BF16)
        trunk_sums(o, 0, covariates_t[first_index[o]], dz)
    for part in range(trunk.shape[0]):
        trunk[part, pair * tile :, :] = bias[part].astype(LINK)

    tail = group * slab
    for half in range(2):
        packed[half, tail:, :] = jnp.zeros((packed.shape[1] - tail, tile), F32)
        packed[half, tail : tail + group, :] = hit_sum[half * group : (half + 1) * group, :]
    keep[...] = packed[core]
    send[...] = packed[1 - core]


def finish_kernel(
    total_cells,
    records,
    place,
    trunk,
    own,
    other,
    lse,
    species_loss,
    head_grad,
    first_grad,
    first_bias_grad,
    second_grad,
    second_bias_grad,
    halves,
):
    core = place[1]
    blocks, tile, _ = first_grad.shape
    block_count, slab, _ = head_grad.shape
    group = block_count // 2
    halves[core] = own[...]
    halves[1 - core] = other[...]
    for b in range(block_count):
        rows = slice((b % group) * slab, (b % group + 1) * slab)
        head_grad[b] = halves[b // group, rows, :].astype(F32)
    tail = group * slab
    for half in range(2):
        rows = slice(half * group, (half + 1) * group)
        hit_mean = halves[half, tail:, :].astype(F32)[:group] * (1.0 / records)
        species_loss[rows, :] = lse[rows, :] - math.log(total_cells) - hit_mean
    half = trunk.shape[0] // 2
    pair = blocks // half
    for layer, (grad, bias_grad) in enumerate(
        ((first_grad, first_bias_grad), (second_grad, second_bias_grad))
    ):
        for part in range(half):
            for at in range(pair):
                rows = slice(at * tile, (at + 1) * tile)
                grad[part * pair + at] = trunk[layer * half + part, rows, :].astype(F32)
            bias = trunk[layer * half + part, pair * tile :, :].astype(F32)
            bias_grad[part * pair : (part + 1) * pair, :] = bias[:pair]


def spread(value, axis, size):
    return lax.all_to_all(jnp.broadcast_to(value[None], (size, *value.shape)), axis, 0, 0)


def join(parts):
    top = jnp.max(parts, axis=0)
    return top + jnp.log(jnp.sum(jnp.exp(parts - top), axis=0))


def forward(
    scalars,
    covariates,
    first_weight,
    first_bias,
    second_weight,
    second_bias,
    head_weight,
    presence_t,
):
    blocks, tile, _ = first_weight.shape
    block_count, _, species = head_weight.shape
    cells = covariates.shape[0]
    by_block = (blocks, cells, tile)
    shape = jax.ShapeDtypeStruct
    return pl.pallas_call(
        forward_kernel,
        name="forward",
        out_shape=(
            shape((block_count, cells, species), F32),
            shape((block_count, cells, species), BF16),
            shape((block_count, species), F32),
            shape((block_count, species), F32),
            shape(by_block, BF16),
            shape(by_block, BF16),
            shape(by_block, F32),
            shape(by_block, F32),
            shape((block_count, tile, species), BF16),
        ),
        in_specs=[SMEM] * 5 + [VMEM] * 7,
        out_specs=[VMEM] * 9,
        scratch_shapes=[pltpu.VMEM((GROUP, 8, species), F32)],
        compiler_params=PARAMS,
    )(
        *scalars,
        covariates,
        first_weight,
        first_bias.reshape(blocks, tile),
        second_weight,
        second_bias.reshape(blocks, tile),
        head_weight,
        presence_t,
    )


def backward(records, scalars, covariates, second_weight, saved, lse, nx):
    logits, hits, _, hit_sum, features, first_act, first_slope, second_slope, wide = saved
    by_block = blocks, cells, tile = features.shape
    block_count, _, species = logits.shape
    width, slab = covariates.shape[1], tile // 2
    shape = jax.ShapeDtypeStruct
    pair = blocks // nx
    part_rows = pair * tile + 8
    group = block_count // 2
    head_rows = group * slab
    half_rows = head_rows + -(-group // 8) * 8
    return pl.pallas_call(
        functools.partial(backward_kernel, records),
        name="backward",
        out_shape=(
            shape((2 * nx, part_rows, tile), LINK),
            shape((half_rows, tile), F32),
            shape((half_rows, tile), F32),
        ),
        in_specs=[SMEM] * 5 + [VMEM] * 11,
        out_specs=[VMEM] * 3,
        scratch_shapes=[
            pltpu.VMEM((2, half_rows, tile), F32),
            pltpu.VMEM((2 * nx, 8, tile), F32),
            pltpu.VMEM((blocks, tile, cells), BF16),
            pltpu.VMEM((blocks, tile, cells), BF16),
            pltpu.VMEM((width // tile, tile, cells), BF16),
            pltpu.VMEM((block_count, cells, species), BF16),
            pltpu.VMEM((GROUP, tile, species), F32),
            pltpu.VMEM(by_block, F32),
            pltpu.VMEM(by_block, F32),
        ],
        compiler_params=PARAMS,
    )(
        *scalars,
        covariates,
        second_weight,
        logits,
        hits,
        lse,
        hit_sum,
        features,
        first_act,
        first_slope,
        second_slope,
        wide,
    )


def body(
    covariates,
    first_weight,
    first_bias,
    first_index,
    second_weight,
    second_bias,
    second_index,
    head_weight,
    clade_block,
    presence,
):
    ny, nz, nx = lax.axis_size("y"), lax.axis_size("z"), lax.axis_size("x")
    core, mine = lax.axis_index("c"), lax.axis_index("x")
    swap = [(0, 1), (1, 0)]
    blocks, tile, _ = first_weight.shape
    block_count, slab, species = head_weight.shape
    records = presence.shape[1]
    own_cells, width = covariates.shape
    cells = own_cells * nx
    first_cell = ((lax.axis_index("y") * nz + lax.axis_index("z")) * 2 + core) * cells
    total_cells = ny * nz * 2 * cells

    presence_t = presence.T
    chunk_of = lax.shift_right_arithmetic(presence_t - first_cell, int(math.log2(CHUNK)))
    chunk_of = chunk_of.reshape(records, block_count, species)
    busy = jnp.stack(
        [jnp.any(chunk_of == k, axis=(0, 2)) for k in range(cells // CHUNK)], axis=1
    )
    busy = busy.astype(jnp.int32).reshape(-1)
    place = jnp.stack([first_cell, core]).astype(jnp.int32)
    scalars = (first_index, second_index, clade_block, busy, place)

    all_covariates = spread(covariates, "x", nx).reshape(cells, width)
    saved = forward(
        scalars,
        all_covariates,
        first_weight,
        first_bias,
        second_weight,
        second_bias,
        head_weight,
        presence_t,
    )
    lse = join(spread(saved[2], "y", ny))
    lse = join(spread(lse, ("z", "c"), nz * 2))

    trunk, keep, send = backward(
        records, scalars, all_covariates, second_weight, saved, lse, nx
    )
    pair, group = blocks // nx, block_count // 2
    head_rows = group * slab
    half_rows = keep.shape[0]

    head = keep + lax.ppermute(send, "c", swap)
    trunk = jnp.sum(lax.all_to_all(trunk, ("c", "x"), 0, 0).astype(F32), axis=0)
    peers = ny * nz
    misc = jnp.concatenate([head[head_rows : head_rows + group], trunk[pair * tile :][:pair]])
    misc = jnp.pad(misc, ((0, peers - misc.shape[0]), (0, 0)))
    trunk_cut, head_cut = pair * tile // peers, head_rows // peers
    cut = jnp.concatenate(
        [
            trunk[: pair * tile].reshape(peers, trunk_cut, tile),
            head[:head_rows].reshape(peers, head_cut, tile),
            misc[:, None],
        ],
        axis=1,
    )
    cut = jnp.pad(cut, ((0, 0), (0, -cut.shape[1] % 8), (0, 0))).astype(LINK)
    cut = jnp.sum(lax.all_to_all(cut, ("y", "z"), 0, 0).astype(F32), axis=0).astype(LINK)

    cut = spread(cut, ("y", "z"), peers)
    misc = cut[:, trunk_cut + head_cut]
    head = jnp.concatenate(
        [
            cut[:, trunk_cut : trunk_cut + head_cut].reshape(head_rows, tile),
            jnp.pad(misc[:group], ((0, -group % 8), (0, 0))),
        ]
    )
    other_head = lax.ppermute(head, "c", swap)
    trunk = jnp.concatenate(
        [
            cut[:, :trunk_cut].reshape(pair * tile, tile),
            jnp.pad(misc[group : group + pair], ((0, -pair % 8), (0, 0))),
        ]
    )
    trunk = spread(trunk, ("c", "x"), 2 * nx)
    shape = jax.ShapeDtypeStruct
    species_loss, head_grad, first_grad, first_bias_grad, second_grad, second_bias_grad = (
        pl.pallas_call(
            functools.partial(finish_kernel, total_cells, records),
            name="finish",
            out_shape=(
                shape((block_count, species), F32),
                shape(head_weight.shape, F32),
                shape(first_weight.shape, F32),
                shape((blocks, tile), F32),
                shape(second_weight.shape, F32),
                shape((blocks, tile), F32),
            ),
            in_specs=[SMEM] + [VMEM] * 4,
            out_specs=[VMEM] * 6,
            scratch_shapes=[pltpu.VMEM((2, half_rows, tile), LINK)],
            compiler_params=PARAMS,
        )(place, trunk, head, other_head, lse)
    )
    return (
        species_loss.reshape(-1),
        head_grad,
        first_grad,
        first_bias_grad.reshape(-1),
        second_grad,
        second_bias_grad.reshape(-1),
    )


def solution(mesh):
    devices = mesh.devices.reshape(8, mesh.shape["bg"] // 16, 2, mesh.shape["sp"])
    torus = Mesh(devices, ("y", "z", "c", "x"))
    placed = (
        P(("y", "z", "c", "x"), None),
        P(),
        P(),
        P(),
        P(),
        P(),
        P(),
        P("x", None, None),
        P("x"),
        P("x", None),
    )
    return jax.shard_map(
        body,
        mesh=torus,
        in_specs=placed,
        out_specs=(P("x"), P("x", None, None), P(), P(), P(), P()),
        check_vma=False,
    )
```

```python
import functools
import math

import jax
import jax.numpy as jnp
from jax import lax
from jax.experimental import pallas as pl
from jax.experimental.pallas import tpu as pltpu
from jax.sharding import Mesh, PartitionSpec as P

BF16 = jnp.bfloat16
F32 = jnp.float32
CHUNK = 128
GROUP = 10
LINK = BF16
VMEM = pl.BlockSpec(memory_space=pltpu.VMEM)
ANY = pl.BlockSpec(memory_space=pl.ANY)
SMEM = pl.BlockSpec(memory_space=pltpu.SMEM)
PARAMS = pltpu.CompilerParams(vmem_limit_bytes=58 << 20)


def dot(a, b):
    return jnp.dot(a, b, preferred_element_type=F32)


def dot_t(a, b):
    return lax.dot_general(a, b, (((1,), (1,)), ((), ())), preferred_element_type=F32)


def hits_of(presence_ref, lanes, first_row):
    shape = (CHUNK // 16, 16, lanes.size)
    rows = 16 * lax.broadcasted_iota(jnp.int32, shape, 0) + lax.broadcasted_iota(jnp.int32, shape, 1)
    rows = rows.astype(F32).astype(BF16)
    local = jnp.clip(presence_ref[:, lanes] - first_row, -1, CHUNK).astype(F32)
    one, zero = jnp.ones(shape, BF16), jnp.zeros(shape, BF16)
    hits = zero
    for record in range(presence_ref.shape[0]):
        there = jnp.broadcast_to(local[record : record + 1], shape[1:]).astype(BF16)
        hits += jnp.where(rows == there[None], one, zero)
    return hits.reshape(CHUNK, lanes.size)


def fetch(sem, *pairs):
    copies = [pltpu.make_async_copy(*pair, sem.at[i]) for i, pair in enumerate(pairs)]
    for copy in copies:
        copy.start()
    return copies


class Part:
    def __init__(self, ref, start):
        self.ref, self.start = ref, start

    def __getitem__(self, i):
        return self.ref[self.start + i]


def scalar_parts(ref, blocks, block_count):
    starts = (2, 2 + blocks, 2 + 2 * blocks, 2 + 2 * blocks + block_count, 0)
    return [Part(ref, start) for start in starts]


def widen(wide_weight, head_weight, clade):
    slab = head_weight.shape[1]
    wide_weight[...] = jnp.zeros_like(wide_weight)
    for b in range(head_weight.shape[0]):
        half = pl.ds(pl.multiple_of((clade[b] % 2) * slab, slab), slab)
        wide_weight[b, half, :] = head_weight[b]


def each_busy(busy, block_count, chunks, act):
    def step(i, carry):
        @pl.when(busy[i] > 0)
        def _():
            b = i // chunks
            act(b, pl.multiple_of((i % chunks) * CHUNK, CHUNK))

        return carry

    lax.fori_loop(0, block_count * chunks, step, 0)


def forward_kernel(
    scalars,
    covariates_in,
    first_weight_in,
    first_bias_in,
    second_weight_in,
    second_bias_in,
    head_weight_in,
    presence_in,
    logits_out,
    hits_out,
    trunk_out,
    local_lse,
    hit_sum,
    covariates,
    first_weight,
    first_bias,
    second_weight,
    second_bias,
    head_weight,
    presence,
    logits,
    hits,
    trunk,
    wide_weight,
    tops,
    fetch_sem,
    logit_sem,
    hit_sem,
    trunk_sem,
):
    fetched = fetch(
        fetch_sem,
        (covariates_in, covariates),
        (first_weight_in, first_weight),
        (first_bias_in, first_bias),
        (second_weight_in, second_weight),
        (second_bias_in, second_bias),
        (head_weight_in, head_weight),
        (presence_in, presence),
    )
    first_act, features, first_slope, second_slope = (trunk.at[i] for i in range(4))
    blocks, cells, tile = features.shape
    block_count, slab, _ = head_weight.shape
    first_index, second_index, clade, busy, place = scalar_parts(scalars, blocks, block_count)
    first_cell = place[0]

    def layer(pre, act_ref, slope_ref, o):
        sigma = 1.0 / (1.0 + jnp.exp(-pre))
        act_ref[o] = (pre * sigma).astype(BF16)
        slope_ref[o] = (sigma * (1.0 + pre * (1.0 - sigma))).astype(BF16)

    for copy in fetched[:5]:
        copy.wait()
    for o in range(blocks):
        columns = pl.ds(pl.multiple_of(first_index[o] * tile, tile), tile)
        pre = dot(covariates[:, columns], first_weight[o]) + first_bias[o : o + 1, :]
        layer(pre, first_act, first_slope, o)
    for o in range(blocks):
        pre = dot(first_act[second_index[o]], second_weight[o]) + second_bias[o : o + 1, :]
        layer(pre, features, second_slope, o)

    trunk_copy = pltpu.make_async_copy(trunk, trunk_out, trunk_sem.at[0])
    trunk_copy.start()
    hit_sum[...] = jnp.zeros_like(hit_sum)
    fetched[5].wait()
    fetched[6].wait()
    widen(wide_weight, head_weight, clade)

    def step(i, carry):
        for g in range(GROUP):
            b = i * GROUP + g
            part = dot(features[clade[b] // 2], wide_weight[b])
            logits[b] = part
            tops[g] = jnp.max(part.reshape(cells // 8, 8, -1), axis=0)
        for g in range(GROUP):
            b = i * GROUP + g
            top = jnp.max(tops[g], axis=0, keepdims=True)
            total = jnp.sum(jnp.exp(logits[b] - top), axis=0, keepdims=True)
            local_lse[pl.ds(b, 1), :] = top + jnp.log(total)
        return carry

    logit_copies = []
    for i in range(block_count // GROUP):
        step(i, 0)
        part = pl.ds(i * GROUP, GROUP)
        logit_copies.append(
            pltpu.make_async_copy(logits.at[part], logits_out.at[part], logit_sem.at[i])
        )
        logit_copies[i].start()

    def add_hits(b, start):
        lanes = pl.ds(pl.multiple_of(b * tile, tile), tile)
        rows = pl.ds(start, CHUNK)
        found = hits_of(presence, lanes, first_cell + start)
        hits[b, rows, :] = found
        part = found.astype(F32) * logits[b, rows, :]
        hit_sum[pl.ds(b, 1), :] += jnp.sum(part, axis=0, keepdims=True)

    each_busy(busy, block_count, cells // CHUNK, add_hits)
    hit_copy = pltpu.make_async_copy(hits, hits_out, hit_sem.at[0])
    hit_copy.start()
    hit_copy.wait()
    for copy in logit_copies:
        copy.wait()
    trunk_copy.wait()


def backward_kernel(
    records,
    scalars,
    covariates_in,
    second_weight_in,
    head_weight_in,
    logits_in,
    hits_in,
    trunk_in,
    lse_in,
    hit_sum_in,
    trunk,
    keep,
    send,
    covariates,
    second_weight,
    head_weight,
    lse,
    hit_sum,
    logits,
    hits,
    layers,
    wide_weight,
    packed,
    bias,
    features_t,
    first_act_t,
    covariates_t,
    weight_cells,
    slab_grad,
    group_back,
    act_grad,
    fetch_sem,
    logit_sem,
    hit_sem,
    trunk_sem,
):
    first_act, features, first_slope, second_slope = (layers.at[i] for i in range(4))
    blocks, cells, tile = features.shape
    block_count, slab, _ = head_weight.shape

    layer_copies = [
        pltpu.make_async_copy(trunk_in.at[part], layers.at[part], trunk_sem.at[i])
        for i, part in enumerate((pl.ds(0, 2), pl.ds(2, 2)))
    ]
    logit_copies = [
        pltpu.make_async_copy(
            logits_in.at[pl.ds(i * GROUP, GROUP)],
            logits.at[pl.ds(i * GROUP, GROUP)],
            logit_sem.at[i],
        )
        for i in range(block_count // GROUP)
    ]

    hit_copy = pltpu.make_async_copy(hits_in, hits, hit_sem.at[0])
    first_index, second_index, clade, busy, place = scalar_parts(scalars, blocks, block_count)
    fetched = fetch(
        fetch_sem,
        (head_weight_in, head_weight),
        (covariates_in, covariates),
        (lse_in, lse),
        (hit_sum_in, hit_sum),
        (second_weight_in, second_weight),
    )
    layer_copies[0].start()
    for copy in logit_copies:
        copy.start()
    layer_copies[1].start()
    hit_copy.start()
    fetched[0].wait()
    fetched[1].wait()
    widen(wide_weight, head_weight, clade)
    for o in range(covariates.shape[1] // tile):
        covariates_t[o] = covariates[:, o * tile : (o + 1) * tile].T
    layer_copies[0].wait()
    group = block_count // 2
    core = place[1]

    for o in range(blocks):
        features_t[o] = features[o].T
        first_act_t[o] = first_act[o].T
    group_back[...] = jnp.zeros_like(group_back)
    act_grad[...] = jnp.zeros_like(act_grad)

    def weigh(i, carry):
        for g in range(GROUP):
            b = i * GROUP + g
            weight_cells[b] = jnp.exp(logits[b] - lse[pl.ds(b, 1), :]).astype(BF16)
        return carry

    fetched[2].wait()
    for i, copy in enumerate(logit_copies):
        copy.wait()
        weigh(i, 0)

    def take_hits(b, start):
        rows = pl.ds(start, CHUNK)
        weights = jnp.exp(logits[b, rows, :] - lse[pl.ds(b, 1), :])
        weights -= hits[b, rows, :].astype(F32) * (1.0 / records)
        weight_cells[b, rows, :] = weights.astype(BF16)

    hit_copy.wait()
    each_busy(busy, block_count, cells // CHUNK, take_hits)

    def step(i, carry):
        for g in range(GROUP):
            b = i * GROUP + g
            slab_grad[g] = dot(features_t[clade[b] // 2], weight_cells[b])
        for g in range(GROUP):
            b = i * GROUP + g
            spot = clade[b]
            source = pl.ds(pl.multiple_of((spot % 2) * slab, slab), slab)
            target = pl.ds(pl.multiple_of((b % group) * slab, slab), slab)
            packed[b // group, target, :] = slab_grad[g, source, :]
            group_back[spot // 2] += dot_t(weight_cells[b], wide_weight[b])
        return carry

    for i in range(block_count // GROUP):
        step(i, 0)

    layer_copies[1].wait()
    fetched[3].wait()
    fetched[4].wait()
    bias[...] = jnp.zeros_like(bias)
    pair = blocks // (trunk.shape[0] // 2)

    def trunk_sums(o, layer, left, dz):
        part, at = layer * (trunk.shape[0] // 2) + o // pair, o % pair
        trunk[part, at * tile : (at + 1) * tile, :] = dot(left, dz).astype(LINK)
        bias[part, at : at + 1, :] = jnp.sum(dz.astype(F32), axis=0, keepdims=True)

    for o in range(blocks):
        dz = (group_back[o] * second_slope[o].astype(F32)).astype(BF16)
        trunk_sums(o, 1, first_act_t[second_index[o]], dz)
        act_grad[second_index[o]] += dot_t(dz, second_weight[o])
    for o in range(blocks):
        dz = (act_grad[o] * first_slope[o].astype(F32)).astype(BF16)
        trunk_sums(o, 0, covariates_t[first_index[o]], dz)
    for part in range(trunk.shape[0]):
        trunk[part, pair * tile :, :] = bias[part].astype(LINK)

    tail = group * slab
    for half in range(2):
        packed[half, tail:, :] = jnp.zeros((packed.shape[1] - tail, tile), F32)
        packed[half, tail : tail + group, :] = hit_sum[half * group : (half + 1) * group, :]
    keep[...] = packed[core]
    send[...] = packed[1 - core]


def finish_kernel(
    total_cells,
    records,
    scalars,
    trunk,
    own,
    other,
    lse,
    species_loss,
    head_grad,
    first_grad,
    first_bias_grad,
    second_grad,
    second_bias_grad,
    halves,
):
    core = scalars[1]
    blocks, tile, _ = first_grad.shape
    block_count, slab, _ = head_grad.shape
    group = block_count // 2
    halves[core] = own[...]
    halves[1 - core] = other[...]
    for b in range(block_count):
        rows = slice((b % group) * slab, (b % group + 1) * slab)
        head_grad[b] = halves[b // group, rows, :].astype(F32)
    tail = group * slab
    for half in range(2):
        rows = slice(half * group, (half + 1) * group)
        hit_mean = halves[half, tail:, :].astype(F32)[:group] * (1.0 / records)
        species_loss[rows, :] = lse[rows, :] - math.log(total_cells) - hit_mean
    half = trunk.shape[0] // 2
    pair = blocks // half
    for layer, (grad, bias_grad) in enumerate(
        ((first_grad, first_bias_grad), (second_grad, second_bias_grad))
    ):
        for part in range(half):
            for at in range(pair):
                rows = slice(at * tile, (at + 1) * tile)
                grad[part * pair + at] = trunk[layer * half + part, rows, :].astype(F32)
            bias = trunk[layer * half + part, pair * tile :, :].astype(F32)
            bias_grad[part * pair : (part + 1) * pair, :] = bias[:pair]


def spread(value, axis, size):
    return lax.all_to_all(jnp.broadcast_to(value[None], (size, *value.shape)), axis, 0, 0)


def join(parts):
    top = jnp.max(parts, axis=0)
    return top + jnp.log(jnp.sum(jnp.exp(parts - top), axis=0))


def forward(
    scalars,
    covariates,
    first_weight,
    first_bias,
    second_weight,
    second_bias,
    head_weight,
    presence_t,
):
    blocks, tile, _ = first_weight.shape
    block_count, _, species = head_weight.shape
    cells = covariates.shape[0]
    by_clade = (block_count, cells, species)
    by_layer = (4, blocks, cells, tile)
    shape = jax.ShapeDtypeStruct
    return pl.pallas_call(
        forward_kernel,
        name="forward",
        out_shape=(
            shape(by_clade, F32),
            shape(by_clade, BF16),
            shape(by_layer, BF16),
            shape((block_count, species), F32),
            shape((block_count, species), F32),
        ),
        in_specs=[SMEM] + [ANY] * 7,
        out_specs=[ANY] * 3 + [VMEM] * 2,
        scratch_shapes=[
            pltpu.VMEM(covariates.shape, BF16),
            pltpu.VMEM(first_weight.shape, BF16),
            pltpu.VMEM((blocks, tile), F32),
            pltpu.VMEM(second_weight.shape, BF16),
            pltpu.VMEM((blocks, tile), F32),
            pltpu.VMEM(head_weight.shape, BF16),
            pltpu.VMEM(presence_t.shape, jnp.int32),
            pltpu.VMEM(by_clade, F32),
            pltpu.VMEM(by_clade, BF16),
            pltpu.VMEM(by_layer, BF16),
            pltpu.VMEM((block_count, tile, species), BF16),
            pltpu.VMEM((GROUP, 8, species), F32),
            pltpu.SemaphoreType.DMA((7,)),
            pltpu.SemaphoreType.DMA((block_count // GROUP,)),
            pltpu.SemaphoreType.DMA((1,)),
            pltpu.SemaphoreType.DMA((1,)),
        ],
        compiler_params=PARAMS,
    )(
        scalars,
        covariates,
        first_weight,
        first_bias.reshape(blocks, tile),
        second_weight,
        second_bias.reshape(blocks, tile),
        head_weight,
        presence_t,
    )


def backward(records, scalars, covariates, second_weight, head_weight, saved, lse, nx):
    logits, hits, layers, _, hit_sum = saved
    _, *by_block = layers.shape
    blocks, cells, tile = by_block
    block_count, slab, species = head_weight.shape
    width = covariates.shape[1]
    shape = jax.ShapeDtypeStruct
    pair = blocks // nx
    part_rows = pair * tile + 8
    group = block_count // 2
    half_rows = group * slab + -(-group // 8) * 8
    return pl.pallas_call(
        functools.partial(backward_kernel, records),
        name="backward",
        out_shape=(
            shape((2 * nx, part_rows, tile), LINK),
            shape((half_rows, tile), F32),
            shape((half_rows, tile), F32),
        ),
        in_specs=[SMEM] + [ANY] * 8,
        out_specs=[VMEM] * 3,
        scratch_shapes=[
            pltpu.VMEM(covariates.shape, BF16),
            pltpu.VMEM(second_weight.shape, BF16),
            pltpu.VMEM(head_weight.shape, BF16),
            pltpu.VMEM(lse.shape, F32),
            pltpu.VMEM(hit_sum.shape, F32),
            pltpu.VMEM(logits.shape, F32),
            pltpu.VMEM(hits.shape, BF16),
            pltpu.VMEM(layers.shape, BF16),
            pltpu.VMEM((block_count, tile, species), BF16),
            pltpu.VMEM((2, half_rows, tile), F32),
            pltpu.VMEM((2 * nx, 8, tile), F32),
            pltpu.VMEM((blocks, tile, cells), BF16),
            pltpu.VMEM((blocks, tile, cells), BF16),
            pltpu.VMEM((width // tile, tile, cells), BF16),
            pltpu.VMEM(hits.shape, BF16),
            pltpu.VMEM((GROUP, tile, species), F32),
            pltpu.VMEM(by_block, F32),
            pltpu.VMEM(by_block, F32),
            pltpu.SemaphoreType.DMA((5,)),
            pltpu.SemaphoreType.DMA((block_count // GROUP,)),
            pltpu.SemaphoreType.DMA((1,)),
            pltpu.SemaphoreType.DMA((2,)),
        ],
        compiler_params=PARAMS,
    )(
        scalars,
        covariates,
        second_weight,
        head_weight,
        logits,
        hits,
        layers,
        lse,
        hit_sum,
    )


def body(
    covariates,
    first_weight,
    first_bias,
    first_index,
    second_weight,
    second_bias,
    second_index,
    head_weight,
    clade_block,
    presence,
):
    ny, nz, nx = lax.axis_size("y"), lax.axis_size("z"), lax.axis_size("x")
    core, mine = lax.axis_index("c"), lax.axis_index("x")
    swap = [(0, 1), (1, 0)]
    blocks, tile, _ = first_weight.shape
    block_count, slab, species = head_weight.shape
    records = presence.shape[1]
    own_cells, width = covariates.shape
    cells = own_cells * nx
    first_cell = ((lax.axis_index("y") * nz + lax.axis_index("z")) * 2 + core) * cells
    total_cells = ny * nz * 2 * cells

    presence_t = presence.T
    chunk_of = lax.shift_right_arithmetic(presence_t - first_cell, int(math.log2(CHUNK)))
    chunk_of = chunk_of.reshape(records, block_count, species)
    busy = jnp.stack(
        [jnp.any(chunk_of == k, axis=(0, 2)) for k in range(cells // CHUNK)], axis=1
    )
    busy = busy.astype(jnp.int32).reshape(-1)
    place = jnp.stack([first_cell, core]).astype(jnp.int32)
    scalars = jnp.concatenate([place, first_index, second_index, clade_block, busy])

    all_covariates = spread(covariates, "x", nx).reshape(cells, width)
    saved = forward(
        scalars,
        all_covariates,
        first_weight,
        first_bias,
        second_weight,
        second_bias,
        head_weight,
        presence_t,
    )
    lse = join(spread(saved[3], "y", ny))
    lse = join(spread(lse, ("z", "c"), nz * 2))

    trunk, keep, send = backward(
        records, scalars, all_covariates, second_weight, head_weight, saved, lse, nx
    )
    pair, group = blocks // nx, block_count // 2
    head_rows = group * slab
    half_rows = keep.shape[0]

    head = keep + lax.ppermute(send, "c", swap)
    trunk = jnp.sum(lax.all_to_all(trunk, ("c", "x"), 0, 0).astype(F32), axis=0)
    peers = ny * nz
    misc = jnp.concatenate([head[head_rows : head_rows + group], trunk[pair * tile :][:pair]])
    misc = jnp.pad(misc, ((0, peers - misc.shape[0]), (0, 0)))
    trunk_cut, head_cut = pair * tile // peers, head_rows // peers
    cut = jnp.concatenate(
        [
            trunk[: pair * tile].reshape(peers, trunk_cut, tile),
            head[:head_rows].reshape(peers, head_cut, tile),
            misc[:, None],
        ],
        axis=1,
    )
    cut = jnp.pad(cut, ((0, 0), (0, -cut.shape[1] % 8), (0, 0))).astype(LINK)
    cut = jnp.sum(lax.all_to_all(cut, ("y", "z"), 0, 0).astype(F32), axis=0).astype(LINK)

    cut = spread(cut, ("y", "z"), peers)
    misc = cut[:, trunk_cut + head_cut]
    head = jnp.concatenate(
        [
            cut[:, trunk_cut : trunk_cut + head_cut].reshape(head_rows, tile),
            jnp.pad(misc[:group], ((0, -group % 8), (0, 0))),
        ]
    )
    other_head = lax.ppermute(head, "c", swap)
    trunk = jnp.concatenate(
        [
            cut[:, :trunk_cut].reshape(pair * tile, tile),
            jnp.pad(misc[group : group + pair], ((0, -pair % 8), (0, 0))),
        ]
    )
    trunk = spread(trunk, ("c", "x"), 2 * nx)
    shape = jax.ShapeDtypeStruct
    species_loss, head_grad, first_grad, first_bias_grad, second_grad, second_bias_grad = (
        pl.pallas_call(
            functools.partial(finish_kernel, total_cells, records),
            name="finish",
            out_shape=(
                shape((block_count, species), F32),
                shape(head_weight.shape, F32),
                shape(first_weight.shape, F32),
                shape((blocks, tile), F32),
                shape(second_weight.shape, F32),
                shape((blocks, tile), F32),
            ),
            in_specs=[SMEM] + [VMEM] * 4,
            out_specs=[VMEM] * 6,
            scratch_shapes=[pltpu.VMEM((2, half_rows, tile), LINK)],
            compiler_params=PARAMS,
        )(scalars, trunk, head, other_head, lse)
    )
    return (
        species_loss.reshape(-1),
        head_grad,
        first_grad,
        first_bias_grad.reshape(-1),
        second_grad,
        second_bias_grad.reshape(-1),
    )


def solution(mesh):
    devices = mesh.devices.reshape(8, mesh.shape["bg"] // 16, 2, mesh.shape["sp"])
    torus = Mesh(devices, ("y", "z", "c", "x"))
    placed = (
        P(("y", "z", "c", "x"), None),
        P(),
        P(),
        P(),
        P(),
        P(),
        P(),
        P("x", None, None),
        P("x"),
        P("x", None),
    )
    return jax.shard_map(
        body,
        mesh=torus,
        in_specs=placed,
        out_specs=(P("x"), P("x", None, None), P(), P(), P(), P()),
        check_vma=False,
    )
```

```python
import functools
import math

import jax
import jax.numpy as jnp
from jax import lax
from jax.experimental import pallas as pl
from jax.experimental.pallas import tpu as pltpu
from jax.sharding import Mesh, PartitionSpec as P

BF16 = jnp.bfloat16
F32 = jnp.float32
CHUNK = 128
GROUP = 10
LINK = BF16
VMEM = pl.BlockSpec(memory_space=pltpu.VMEM)
ANY = pl.BlockSpec(memory_space=pl.ANY)
SMEM = pl.BlockSpec(memory_space=pltpu.SMEM)
PARAMS = pltpu.CompilerParams(vmem_limit_bytes=58 << 20)


def dot(a, b):
    return jnp.dot(a, b, preferred_element_type=F32)


def dot_t(a, b):
    return lax.dot_general(a, b, (((1,), (1,)), ((), ())), preferred_element_type=F32)


def hits_of(presence_ref, lanes, first_row):
    shape = (CHUNK // 16, 16, lanes.size)
    rows = 16 * lax.broadcasted_iota(jnp.int32, shape, 0) + lax.broadcasted_iota(jnp.int32, shape, 1)
    rows = rows.astype(F32).astype(BF16)
    local = jnp.clip(presence_ref[:, lanes] - first_row, -1, CHUNK).astype(F32)
    one, zero = jnp.ones(shape, BF16), jnp.zeros(shape, BF16)
    hits = zero
    for record in range(presence_ref.shape[0]):
        there = jnp.broadcast_to(local[record : record + 1], shape[1:]).astype(BF16)
        hits += jnp.where(rows == there[None], one, zero)
    return hits.reshape(CHUNK, lanes.size)


def fetch(sem, *pairs):
    copies = [pltpu.make_async_copy(*pair, sem.at[i]) for i, pair in enumerate(pairs)]
    for copy in copies:
        copy.start()
    return copies


class Part:
    def __init__(self, ref, start):
        self.ref, self.start = ref, start

    def __getitem__(self, i):
        return self.ref[self.start + i]


def scalar_parts(ref, blocks, block_count):
    starts = (2, 2 + blocks, 2 + 2 * blocks, 2 + 2 * blocks + block_count, 0)
    return [Part(ref, start) for start in starts]


def widen(wide_weight, head_weight, clade):
    slab = head_weight.shape[1]
    wide_weight[...] = jnp.zeros_like(wide_weight)
    for b in range(head_weight.shape[0]):
        half = pl.ds(pl.multiple_of((clade[b] % 2) * slab, slab), slab)
        wide_weight[b, half, :] = head_weight[b]


def each_busy(busy, block_count, chunks, act):
    def step(i, carry):
        @pl.when(busy[i] > 0)
        def _():
            b = i // chunks
            act(b, pl.multiple_of((i % chunks) * CHUNK, CHUNK))

        return carry

    lax.fori_loop(0, block_count * chunks, step, 0)


def forward_kernel(
    scalars,
    covariates_in,
    first_weight_in,
    first_bias_in,
    second_weight_in,
    second_bias_in,
    head_weight_in,
    presence_in,
    logits_out,
    hits_out,
    trunk_out,
    local_lse,
    hit_sum,
    covariates,
    first_weight,
    first_bias,
    second_weight,
    second_bias,
    head_weight,
    presence,
    logits,
    hits,
    trunk,
    wide_weight,
    tops,
    fetch_sem,
    logit_sem,
    hit_sem,
    trunk_sem,
):
    fetched = fetch(
        fetch_sem,
        (covariates_in, covariates),
        (first_weight_in, first_weight),
        (first_bias_in, first_bias),
        (second_weight_in, second_weight),
        (second_bias_in, second_bias),
        (head_weight_in, head_weight),
        (presence_in, presence),
    )
    first_act, features, first_slope, second_slope = (trunk.at[i] for i in range(4))
    blocks, cells, tile = features.shape
    block_count, slab, _ = head_weight.shape
    first_index, second_index, clade, busy, place = scalar_parts(scalars, blocks, block_count)
    first_cell = place[0]

    def layer(pre, act_ref, slope_ref, o):
        sigma = 1.0 / (1.0 + jnp.exp(-pre))
        act_ref[o] = (pre * sigma).astype(BF16)
        slope_ref[o] = (sigma * (1.0 + pre * (1.0 - sigma))).astype(BF16)

    for copy in fetched[:5]:
        copy.wait()
    for o in range(blocks):
        columns = pl.ds(pl.multiple_of(first_index[o] * tile, tile), tile)
        pre = dot(covariates[:, columns], first_weight[o]) + first_bias[o : o + 1, :]
        layer(pre, first_act, first_slope, o)
    for o in range(blocks):
        pre = dot(first_act[second_index[o]], second_weight[o]) + second_bias[o : o + 1, :]
        layer(pre, features, second_slope, o)

    trunk_copy = pltpu.make_async_copy(trunk, trunk_out, trunk_sem.at[0])
    trunk_copy.start()
    hit_sum[...] = jnp.zeros_like(hit_sum)
    fetched[5].wait()
    fetched[6].wait()
    widen(wide_weight, head_weight, clade)

    def step(i, carry):
        for g in range(GROUP):
            b = i * GROUP + g
            part = dot(features[clade[b] // 2], wide_weight[b])
            logits[b] = part
            tops[g] = jnp.max(part.reshape(cells // 8, 8, -1), axis=0)
        for g in range(GROUP):
            b = i * GROUP + g
            top = jnp.max(tops[g], axis=0, keepdims=True)
            total = jnp.sum(jnp.exp(logits[b] - top), axis=0, keepdims=True)
            spread_lse = top + jnp.log(total)
            for peer in range(local_lse.shape[0]):
                local_lse[peer, pl.ds(b, 1), :] = spread_lse
        return carry

    logit_copies = []
    for i in range(block_count // GROUP):
        step(i, 0)
        part = pl.ds(i * GROUP, GROUP)
        logit_copies.append(
            pltpu.make_async_copy(logits.at[part], logits_out.at[part], logit_sem.at[i])
        )
        logit_copies[i].start()

    def add_hits(b, start):
        lanes = pl.ds(pl.multiple_of(b * tile, tile), tile)
        rows = pl.ds(start, CHUNK)
        found = hits_of(presence, lanes, first_cell + start)
        hits[b, rows, :] = found
        part = found.astype(F32) * logits[b, rows, :]
        hit_sum[pl.ds(b, 1), :] += jnp.sum(part, axis=0, keepdims=True)

    each_busy(busy, block_count, cells // CHUNK, add_hits)
    hit_copy = pltpu.make_async_copy(hits, hits_out, hit_sem.at[0])
    hit_copy.start()
    hit_copy.wait()
    for copy in logit_copies:
        copy.wait()
    trunk_copy.wait()


def join(parts):
    top = functools.reduce(jnp.maximum, [parts[i] for i in range(len(parts))])
    return top + jnp.log(sum(jnp.exp(parts[i] - top) for i in range(len(parts))))


def backward_kernel(
    records,
    scalars,
    covariates_in,
    second_weight_in,
    head_weight_in,
    logits_in,
    hits_in,
    trunk_in,
    lses_in,
    hit_sum_in,
    keep,
    send,
    lse,
    covariates,
    second_weight,
    head_weight,
    lses,
    hit_sum,
    logits,
    hits,
    layers,
    wide_weight,
    packed,
    bias,
    features_t,
    first_act_t,
    covariates_t,
    weight_cells,
    slab_grad,
    group_back,
    act_grad,
    out_sem,
    fetch_sem,
    logit_sem,
    hit_sem,
    trunk_sem,
):
    first_act, features, first_slope, second_slope = (layers.at[i] for i in range(4))
    blocks, cells, tile = features.shape
    block_count, slab, _ = head_weight.shape

    layer_copies = [
        pltpu.make_async_copy(trunk_in.at[part], layers.at[part], trunk_sem.at[i])
        for i, part in enumerate((pl.ds(0, 2), pl.ds(2, 2)))
    ]
    logit_copies = [
        pltpu.make_async_copy(
            logits_in.at[pl.ds(i * GROUP, GROUP)],
            logits.at[pl.ds(i * GROUP, GROUP)],
            logit_sem.at[i],
        )
        for i in range(block_count // GROUP)
    ]

    hit_copy = pltpu.make_async_copy(hits_in, hits, hit_sem.at[0])
    first_index, second_index, clade, busy, place = scalar_parts(scalars, blocks, block_count)
    fetched = fetch(
        fetch_sem,
        (head_weight_in, head_weight),
        (covariates_in, covariates),
        (lses_in, lses),
        (hit_sum_in, hit_sum),
        (second_weight_in, second_weight),
    )
    layer_copies[0].start()
    for copy in logit_copies:
        copy.start()
    layer_copies[1].start()
    hit_copy.start()
    fetched[0].wait()
    fetched[1].wait()
    widen(wide_weight, head_weight, clade)
    for o in range(covariates.shape[1] // tile):
        covariates_t[o] = covariates[:, o * tile : (o + 1) * tile].T
    layer_copies[0].wait()
    group = block_count // 2
    core = place[1]

    for o in range(blocks):
        features_t[o] = features[o].T
        first_act_t[o] = first_act[o].T
    group_back[...] = jnp.zeros_like(group_back)
    act_grad[...] = jnp.zeros_like(act_grad)

    def weigh(i, carry):
        for g in range(GROUP):
            b = i * GROUP + g
            weight_cells[b] = jnp.exp(logits[b] - lse[pl.ds(b, 1), :]).astype(BF16)
        return carry

    fetched[2].wait()
    lse[...] = join([lses[i] for i in range(lses.shape[0])])
    for i, copy in enumerate(logit_copies):
        copy.wait()
        weigh(i, 0)

    def take_hits(b, start):
        rows = pl.ds(start, CHUNK)
        weights = jnp.exp(logits[b, rows, :] - lse[pl.ds(b, 1), :])
        weights -= hits[b, rows, :].astype(F32) * (1.0 / records)
        weight_cells[b, rows, :] = weights.astype(BF16)

    hit_copy.wait()
    each_busy(busy, block_count, cells // CHUNK, take_hits)

    def step(i, carry):
        for g in range(GROUP):
            b = i * GROUP + g
            slab_grad[g] = dot(features_t[clade[b] // 2], weight_cells[b])
        for g in range(GROUP):
            b = i * GROUP + g
            spot = clade[b]
            source = pl.ds(pl.multiple_of((spot % 2) * slab, slab), slab)
            target = pl.ds(pl.multiple_of((b % group) * slab, slab), slab)
            packed[b // group, target, :] = slab_grad[g, source, :]
            group_back[spot // 2] += dot_t(weight_cells[b], wide_weight[b])
        return carry

    for i in range(block_count // GROUP):
        step(i, 0)

    layer_copies[1].wait()
    fetched[3].wait()
    fetched[4].wait()
    head_rows = group * slab
    trunk_at = head_rows + -(-group // 8) * 8
    parts = bias.shape[1]
    pair = blocks // parts
    part_rows = pair * tile + 8
    for half in range(2):
        packed[half, head_rows:trunk_at, :] = jnp.zeros((trunk_at - head_rows, tile), F32)
        sums = hit_sum[half * group : (half + 1) * group, :]
        packed[half, head_rows : head_rows + group, :] = sums
    bias[...] = jnp.zeros_like(bias)

    def trunk_sums(o, layer, left, dz):
        part, at = o // pair, o % pair
        start = trunk_at + part * part_rows + at * tile
        packed[layer, start : start + tile, :] = dot(left, dz)
        bias[layer, part, at : at + 1, :] = jnp.sum(dz.astype(F32), axis=0, keepdims=True)

    for o in range(blocks):
        dz = (group_back[o] * second_slope[o].astype(F32)).astype(BF16)
        trunk_sums(o, 1, first_act_t[second_index[o]], dz)
        act_grad[second_index[o]] += dot_t(dz, second_weight[o])
    for o in range(blocks):
        dz = (act_grad[o] * first_slope[o].astype(F32)).astype(BF16)
        trunk_sums(o, 0, covariates_t[first_index[o]], dz)
    for layer in range(2):
        for part in range(parts):
            start = trunk_at + (part + 1) * part_rows
            packed[layer, start - 8 : start, :] = bias[layer, part]
    out = fetch(out_sem, (packed.at[1 - core], send), (packed.at[core], keep))
    for copy in out:
        copy.wait()


def finish_kernel(
    total_cells,
    records,
    scalars,
    own_trunk,
    other_trunk,
    own,
    other,
    lse,
    species_loss,
    head_grad,
    first_grad,
    first_bias_grad,
    second_grad,
    second_bias_grad,
    halves,
    trunk,
):
    core = scalars[1]
    blocks, tile, _ = first_grad.shape
    block_count, slab, _ = head_grad.shape
    group = block_count // 2
    halves[core] = own[...]
    halves[1 - core] = other[...]
    trunk[core] = own_trunk[...]
    trunk[1 - core] = other_trunk[...]
    for b in range(block_count):
        rows = slice((b % group) * slab, (b % group + 1) * slab)
        head_grad[b] = halves[b // group, rows, :].astype(F32)
    tail = group * slab
    for half in range(2):
        rows = slice(half * group, (half + 1) * group)
        hit_mean = halves[half, tail:, :].astype(F32)[:group] * (1.0 / records)
        species_loss[rows, :] = lse[rows, :] - math.log(total_cells) - hit_mean
    parts = trunk.shape[1]
    pair = blocks // parts
    for layer, (grad, bias_grad) in enumerate(
        ((first_grad, first_bias_grad), (second_grad, second_bias_grad))
    ):
        for part in range(parts):
            for at in range(pair):
                rows = slice(at * tile, (at + 1) * tile)
                grad[part * pair + at] = trunk[layer, part, rows, :].astype(F32)
            bias = trunk[layer, part, pair * tile :, :].astype(F32)
            bias_grad[part * pair : (part + 1) * pair, :] = bias[:pair]


def spread(value, axis, size):
    return lax.all_to_all(jnp.broadcast_to(value[None], (size, *value.shape)), axis, 0, 0)


def forward(
    peers,
    scalars,
    covariates,
    first_weight,
    first_bias,
    second_weight,
    second_bias,
    head_weight,
    presence_t,
):
    blocks, tile, _ = first_weight.shape
    block_count, _, species = head_weight.shape
    cells = covariates.shape[0]
    by_clade = (block_count, cells, species)
    by_layer = (4, blocks, cells, tile)
    shape = jax.ShapeDtypeStruct
    return pl.pallas_call(
        forward_kernel,
        name="forward",
        out_shape=(
            shape(by_clade, F32),
            shape(by_clade, BF16),
            shape(by_layer, BF16),
            shape((peers, block_count, species), F32),
            shape((block_count, species), F32),
        ),
        in_specs=[SMEM] + [ANY] + [ANY] * 6,
        out_specs=[ANY] * 3 + [VMEM] * 2,
        scratch_shapes=[
            pltpu.VMEM(covariates.shape, BF16),
            pltpu.VMEM(first_weight.shape, BF16),
            pltpu.VMEM((blocks, tile), F32),
            pltpu.VMEM(second_weight.shape, BF16),
            pltpu.VMEM((blocks, tile), F32),
            pltpu.VMEM(head_weight.shape, BF16),
            pltpu.VMEM(presence_t.shape, jnp.int32),
            pltpu.VMEM(by_clade, F32),
            pltpu.VMEM(by_clade, BF16),
            pltpu.VMEM(by_layer, BF16),
            pltpu.VMEM((block_count, tile, species), BF16),
            pltpu.VMEM((GROUP, 8, species), F32),
            pltpu.SemaphoreType.DMA((7,)),
            pltpu.SemaphoreType.DMA((block_count // GROUP,)),
            pltpu.SemaphoreType.DMA((1,)),
            pltpu.SemaphoreType.DMA((1,)),
        ],
        compiler_params=PARAMS,
    )(
        scalars,
        covariates,
        first_weight,
        first_bias.reshape(blocks, tile),
        second_weight,
        second_bias.reshape(blocks, tile),
        head_weight,
        presence_t,
    )


def backward(records, scalars, covariates, second_weight, head_weight, saved, lse, nx):
    logits, hits, layers, _, hit_sum = saved
    _, *by_block = layers.shape
    blocks, cells, tile = by_block
    block_count, slab, species = head_weight.shape
    width = covariates.shape[1]
    shape = jax.ShapeDtypeStruct
    pair = blocks // nx
    group = block_count // 2
    rows = group * slab + -(-group // 8) * 8 + nx * (pair * tile + 8)
    return pl.pallas_call(
        functools.partial(backward_kernel, records),
        name="backward",
        out_shape=(
            shape((rows, tile), F32),
            shape((rows, tile), F32),
            shape((block_count, species), F32),
        ),
        in_specs=[SMEM, ANY, ANY, ANY, ANY, ANY, ANY, ANY, ANY],
        out_specs=[ANY, ANY, VMEM],
        scratch_shapes=[
            pltpu.VMEM(covariates.shape, BF16),
            pltpu.VMEM(second_weight.shape, BF16),
            pltpu.VMEM(head_weight.shape, BF16),
            pltpu.VMEM(lse.shape, F32),
            pltpu.VMEM(hit_sum.shape, F32),
            pltpu.VMEM(logits.shape, F32),
            pltpu.VMEM(hits.shape, BF16),
            pltpu.VMEM(layers.shape, BF16),
            pltpu.VMEM((block_count, tile, species), BF16),
            pltpu.VMEM((2, rows, tile), F32),
            pltpu.VMEM((2, nx, 8, tile), F32),
            pltpu.VMEM((blocks, tile, cells), BF16),
            pltpu.VMEM((blocks, tile, cells), BF16),
            pltpu.VMEM((width // tile, tile, cells), BF16),
            pltpu.VMEM(hits.shape, BF16),
            pltpu.VMEM((GROUP, tile, species), F32),
            pltpu.VMEM(by_block, F32),
            pltpu.VMEM(by_block, F32),
            pltpu.SemaphoreType.DMA((2,)),
            pltpu.SemaphoreType.DMA((5,)),
            pltpu.SemaphoreType.DMA((block_count // GROUP,)),
            pltpu.SemaphoreType.DMA((1,)),
            pltpu.SemaphoreType.DMA((2,)),
        ],
        compiler_params=PARAMS,
    )(
        scalars,
        covariates,
        second_weight,
        head_weight,
        logits,
        hits,
        layers,
        lse,
        hit_sum,
    )


def body(
    covariates,
    first_weight,
    first_bias,
    first_index,
    second_weight,
    second_bias,
    second_index,
    head_weight,
    clade_block,
    presence,
):
    ny, nz, nx = lax.axis_size("y"), lax.axis_size("z"), lax.axis_size("x")
    core, mine = lax.axis_index("c"), lax.axis_index("x")
    swap = [(0, 1), (1, 0)]
    blocks, tile, _ = first_weight.shape
    block_count, slab, species = head_weight.shape
    records = presence.shape[1]
    own_cells, width = covariates.shape
    cells = own_cells * nx
    first_cell = ((lax.axis_index("y") * nz + lax.axis_index("z")) * 2 + core) * cells
    total_cells = ny * nz * 2 * cells

    presence_t = presence.T
    chunk_of = lax.shift_right_arithmetic(presence_t - first_cell, int(math.log2(CHUNK)))
    chunk_of = chunk_of.reshape(records, block_count, species)
    busy = jnp.stack(
        [jnp.any(chunk_of == k, axis=(0, 2)) for k in range(cells // CHUNK)], axis=1
    )
    busy = busy.astype(jnp.int32).reshape(-1)
    place = jnp.stack([first_cell, core]).astype(jnp.int32)
    scalars = jnp.concatenate([place, first_index, second_index, clade_block, busy])

    all_covariates = spread(covariates, "x", nx).reshape(cells, width)
    saved = forward(
        ny,
        scalars,
        all_covariates,
        first_weight,
        first_bias,
        second_weight,
        second_bias,
        head_weight,
        presence_t,
    )
    lse = join(lax.all_to_all(saved[3], "y", 0, 0))
    lse = spread(lse, ("z", "c"), nz * 2)

    keep, send, lse = backward(
        records, scalars, all_covariates, second_weight, head_weight, saved, lse, nx
    )
    pair, group = blocks // nx, block_count // 2
    head_rows = group * slab
    half_rows = head_rows + -(-group // 8) * 8

    other = lax.ppermute(send, "c", swap)
    trunk = (keep[half_rows:] + other[half_rows:]).astype(LINK).reshape(nx, -1, tile)
    trunk = jnp.sum(lax.all_to_all(trunk, "x", 0, 0).astype(F32), axis=0)
    head = keep[:half_rows] + other[:half_rows]
    peers = ny * nz
    misc = jnp.concatenate([head[head_rows : head_rows + group], trunk[pair * tile :][:pair]])
    misc = jnp.pad(misc, ((0, peers - misc.shape[0]), (0, 0)))
    trunk_cut, head_cut = pair * tile // peers, head_rows // peers
    cut = jnp.concatenate(
        [
            trunk[: pair * tile].reshape(peers, trunk_cut, tile),
            head[:head_rows].reshape(peers, head_cut, tile),
            misc[:, None],
        ],
        axis=1,
    )
    cut = jnp.pad(cut, ((0, 0), (0, -cut.shape[1] % 8), (0, 0))).astype(LINK)
    cut = jnp.sum(lax.all_to_all(cut, ("y", "z"), 0, 0).astype(F32), axis=0).astype(LINK)

    cut = spread(cut, ("y", "z"), peers)
    misc = cut[:, trunk_cut + head_cut]
    head = jnp.concatenate(
        [
            cut[:, trunk_cut : trunk_cut + head_cut].reshape(head_rows, tile),
            jnp.pad(misc[:group], ((0, -group % 8), (0, 0))),
        ]
    )
    other_head = lax.ppermute(head, "c", swap)
    trunk = jnp.concatenate(
        [
            cut[:, :trunk_cut].reshape(pair * tile, tile),
            jnp.pad(misc[group : group + pair], ((0, -pair % 8), (0, 0))),
        ]
    )
    trunk = spread(trunk, "x", nx)
    other_trunk = lax.ppermute(trunk, "c", swap)
    shape = jax.ShapeDtypeStruct
    species_loss, head_grad, first_grad, first_bias_grad, second_grad, second_bias_grad = (
        pl.pallas_call(
            functools.partial(finish_kernel, total_cells, records),
            name="finish",
            out_shape=(
                shape((block_count, species), F32),
                shape(head_weight.shape, F32),
                shape(first_weight.shape, F32),
                shape((blocks, tile), F32),
                shape(second_weight.shape, F32),
                shape((blocks, tile), F32),
            ),
            in_specs=[SMEM] + [VMEM] * 5,
            out_specs=[VMEM] * 6,
            scratch_shapes=[
                pltpu.VMEM((2, half_rows, tile), LINK),
                pltpu.VMEM((2, *trunk.shape), LINK),
            ],
            compiler_params=pltpu.CompilerParams(vmem_limit_bytes=16 << 20),
        )(scalars, trunk, other_trunk, head, other_head, lse)
    )
    return (
        species_loss.reshape(-1),
        head_grad,
        first_grad,
        first_bias_grad.reshape(-1),
        second_grad,
        second_bias_grad.reshape(-1),
    )


def solution(mesh):
    devices = mesh.devices.reshape(8, mesh.shape["bg"] // 16, 2, mesh.shape["sp"])
    torus = Mesh(devices, ("y", "z", "c", "x"))
    placed = (
        P(("y", "z", "c", "x"), None),
        P(),
        P(),
        P(),
        P(),
        P(),
        P(),
        P("x", None, None),
        P("x"),
        P("x", None),
    )
    return jax.shard_map(
        body,
        mesh=torus,
        in_specs=placed,
        out_specs=(P("x"), P("x", None, None), P(), P(), P(), P()),
        check_vma=False,
    )
```

```python
import functools
import math

import jax
import jax.numpy as jnp
from jax import lax
from jax.experimental import pallas as pl
from jax.experimental.pallas import tpu as pltpu
from jax.sharding import Mesh, PartitionSpec as P

BF16 = jnp.bfloat16
F32 = jnp.float32
CHUNK = 128
GROUP = 10
LINK = BF16
VMEM = pl.BlockSpec(memory_space=pltpu.VMEM)
ANY = pl.BlockSpec(memory_space=pl.ANY)
SMEM = pl.BlockSpec(memory_space=pltpu.SMEM)
PARAMS = pltpu.CompilerParams(vmem_limit_bytes=58 << 20)


def dot(a, b):
    return jnp.dot(a, b, preferred_element_type=F32)


def dot_t(a, b):
    return lax.dot_general(a, b, (((1,), (1,)), ((), ())), preferred_element_type=F32)


def hits_of(presence_ref, lanes, first_row):
    shape = (CHUNK // 16, 16, lanes.size)
    rows = 16 * lax.broadcasted_iota(jnp.int32, shape, 0) + lax.broadcasted_iota(jnp.int32, shape, 1)
    rows = rows.astype(F32).astype(BF16)
    local = jnp.clip(presence_ref[:, lanes] - first_row, -1, CHUNK).astype(F32)
    one, zero = jnp.ones(shape, BF16), jnp.zeros(shape, BF16)
    hits = zero
    for record in range(presence_ref.shape[0]):
        there = jnp.broadcast_to(local[record : record + 1], shape[1:]).astype(BF16)
        hits += jnp.where(rows == there[None], one, zero)
    return hits.reshape(CHUNK, lanes.size)


def fetch(sem, *pairs):
    copies = [pltpu.make_async_copy(*pair, sem.at[i]) for i, pair in enumerate(pairs)]
    for copy in copies:
        copy.start()
    return copies


class Part:
    def __init__(self, ref, start):
        self.ref, self.start = ref, start

    def __getitem__(self, i):
        return self.ref[self.start + i]


def scalar_parts(ref, blocks, block_count):
    starts = (2, 2 + blocks, 2 + 2 * blocks, 2 + 2 * blocks + block_count, 0)
    return [Part(ref, start) for start in starts]


def widen(wide_weight, head_weight, clade):
    slab = head_weight.shape[1]
    wide_weight[...] = jnp.zeros_like(wide_weight)
    for b in range(head_weight.shape[0]):
        half = pl.ds(pl.multiple_of((clade[b] % 2) * slab, slab), slab)
        wide_weight[b, half, :] = head_weight[b]


def each_busy(busy, block_count, chunks, act):
    def step(i, carry):
        @pl.when(busy[i] > 0)
        def _():
            b = i // chunks
            act(b, pl.multiple_of((i % chunks) * CHUNK, CHUNK))

        return carry

    lax.fori_loop(0, block_count * chunks, step, 0)


def forward_kernel(
    scalars,
    covariates_in,
    first_weight_in,
    first_bias_in,
    second_weight_in,
    second_bias_in,
    head_weight_in,
    logits_out,
    trunk_out,
    local_lse,
    covariates,
    first_weight,
    first_bias,
    second_weight,
    second_bias,
    head_weight,
    logits,
    trunk,
    wide_weight,
    tops,
    fetch_sem,
    logit_sem,
    trunk_sem,
):
    fetched = fetch(
        fetch_sem,
        (covariates_in, covariates),
        (first_weight_in, first_weight),
        (first_bias_in, first_bias),
        (second_weight_in, second_weight),
        (second_bias_in, second_bias),
        (head_weight_in, head_weight),
    )
    first_act, features, first_slope, second_slope = (trunk.at[i] for i in range(4))
    blocks, cells, tile = features.shape
    block_count, slab, _ = head_weight.shape
    first_index, second_index, clade, _, _ = scalar_parts(scalars, blocks, block_count)

    def layer(pre, act_ref, slope_ref, o):
        sigma = 1.0 / (1.0 + jnp.exp(-pre))
        act_ref[o] = (pre * sigma).astype(BF16)
        slope_ref[o] = (sigma * (1.0 + pre * (1.0 - sigma))).astype(BF16)

    for copy in fetched[:5]:
        copy.wait()
    for o in range(blocks):
        columns = pl.ds(pl.multiple_of(first_index[o] * tile, tile), tile)
        pre = dot(covariates[:, columns], first_weight[o]) + first_bias[o : o + 1, :]
        layer(pre, first_act, first_slope, o)
    for o in range(blocks):
        pre = dot(first_act[second_index[o]], second_weight[o]) + second_bias[o : o + 1, :]
        layer(pre, features, second_slope, o)

    trunk_copy = pltpu.make_async_copy(trunk, trunk_out, trunk_sem.at[0])
    trunk_copy.start()
    fetched[5].wait()
    widen(wide_weight, head_weight, clade)

    def step(i, carry):
        for g in range(GROUP):
            b = i * GROUP + g
            part = dot(features[clade[b] // 2], wide_weight[b])
            logits[b] = part
            tops[g] = jnp.max(part.reshape(cells // 8, 8, -1), axis=0)
        for g in range(GROUP):
            b = i * GROUP + g
            top = jnp.max(tops[g], axis=0, keepdims=True)
            total = jnp.sum(jnp.exp(logits[b] - top), axis=0, keepdims=True)
            lse = top + jnp.log(total)
            for peer in range(local_lse.shape[0]):
                local_lse[peer, pl.ds(b, 1), :] = lse
        return carry

    logit_copies = []
    for i in range(block_count // GROUP):
        step(i, 0)
        part = pl.ds(i * GROUP, GROUP)
        logit_copies.append(
            pltpu.make_async_copy(logits.at[part], logits_out.at[part], logit_sem.at[i])
        )
        logit_copies[i].start()

    for copy in logit_copies:
        copy.wait()
    trunk_copy.wait()


def join(parts):
    top = functools.reduce(jnp.maximum, [parts[i] for i in range(len(parts))])
    return top + jnp.log(sum(jnp.exp(parts[i] - top) for i in range(len(parts))))


def middle_kernel(
    scalars,
    covariates_in,
    presence_in,
    local_lse_in,
    trunk_in,
    logits_in,
    hits_out,
    covariates_t_out,
    first_act_t_out,
    soft_grad,
    hit_grad,
    hit_sum,
    covariates,
    presence,
    local_lse,
    trunk,
    logits,
    hits,
    covariates_t,
    first_act_t,
    features_t,
    weight_cells,
    product,
    fetch_sem,
    logit_sem,
    out_sem,
):
    _, blocks, cells, tile = trunk.shape
    block_count, slab, _ = soft_grad.shape
    _, _, clade, busy, place = scalar_parts(scalars, blocks, block_count)
    first_cell = place[0]
    fetched = fetch(
        fetch_sem,
        (trunk_in.at[pl.ds(0, 2)], trunk),
        (local_lse_in.at[0], local_lse),
        (covariates_in, covariates),
        (presence_in, presence),
    )
    pieces = [pl.ds(i * GROUP, GROUP) for i in range(block_count // GROUP)]
    logit_copies = fetch(logit_sem, *[(logits_in.at[p], logits.at[p]) for p in pieces])
    hit_sum[...] = jnp.zeros_like(hit_sum)
    hit_grad[...] = jnp.zeros_like(hit_grad)
    fetched[0].wait()
    for o in range(blocks):
        first_act_t[o] = trunk[0, o].T
        features_t[o] = trunk[1, o].T
    fetched[1].wait()
    fetched[2].wait()
    for o in range(covariates.shape[1] // tile):
        covariates_t[o] = covariates[:, o * tile : (o + 1) * tile].T
    out = fetch(out_sem, (covariates_t, covariates_t_out), (first_act_t, first_act_t_out))

    for i, copy in enumerate(logit_copies):
        copy.wait()
        for g in range(GROUP):
            b = i * GROUP + g
            weight_cells[g] = jnp.exp(logits[b] - local_lse[b : b + 1, :]).astype(BF16)
        for g in range(GROUP):
            product[g] = dot(features_t[clade[i * GROUP + g] // 2], weight_cells[g])
        for g in range(GROUP):
            b = i * GROUP + g
            half = pl.ds(pl.multiple_of((clade[b] % 2) * slab, slab), slab)
            soft_grad[b] = product[g, half, :]
    fetched[3].wait()

    def add_hits(b, start):
        lanes = pl.ds(pl.multiple_of(b * tile, tile), tile)
        rows = pl.ds(start, CHUNK)
        found = hits_of(presence, lanes, first_cell + start)
        hits[b, rows, :] = found
        part = found.astype(F32) * logits[b, rows, :]
        hit_sum[pl.ds(b, 1), :] += jnp.sum(part, axis=0, keepdims=True)
        half = pl.ds(pl.multiple_of((clade[b] % 2) * slab, slab), slab)
        hit_grad[b] += dot(features_t[clade[b] // 2, half, rows], found)

    each_busy(busy, block_count, cells // CHUNK, add_hits)
    hit_copy = pltpu.make_async_copy(hits, hits_out, out_sem.at[2])
    hit_copy.start()
    for copy in out:
        copy.wait()
    hit_copy.wait()


def backward_kernel(
    records,
    scalars,
    second_weight_in,
    head_weight_in,
    logits_in,
    hits_in,
    trunk_in,
    local_lse_in,
    lses_in,
    hit_sum_in,
    covariates_t_in,
    first_act_t_in,
    soft_grad_in,
    hit_grad_in,
    trunk,
    keep,
    send,
    lse,
    second_weight,
    head_weight,
    local_lse,
    lses,
    hit_sum,
    covariates_t,
    first_act_t,
    soft_grad,
    hit_grad,
    logits,
    hits,
    slopes,
    wide_weight,
    packed,
    bias,
    weight_cells,
    group_back,
    act_grad,
    fetch_sem,
    logit_sem,
):
    first_slope, second_slope = slopes.at[0], slopes.at[1]
    blocks, cells, tile = first_slope.shape
    block_count, slab, _ = head_weight.shape
    first_index, second_index, clade, busy, place = scalar_parts(scalars, blocks, block_count)
    fetched = fetch(
        fetch_sem,
        (head_weight_in, head_weight),
        (lses_in, lses),
        (local_lse_in.at[0], local_lse),
        (hits_in, hits),
        (soft_grad_in, soft_grad),
        (hit_grad_in, hit_grad),
        (hit_sum_in, hit_sum),
        (second_weight_in, second_weight),
        (first_act_t_in, first_act_t),
        (trunk_in.at[pl.ds(2, 2)], slopes),
        (covariates_t_in, covariates_t),
    )
    logit_copies = [
        pltpu.make_async_copy(
            logits_in.at[pl.ds(i * GROUP, GROUP)],
            logits.at[pl.ds(i * GROUP, GROUP)],
            logit_sem.at[i],
        )
        for i in range(block_count // GROUP)
    ]

    for copy in logit_copies:
        copy.start()
    fetched[0].wait()
    widen(wide_weight, head_weight, clade)
    fetched[1].wait()
    lse[...] = join([lses[i] for i in range(lses.shape[0])])
    group = block_count // 2
    core = place[1]

    group_back[...] = jnp.zeros_like(group_back)
    act_grad[...] = jnp.zeros_like(act_grad)

    def weigh(i, carry):
        for g in range(GROUP):
            b = i * GROUP + g
            weight_cells[b] = jnp.exp(logits[b] - lse[pl.ds(b, 1), :]).astype(BF16)
        return carry

    for i, copy in enumerate(logit_copies):
        copy.wait()
        weigh(i, 0)
    for copy in fetched[2:]:
        copy.wait()

    def take_hits(b, start):
        rows = pl.ds(start, CHUNK)
        weights = jnp.exp(logits[b, rows, :] - lse[pl.ds(b, 1), :])
        weights -= hits[b, rows, :].astype(F32) * (1.0 / records)
        weight_cells[b, rows, :] = weights.astype(BF16)

    each_busy(busy, block_count, cells // CHUNK, take_hits)

    def step(i, carry):
        for g in range(GROUP):
            b = i * GROUP + g
            scale = jnp.exp(local_lse[b : b + 1, :] - lse[b : b + 1, :])
            grad = soft_grad[b] * scale - hit_grad[b] * (1.0 / records)
            packed[b // group, (b % group) * slab : (b % group + 1) * slab, :] = grad
        for g in range(GROUP):
            b = i * GROUP + g
            spot = clade[b]
            group_back[spot // 2] += dot_t(weight_cells[b], wide_weight[b])
        return carry

    for i in range(block_count // GROUP):
        step(i, 0)

    bias[...] = jnp.zeros_like(bias)
    pair = blocks // (trunk.shape[0] // 2)

    def trunk_sums(o, layer, left, dz):
        part, at = layer * (trunk.shape[0] // 2) + o // pair, o % pair
        trunk[part, at * tile : (at + 1) * tile, :] = dot(left, dz).astype(LINK)
        bias[part, at : at + 1, :] = jnp.sum(dz.astype(F32), axis=0, keepdims=True)

    for o in range(blocks):
        dz = (group_back[o] * second_slope[o].astype(F32)).astype(BF16)
        trunk_sums(o, 1, first_act_t[second_index[o]], dz)
        act_grad[second_index[o]] += dot_t(dz, second_weight[o])
    for o in range(blocks):
        dz = (act_grad[o] * first_slope[o].astype(F32)).astype(BF16)
        trunk_sums(o, 0, covariates_t[first_index[o]], dz)
    for part in range(trunk.shape[0]):
        trunk[part, pair * tile :, :] = bias[part].astype(LINK)

    tail = group * slab
    for half in range(2):
        packed[half, tail:, :] = jnp.zeros((packed.shape[1] - tail, tile), F32)
        packed[half, tail : tail + group, :] = hit_sum[half * group : (half + 1) * group, :]
    keep[...] = packed[core]
    send[...] = packed[1 - core]


def finish_kernel(
    total_cells,
    records,
    scalars,
    trunk,
    own,
    other,
    lse,
    species_loss,
    head_grad,
    first_grad,
    first_bias_grad,
    second_grad,
    second_bias_grad,
    halves,
):
    core = scalars[1]
    blocks, tile, _ = first_grad.shape
    block_count, slab, _ = head_grad.shape
    group = block_count // 2
    halves[core] = own[...]
    halves[1 - core] = other[...]
    for b in range(block_count):
        rows = slice((b % group) * slab, (b % group + 1) * slab)
        head_grad[b] = halves[b // group, rows, :].astype(F32)
    tail = group * slab
    for half in range(2):
        rows = slice(half * group, (half + 1) * group)
        hit_mean = halves[half, tail:, :].astype(F32)[:group] * (1.0 / records)
        species_loss[rows, :] = lse[rows, :] - math.log(total_cells) - hit_mean
    half = trunk.shape[0] // 2
    pair = blocks // half
    for layer, (grad, bias_grad) in enumerate(
        ((first_grad, first_bias_grad), (second_grad, second_bias_grad))
    ):
        for part in range(half):
            for at in range(pair):
                rows = slice(at * tile, (at + 1) * tile)
                grad[part * pair + at] = trunk[layer * half + part, rows, :].astype(F32)
            bias = trunk[layer * half + part, pair * tile :, :].astype(F32)
            bias_grad[part * pair : (part + 1) * pair, :] = bias[:pair]


def spread(value, axis, size):
    return lax.all_to_all(jnp.broadcast_to(value[None], (size, *value.shape)), axis, 0, 0)


def forward(
    peers,
    scalars,
    covariates,
    first_weight,
    first_bias,
    second_weight,
    second_bias,
    head_weight,
):
    blocks, tile, _ = first_weight.shape
    block_count, _, species = head_weight.shape
    cells = covariates.shape[0]
    by_clade = (block_count, cells, species)
    by_layer = (4, blocks, cells, tile)
    shape = jax.ShapeDtypeStruct
    return pl.pallas_call(
        forward_kernel,
        name="forward",
        out_shape=(
            shape(by_clade, F32),
            shape(by_layer, BF16),
            shape((peers, block_count, species), F32),
        ),
        in_specs=[SMEM] + [ANY] * 6,
        out_specs=[ANY] * 2 + [VMEM],
        scratch_shapes=[
            pltpu.VMEM(covariates.shape, BF16),
            pltpu.VMEM(first_weight.shape, BF16),
            pltpu.VMEM((blocks, tile), F32),
            pltpu.VMEM(second_weight.shape, BF16),
            pltpu.VMEM((blocks, tile), F32),
            pltpu.VMEM(head_weight.shape, BF16),
            pltpu.VMEM(by_clade, F32),
            pltpu.VMEM(by_layer, BF16),
            pltpu.VMEM((block_count, tile, species), BF16),
            pltpu.VMEM((GROUP, 8, species), F32),
            pltpu.SemaphoreType.DMA((6,)),
            pltpu.SemaphoreType.DMA((block_count // GROUP,)),
            pltpu.SemaphoreType.DMA((1,)),
        ],
        compiler_params=PARAMS,
    )(
        scalars,
        covariates,
        first_weight,
        first_bias.reshape(blocks, tile),
        second_weight,
        second_bias.reshape(blocks, tile),
        head_weight,
    )


def middle(scalars, covariates, presence_t, local_lse, layers, logits, slab):
    _, blocks, cells, tile = layers.shape
    block_count, _, species = logits.shape
    width = covariates.shape[1]
    shape = jax.ShapeDtypeStruct
    shapes = (
        shape(logits.shape, BF16),
        shape((width // tile, tile, cells), BF16),
        shape((blocks, tile, cells), BF16),
        shape((block_count, slab, species), F32),
        shape((block_count, slab, species), F32),
        shape((block_count, species), F32),
    )
    return pl.pallas_call(
        middle_kernel,
        name="middle",
        out_shape=shapes,
        in_specs=[SMEM] + [ANY] * 5,
        out_specs=[ANY] * 3 + [VMEM] * 3,
        scratch_shapes=[
            pltpu.VMEM(covariates.shape, BF16),
            pltpu.VMEM(presence_t.shape, jnp.int32),
            pltpu.VMEM((block_count, species), F32),
            pltpu.VMEM((2, blocks, cells, tile), BF16),
            pltpu.VMEM(logits.shape, F32),
            pltpu.VMEM(logits.shape, BF16),
            pltpu.VMEM((width // tile, tile, cells), BF16),
            pltpu.VMEM((blocks, tile, cells), BF16),
            pltpu.VMEM((blocks, tile, cells), BF16),
            pltpu.VMEM((GROUP, cells, species), BF16),
            pltpu.VMEM((GROUP, tile, species), F32),
            pltpu.SemaphoreType.DMA((4,)),
            pltpu.SemaphoreType.DMA((block_count // GROUP,)),
            pltpu.SemaphoreType.DMA((3,)),
        ],
        compiler_params=PARAMS,
        cost_estimate=pl.CostEstimate(
            flops=8 * logits.size * tile, bytes_accessed=12 * logits.size, transcendentals=logits.size
        ),
    )(scalars, covariates, presence_t, local_lse, layers, logits)


def backward(
    records, scalars, second_weight, head_weight, logits, layers, local_lse, lses, mids, nx
):
    hits, covariates_t, first_act_t, soft_grad, hit_grad, hit_sum = mids
    _, *by_block = layers.shape
    blocks, cells, tile = by_block
    block_count, slab, species = head_weight.shape
    shape = jax.ShapeDtypeStruct
    pair = blocks // nx
    part_rows = pair * tile + 8
    group = block_count // 2
    half_rows = group * slab + -(-group // 8) * 8
    return pl.pallas_call(
        functools.partial(backward_kernel, records),
        name="backward",
        out_shape=(
            shape((2 * nx, part_rows, tile), LINK),
            shape((half_rows, tile), F32),
            shape((half_rows, tile), F32),
            shape((block_count, species), F32),
        ),
        in_specs=[SMEM] + [ANY] * 12,
        out_specs=[VMEM] * 4,
        scratch_shapes=[
            pltpu.VMEM(second_weight.shape, BF16),
            pltpu.VMEM(head_weight.shape, BF16),
            pltpu.VMEM((block_count, species), F32),
            pltpu.VMEM(lses.shape, F32),
            pltpu.VMEM(hit_sum.shape, F32),
            pltpu.VMEM(covariates_t.shape, BF16),
            pltpu.VMEM(first_act_t.shape, BF16),
            pltpu.VMEM(soft_grad.shape, F32),
            pltpu.VMEM(hit_grad.shape, F32),
            pltpu.VMEM(logits.shape, F32),
            pltpu.VMEM(hits.shape, BF16),
            pltpu.VMEM((2, *by_block), BF16),
            pltpu.VMEM((block_count, tile, species), BF16),
            pltpu.VMEM((2, half_rows, tile), F32),
            pltpu.VMEM((2 * nx, 8, tile), F32),
            pltpu.VMEM(hits.shape, BF16),
            pltpu.VMEM(by_block, F32),
            pltpu.VMEM(by_block, F32),
            pltpu.SemaphoreType.DMA((11,)),
            pltpu.SemaphoreType.DMA((block_count // GROUP,)),
        ],
        compiler_params=PARAMS,
    )(
        scalars,
        second_weight,
        head_weight,
        logits,
        hits,
        layers,
        local_lse,
        lses,
        hit_sum,
        covariates_t,
        first_act_t,
        soft_grad,
        hit_grad,
    )


def body(
    covariates,
    first_weight,
    first_bias,
    first_index,
    second_weight,
    second_bias,
    second_index,
    head_weight,
    clade_block,
    presence,
):
    ny, nz, nx = lax.axis_size("y"), lax.axis_size("z"), lax.axis_size("x")
    core, mine = lax.axis_index("c"), lax.axis_index("x")
    swap = [(0, 1), (1, 0)]
    blocks, tile, _ = first_weight.shape
    block_count, slab, species = head_weight.shape
    records = presence.shape[1]
    own_cells, width = covariates.shape
    cells = own_cells * nx
    first_cell = ((lax.axis_index("y") * nz + lax.axis_index("z")) * 2 + core) * cells
    total_cells = ny * nz * 2 * cells

    presence_t = presence.T
    chunk_of = lax.shift_right_arithmetic(presence_t - first_cell, int(math.log2(CHUNK)))
    chunk_of = chunk_of.reshape(records, block_count, species)
    busy = jnp.stack(
        [jnp.any(chunk_of == k, axis=(0, 2)) for k in range(cells // CHUNK)], axis=1
    )
    busy = busy.astype(jnp.int32).reshape(-1)
    place = jnp.stack([first_cell, core]).astype(jnp.int32)
    scalars = jnp.concatenate([place, first_index, second_index, clade_block, busy])

    all_covariates = spread(covariates, "x", nx).reshape(cells, width)
    logits, layers, local_lse = forward(
        ny,
        scalars,
        all_covariates,
        first_weight,
        first_bias,
        second_weight,
        second_bias,
        head_weight,
    )
    lses = lax.all_to_all(local_lse, "y", 0, 0)
    mids = middle(scalars, all_covariates, presence_t, local_lse, layers, logits, slab)
    lses = spread(join(lses), ("z", "c"), nz * 2)
    trunk, keep, send, lse = backward(
        records, scalars, second_weight, head_weight, logits, layers, local_lse, lses, mids, nx
    )
    pair, group = blocks // nx, block_count // 2
    head_rows = group * slab
    half_rows = keep.shape[0]

    head = keep + lax.ppermute(send, "c", swap)
    trunk = jnp.sum(lax.all_to_all(trunk, ("c", "x"), 0, 0).astype(F32), axis=0)
    peers = ny * nz
    misc = jnp.concatenate([head[head_rows : head_rows + group], trunk[pair * tile :][:pair]])
    misc = jnp.pad(misc, ((0, peers - misc.shape[0]), (0, 0)))
    trunk_cut, head_cut = pair * tile // peers, head_rows // peers
    cut = jnp.concatenate(
        [
            trunk[: pair * tile].reshape(peers, trunk_cut, tile),
            head[:head_rows].reshape(peers, head_cut, tile),
            misc[:, None],
        ],
        axis=1,
    )
    cut = jnp.pad(cut, ((0, 0), (0, -cut.shape[1] % 8), (0, 0))).astype(LINK)
    cut = jnp.sum(lax.all_to_all(cut, ("y", "z"), 0, 0).astype(F32), axis=0).astype(LINK)

    cut = spread(cut, ("y", "z"), peers)
    misc = cut[:, trunk_cut + head_cut]
    head = jnp.concatenate(
        [
            cut[:, trunk_cut : trunk_cut + head_cut].reshape(head_rows, tile),
            jnp.pad(misc[:group], ((0, -group % 8), (0, 0))),
        ]
    )
    other_head = lax.ppermute(head, "c", swap)
    trunk = jnp.concatenate(
        [
            cut[:, :trunk_cut].reshape(pair * tile, tile),
            jnp.pad(misc[group : group + pair], ((0, -pair % 8), (0, 0))),
        ]
    )
    trunk = spread(trunk, ("c", "x"), 2 * nx)
    shape = jax.ShapeDtypeStruct
    species_loss, head_grad, first_grad, first_bias_grad, second_grad, second_bias_grad = (
        pl.pallas_call(
            functools.partial(finish_kernel, total_cells, records),
            name="finish",
            out_shape=(
                shape((block_count, species), F32),
                shape(head_weight.shape, F32),
                shape(first_weight.shape, F32),
                shape((blocks, tile), F32),
                shape(second_weight.shape, F32),
                shape((blocks, tile), F32),
            ),
            in_specs=[SMEM] + [VMEM] * 4,
            out_specs=[VMEM] * 6,
            scratch_shapes=[pltpu.VMEM((2, half_rows, tile), LINK)],
            compiler_params=pltpu.CompilerParams(vmem_limit_bytes=16 << 20),
        )(scalars, trunk, head, other_head, lse)
    )
    return (
        species_loss.reshape(-1),
        head_grad,
        first_grad,
        first_bias_grad.reshape(-1),
        second_grad,
        second_bias_grad.reshape(-1),
    )


def solution(mesh):
    devices = mesh.devices.reshape(8, mesh.shape["bg"] // 16, 2, mesh.shape["sp"])
    torus = Mesh(devices, ("y", "z", "c", "x"))
    placed = (
        P(("y", "z", "c", "x"), None),
        P(),
        P(),
        P(),
        P(),
        P(),
        P(),
        P("x", None, None),
        P("x"),
        P("x", None),
    )
    return jax.shard_map(
        body,
        mesh=torus,
        in_specs=placed,
        out_specs=(P("x"), P("x", None, None), P(), P(), P(), P()),
        check_vma=False,
    )
```

```python
import functools
import math

import jax
import jax.numpy as jnp
from jax import lax
from jax.experimental import pallas as pl
from jax.experimental.pallas import tpu as pltpu
from jax.sharding import Mesh, PartitionSpec as P

BF16 = jnp.bfloat16
F32 = jnp.float32
CHUNK = 128
GROUP = 10
AT_ONCE = 4
NOWHERE = -(1 << 30)
LINK = BF16
VMEM = pl.BlockSpec(memory_space=pltpu.VMEM)
ANY = pl.BlockSpec(memory_space=pl.ANY)
SMEM = pl.BlockSpec(memory_space=pltpu.SMEM)
PARAMS = pltpu.CompilerParams(vmem_limit_bytes=58 << 20)


def dot(a, b):
    return jnp.dot(a, b, preferred_element_type=F32)


def dot_t(a, b):
    return lax.dot_general(a, b, (((1,), (1,)), ((), ())), preferred_element_type=F32)


def hits_of(presence_ref, lanes, first_row):
    shape = (CHUNK // 16, 16, lanes.size)
    rows = 16 * lax.broadcasted_iota(jnp.int32, shape, 0) + lax.broadcasted_iota(jnp.int32, shape, 1)
    rows = rows.astype(F32).astype(BF16)
    local = jnp.clip(presence_ref[:, lanes] - first_row, -1, CHUNK).astype(F32)
    one, zero = jnp.full(shape, 1.0 / presence_ref.shape[0], BF16), jnp.zeros(shape, BF16)
    hits = zero
    for record in range(presence_ref.shape[0]):
        there = jnp.broadcast_to(local[record : record + 1], shape[1:]).astype(BF16)
        hits += jnp.where(rows == there[None], one, zero)
    return hits.reshape(CHUNK, lanes.size)


def fetch(sem, *pairs):
    copies = [pltpu.make_async_copy(*pair, sem.at[i]) for i, pair in enumerate(pairs)]
    for copy in copies:
        copy.start()
    return copies


class Part:
    def __init__(self, ref, start):
        self.ref, self.start = ref, start

    def __getitem__(self, i):
        return self.ref[self.start + i]


def scalar_parts(ref, blocks, block_count):
    starts = (2, 2 + blocks, 2 + 2 * blocks, 2 + 2 * blocks + block_count, 0)
    return [Part(ref, start) for start in starts]


def widen(wide_weight, head_weight, clade):
    slab = head_weight.shape[1]
    wide_weight[...] = jnp.zeros_like(wide_weight)
    for b in range(head_weight.shape[0]):
        half = pl.ds(pl.multiple_of((clade[b] % 2) * slab, slab), slab)
        wide_weight[b, half, :] = head_weight[b]


def each_busy(busy, found, count, act):
    def note(i, n):
        found[n] = i
        return n + jnp.where(busy[i] > 0, 1, 0)

    total = lax.fori_loop(0, count, note, 0)

    def step(j, carry):
        spots = [j * AT_ONCE + u for u in range(AT_ONCE)]
        act([(jnp.where(spot < total, found[spot], 0), spot < total) for spot in spots])
        return carry

    lax.fori_loop(0, (total + AT_ONCE - 1) // AT_ONCE, step, 0)


def forward_kernel(
    scalars,
    covariates_in,
    first_weight_in,
    first_bias_in,
    second_weight_in,
    second_bias_in,
    head_weight_in,
    terms_out,
    trunk_out,
    local_lse,
    high,
    covariates,
    first_weight,
    first_bias,
    second_weight,
    second_bias,
    head_weight,
    terms,
    trunk,
    wide_weight,
    logits,
    tops,
    fetch_sem,
    term_sem,
    trunk_sem,
):
    fetched = fetch(
        fetch_sem,
        (covariates_in, covariates),
        (first_weight_in, first_weight),
        (first_bias_in, first_bias),
        (second_weight_in, second_weight),
        (second_bias_in, second_bias),
        (head_weight_in, head_weight),
    )
    first_act, features, first_slope, second_slope = (trunk.at[i] for i in range(4))
    blocks, cells, tile = features.shape
    block_count, slab, _ = head_weight.shape
    first_index, second_index, clade, _, _ = scalar_parts(scalars, blocks, block_count)

    def layer(pre, act_ref, slope_ref, o):
        sigma = 1.0 / (1.0 + jnp.exp(-pre))
        act_ref[o] = (pre * sigma).astype(BF16)
        slope_ref[o] = (sigma * (1.0 + pre * (1.0 - sigma))).astype(BF16)

    for copy in fetched[:5]:
        copy.wait()
    for o in range(blocks):
        columns = pl.ds(pl.multiple_of(first_index[o] * tile, tile), tile)
        pre = dot(covariates[:, columns], first_weight[o]) + first_bias[o : o + 1, :]
        layer(pre, first_act, first_slope, o)
    for o in range(blocks):
        pre = dot(first_act[second_index[o]], second_weight[o]) + second_bias[o : o + 1, :]
        layer(pre, features, second_slope, o)

    trunk_copy = pltpu.make_async_copy(trunk, trunk_out, trunk_sem.at[0])
    trunk_copy.start()
    fetched[5].wait()
    widen(wide_weight, head_weight, clade)

    def step(i):
        for g in range(GROUP):
            b = i * GROUP + g
            part = dot(features[clade[b] // 2], wide_weight[b])
            logits[g] = part
            tops[g] = jnp.max(part.reshape(cells // 8, 8, -1), axis=0)
        for g in range(GROUP):
            b = i * GROUP + g
            top = jnp.max(tops[g], axis=0, keepdims=True)
            part = jnp.exp(logits[g] - top)
            terms[b] = part.astype(BF16)
            lse = top + jnp.log(jnp.sum(part, axis=0, keepdims=True))
            high[b : b + 1, :] = top
            for peer in range(local_lse.shape[0]):
                local_lse[peer, b : b + 1, :] = lse

    term_copies = []
    for i in range(block_count // GROUP):
        step(i)
        part = pl.ds(i * GROUP, GROUP)
        copy = pltpu.make_async_copy(terms.at[part], terms_out.at[part], term_sem.at[i])
        copy.start()
        term_copies.append(copy)
    for copy in term_copies:
        copy.wait()
    trunk_copy.wait()


def join(parts):
    top = functools.reduce(jnp.maximum, [parts[i] for i in range(len(parts))])
    return top + jnp.log(sum(jnp.exp(parts[i] - top) for i in range(len(parts))))


def middle_kernel(
    scalars,
    presence_in,
    head_weight_in,
    trunk_in,
    hit_back,
    hit_grad,
    hit_sum,
    presence,
    head_weight,
    features,
    wide_weight,
    back,
    found,
    fetch_sem,
):
    blocks, cells, tile = features.shape
    block_count, slab, _ = head_weight.shape
    _, _, clade, busy, place = scalar_parts(scalars, blocks, block_count)
    first_cell = place[0]
    fetched = fetch(
        fetch_sem,
        (head_weight_in, head_weight),
        (presence_in, presence),
        (trunk_in.at[1], features),
    )
    hit_grad[...] = jnp.zeros_like(hit_grad)
    back[...] = jnp.zeros_like(back)
    fetched[0].wait()
    widen(wide_weight, head_weight, clade)
    for copy in fetched[1:]:
        copy.wait()

    def add_hits(chosen):
        products = []
        for i, valid in chosen:
            b, start = i // (cells // CHUNK), pl.multiple_of((i % (cells // CHUNK)) * CHUNK, CHUNK)
            lanes = pl.ds(pl.multiple_of(b * tile, tile), tile)
            rows = pl.ds(start, CHUNK)
            hits = hits_of(presence, lanes, jnp.where(valid, first_cell + start, NOWHERE))
            grad = lax.dot_general(
                features[clade[b] // 2, rows, :],
                hits,
                (((0,), (0,)), ((), ())),
                preferred_element_type=F32,
            )
            products.append((b, rows, grad, dot_t(hits, wide_weight[b])))
        for b, rows, grad, part in products:
            hit_grad[b] += grad
            back[clade[b] // 2, rows, :] += part

    each_busy(busy, found, block_count * (cells // CHUNK), add_hits)
    for b in range(block_count):
        terms = hit_grad[b] * wide_weight[b].astype(F32)
        hit_sum[b : b + 1, :] = jnp.sum(terms, axis=0, keepdims=True)
    for o in range(blocks):
        hit_back[o] = back[o].astype(BF16)


def backward_kernel(
    scalars,
    covariates_in,
    second_weight_in,
    head_weight_in,
    terms_in,
    trunk_in,
    high_in,
    lses_in,
    hit_back_in,
    hit_grad_in,
    hit_sum_in,
    trunk,
    keep,
    send,
    lse,
    covariates,
    second_weight,
    head_weight,
    terms,
    layers,
    high,
    lses,
    hit_back,
    hit_grad,
    hit_sum,
    wide_weight,
    packed,
    bias,
    features_t,
    first_act_t,
    covariates_t,
    weight_cells,
    slab_grad,
    group_back,
    act_grad,
    fetch_sem,
    term_sem,
):
    first_act, features, first_slope, second_slope = (layers.at[i] for i in range(4))
    blocks, cells, tile = features.shape
    block_count, slab, _ = head_weight.shape
    first_index, second_index, clade, _, place = scalar_parts(scalars, blocks, block_count)
    early = fetch(
        fetch_sem,
        (lses_in, lses),
        (high_in, high),
        (head_weight_in, head_weight),
        (trunk_in.at[pl.ds(0, 2)], layers.at[pl.ds(0, 2)]),
        (covariates_in, covariates),
    )
    pieces = [pl.ds(i * GROUP, GROUP) for i in range(block_count // GROUP)]
    term_copies = fetch(term_sem, *[(terms_in.at[p], terms.at[p]) for p in pieces])
    late = fetch(
        fetch_sem.at[pl.ds(len(early), 5)],
        (hit_back_in, hit_back),
        (hit_grad_in, hit_grad),
        (hit_sum_in, hit_sum),
        (trunk_in.at[pl.ds(2, 2)], layers.at[pl.ds(2, 2)]),
        (second_weight_in, second_weight),
    )
    early[0].wait()
    early[1].wait()
    lse[...] = join([lses[i] for i in range(lses.shape[0])])
    high[...] = jnp.exp(high[...] - lse[...])
    early[2].wait()
    widen(wide_weight, head_weight, clade)
    early[3].wait()
    for o in range(blocks):
        features_t[o] = features[o].T
        first_act_t[o] = first_act[o].T
    early[4].wait()
    for o in range(covariates.shape[1] // tile):
        covariates_t[o] = covariates[:, o * tile : (o + 1) * tile].T
    group = block_count // 2
    core = place[1]

    act_grad[...] = jnp.zeros_like(act_grad)
    for i, copy in enumerate(term_copies):
        copy.wait()
        for b in range(i * GROUP, (i + 1) * GROUP):
            weights = terms[b].astype(F32) * high[b : b + 1, :]
            weight_cells[b] = weights.astype(BF16)
    for copy in late:
        copy.wait()
    for o in range(blocks):
        group_back[o] = -hit_back[o].astype(F32)
    for i in range(block_count // GROUP):
        for g in range(GROUP):
            b = i * GROUP + g
            slab_grad[g] = dot(features_t[clade[b] // 2], weight_cells[b])
        for g in range(GROUP):
            b = i * GROUP + g
            half = pl.ds(pl.multiple_of((clade[b] % 2) * slab, slab), slab)
            rows = slice((b % group) * slab, (b % group + 1) * slab)
            grad = slab_grad[g, half, :] - hit_grad[b, half, :]
            packed[b // group, rows, :] = grad
            group_back[clade[b] // 2] += dot_t(weight_cells[b], wide_weight[b])

    bias[...] = jnp.zeros_like(bias)
    pair = blocks // (trunk.shape[0] // 2)

    def trunk_sums(o, layer, left, dz):
        part, at = layer * (trunk.shape[0] // 2) + o // pair, o % pair
        trunk[part, at * tile : (at + 1) * tile, :] = dot(left, dz).astype(LINK)
        bias[part, at : at + 1, :] = jnp.sum(dz.astype(F32), axis=0, keepdims=True)

    for o in range(blocks):
        dz = (group_back[o] * second_slope[o].astype(F32)).astype(BF16)
        trunk_sums(o, 1, first_act_t[second_index[o]], dz)
        act_grad[second_index[o]] += dot_t(dz, second_weight[o])
    for o in range(blocks):
        dz = (act_grad[o] * first_slope[o].astype(F32)).astype(BF16)
        trunk_sums(o, 0, covariates_t[first_index[o]], dz)
    for part in range(trunk.shape[0]):
        trunk[part, pair * tile :, :] = bias[part].astype(LINK)

    tail = group * slab
    for half in range(2):
        packed[half, tail:, :] = jnp.zeros((packed.shape[1] - tail, tile), F32)
        packed[half, tail : tail + group, :] = hit_sum[half * group : (half + 1) * group, :]
    keep[...] = packed[core]
    send[...] = packed[1 - core]


def finish_kernel(
    total_cells,
    scalars,
    trunk,
    own,
    other,
    lse,
    species_loss,
    head_grad,
    first_grad,
    first_bias_grad,
    second_grad,
    second_bias_grad,
    halves,
):
    core = scalars[1]
    blocks, tile, _ = first_grad.shape
    block_count, slab, _ = head_grad.shape
    group = block_count // 2
    halves[core] = own[...]
    halves[1 - core] = other[...]
    for b in range(block_count):
        rows = slice((b % group) * slab, (b % group + 1) * slab)
        head_grad[b] = halves[b // group, rows, :].astype(F32)
    tail = group * slab
    for half in range(2):
        rows = slice(half * group, (half + 1) * group)
        hit_mean = halves[half, tail:, :].astype(F32)[:group]
        species_loss[rows, :] = lse[rows, :] - math.log(total_cells) - hit_mean
    half = trunk.shape[0] // 2
    pair = blocks // half
    for layer, (grad, bias_grad) in enumerate(
        ((first_grad, first_bias_grad), (second_grad, second_bias_grad))
    ):
        for part in range(half):
            for at in range(pair):
                rows = slice(at * tile, (at + 1) * tile)
                grad[part * pair + at] = trunk[layer * half + part, rows, :].astype(F32)
            bias = trunk[layer * half + part, pair * tile :, :].astype(F32)
            bias_grad[part * pair : (part + 1) * pair, :] = bias[:pair]


def spread(value, axis, size):
    return lax.all_to_all(jnp.broadcast_to(value[None], (size, *value.shape)), axis, 0, 0)


def forward(
    peers,
    scalars,
    covariates,
    first_weight,
    first_bias,
    second_weight,
    second_bias,
    head_weight,
):
    blocks, tile, _ = first_weight.shape
    block_count, _, species = head_weight.shape
    cells = covariates.shape[0]
    by_clade = (block_count, cells, species)
    by_layer = (4, blocks, cells, tile)
    shape = jax.ShapeDtypeStruct
    return pl.pallas_call(
        forward_kernel,
        name="forward",
        out_shape=(
            shape(by_clade, BF16),
            shape(by_layer, BF16),
            shape((peers, block_count, species), F32),
            shape((block_count, species), F32),
        ),
        in_specs=[SMEM] + [ANY] * 6,
        out_specs=[ANY] * 2 + [VMEM] * 2,
        scratch_shapes=[
            pltpu.VMEM(covariates.shape, BF16),
            pltpu.VMEM(first_weight.shape, BF16),
            pltpu.VMEM((blocks, tile), F32),
            pltpu.VMEM(second_weight.shape, BF16),
            pltpu.VMEM((blocks, tile), F32),
            pltpu.VMEM(head_weight.shape, BF16),
            pltpu.VMEM(by_clade, BF16),
            pltpu.VMEM(by_layer, BF16),
            pltpu.VMEM((block_count, tile, species), BF16),
            pltpu.VMEM((GROUP, cells, species), F32),
            pltpu.VMEM((GROUP, 8, species), F32),
            pltpu.SemaphoreType.DMA((6,)),
            pltpu.SemaphoreType.DMA((block_count // GROUP,)),
            pltpu.SemaphoreType.DMA((1,)),
        ],
        compiler_params=PARAMS,
    )(
        scalars,
        covariates,
        first_weight,
        first_bias.reshape(blocks, tile),
        second_weight,
        second_bias.reshape(blocks, tile),
        head_weight,
    )


def middle(scalars, presence_t, head_weight, layers):
    _, *by_block = layers.shape
    blocks, cells, tile = by_block
    block_count, _, species = head_weight.shape
    shape = jax.ShapeDtypeStruct
    return pl.pallas_call(
        middle_kernel,
        name="middle",
        out_shape=(
            shape(by_block, BF16),
            shape((block_count, tile, species), F32),
            shape((block_count, species), F32),
        ),
        in_specs=[SMEM] + [ANY] * 3,
        out_specs=[VMEM] * 3,
        scratch_shapes=[
            pltpu.VMEM(presence_t.shape, jnp.int32),
            pltpu.VMEM(head_weight.shape, BF16),
            pltpu.VMEM(by_block, BF16),
            pltpu.VMEM((block_count, tile, species), BF16),
            pltpu.VMEM(by_block, F32),
            pltpu.SMEM((block_count * (cells // CHUNK) + AT_ONCE,), jnp.int32),
            pltpu.SemaphoreType.DMA((3,)),
        ],
        compiler_params=PARAMS,
        cost_estimate=pl.CostEstimate(
            flops=8 * block_count * cells * species * tile,
            bytes_accessed=8 * blocks * cells * tile,
            transcendentals=0,
        ),
    )(scalars, presence_t, head_weight, layers)


def backward(
    scalars, covariates, second_weight, head_weight, terms, layers, high, lses, hits, nx
):
    hit_back, hit_grad, hit_sum = hits
    _, *by_block = layers.shape
    blocks, cells, tile = by_block
    block_count, slab, species = head_weight.shape
    width = covariates.shape[1]
    shape = jax.ShapeDtypeStruct
    pair = blocks // nx
    part_rows = pair * tile + 8
    group = block_count // 2
    half_rows = group * slab + -(-group // 8) * 8
    return pl.pallas_call(
        backward_kernel,
        name="backward",
        out_shape=(
            shape((2 * nx, part_rows, tile), LINK),
            shape((half_rows, tile), F32),
            shape((half_rows, tile), F32),
            shape((block_count, species), F32),
        ),
        in_specs=[SMEM] + [ANY] * 10,
        out_specs=[VMEM] * 4,
        scratch_shapes=[
            pltpu.VMEM(covariates.shape, BF16),
            pltpu.VMEM(second_weight.shape, BF16),
            pltpu.VMEM(head_weight.shape, BF16),
            pltpu.VMEM(terms.shape, BF16),
            pltpu.VMEM(layers.shape, BF16),
            pltpu.VMEM(high.shape, F32),
            pltpu.VMEM(lses.shape, F32),
            pltpu.VMEM(by_block, BF16),
            pltpu.VMEM(hit_grad.shape, F32),
            pltpu.VMEM(hit_sum.shape, F32),
            pltpu.VMEM((block_count, tile, species), BF16),
            pltpu.VMEM((2, half_rows, tile), F32),
            pltpu.VMEM((2 * nx, 8, tile), F32),
            pltpu.VMEM((blocks, tile, cells), BF16),
            pltpu.VMEM((blocks, tile, cells), BF16),
            pltpu.VMEM((width // tile, tile, cells), BF16),
            pltpu.VMEM(terms.shape, BF16),
            pltpu.VMEM((GROUP, tile, species), F32),
            pltpu.VMEM(by_block, F32),
            pltpu.VMEM(by_block, F32),
            pltpu.SemaphoreType.DMA((10,)),
            pltpu.SemaphoreType.DMA((block_count // GROUP,)),
        ],
        compiler_params=PARAMS,
    )(
        scalars,
        covariates,
        second_weight,
        head_weight,
        terms,
        layers,
        high,
        lses,
        hit_back,
        hit_grad,
        hit_sum,
    )


def body(
    covariates,
    first_weight,
    first_bias,
    first_index,
    second_weight,
    second_bias,
    second_index,
    head_weight,
    clade_block,
    presence,
):
    ny, nz, nx = lax.axis_size("y"), lax.axis_size("z"), lax.axis_size("x")
    core, mine = lax.axis_index("c"), lax.axis_index("x")
    swap = [(0, 1), (1, 0)]
    blocks, tile, _ = first_weight.shape
    block_count, slab, species = head_weight.shape
    records = presence.shape[1]
    own_cells, width = covariates.shape
    cells = own_cells * nx
    first_cell = ((lax.axis_index("y") * nz + lax.axis_index("z")) * 2 + core) * cells
    total_cells = ny * nz * 2 * cells

    presence_t = presence.T
    chunk_of = lax.shift_right_arithmetic(presence_t - first_cell, int(math.log2(CHUNK)))
    chunk_of = chunk_of.reshape(records, block_count, species)
    busy = jnp.stack(
        [jnp.any(chunk_of == k, axis=(0, 2)) for k in range(cells // CHUNK)], axis=1
    )
    busy = busy.astype(jnp.int32).reshape(-1)
    place = jnp.stack([first_cell, core]).astype(jnp.int32)
    scalars = jnp.concatenate([place, first_index, second_index, clade_block, busy])

    all_covariates = spread(covariates, "x", nx).reshape(cells, width)
    terms, layers, local_lse, high = forward(
        ny,
        scalars,
        all_covariates,
        first_weight,
        first_bias,
        second_weight,
        second_bias,
        head_weight,
    )
    lses = lax.all_to_all(local_lse, "y", 0, 0)
    hits = middle(scalars, presence_t, head_weight, layers)
    lses = spread(join(lses), ("z", "c"), nz * 2)
    trunk, keep, send, lse = backward(
        scalars,
        all_covariates,
        second_weight,
        head_weight,
        terms,
        layers,
        high,
        lses,
        hits,
        nx,
    )
    pair, group = blocks // nx, block_count // 2
    head_rows = group * slab
    half_rows = keep.shape[0]

    head = keep + lax.ppermute(send, "c", swap)
    trunk = jnp.sum(lax.all_to_all(trunk, ("c", "x"), 0, 0).astype(F32), axis=0)
    peers = ny * nz
    misc = jnp.concatenate([head[head_rows : head_rows + group], trunk[pair * tile :][:pair]])
    misc = jnp.pad(misc, ((0, peers - misc.shape[0]), (0, 0)))
    trunk_cut, head_cut = pair * tile // peers, head_rows // peers
    cut = jnp.concatenate(
        [
            trunk[: pair * tile].reshape(peers, trunk_cut, tile),
            head[:head_rows].reshape(peers, head_cut, tile),
            misc[:, None],
        ],
        axis=1,
    )
    cut = jnp.pad(cut, ((0, 0), (0, -cut.shape[1] % 8), (0, 0))).astype(LINK)
    cut = jnp.sum(lax.all_to_all(cut, ("y", "z"), 0, 0).astype(F32), axis=0).astype(LINK)

    cut = spread(cut, ("y", "z"), peers)
    misc = cut[:, trunk_cut + head_cut]
    head = jnp.concatenate(
        [
            cut[:, trunk_cut : trunk_cut + head_cut].reshape(head_rows, tile),
            jnp.pad(misc[:group], ((0, -group % 8), (0, 0))),
        ]
    )
    other_head = lax.ppermute(head, "c", swap)
    trunk = jnp.concatenate(
        [
            cut[:, :trunk_cut].reshape(pair * tile, tile),
            jnp.pad(misc[group : group + pair], ((0, -pair % 8), (0, 0))),
        ]
    )
    trunk = spread(trunk, ("c", "x"), 2 * nx)
    shape = jax.ShapeDtypeStruct
    species_loss, head_grad, first_grad, first_bias_grad, second_grad, second_bias_grad = (
        pl.pallas_call(
            functools.partial(finish_kernel, total_cells),
            name="finish",
            out_shape=(
                shape((block_count, species), F32),
                shape(head_weight.shape, F32),
                shape(first_weight.shape, F32),
                shape((blocks, tile), F32),
                shape(second_weight.shape, F32),
                shape((blocks, tile), F32),
            ),
            in_specs=[SMEM] + [VMEM] * 4,
            out_specs=[VMEM] * 6,
            scratch_shapes=[pltpu.VMEM((2, half_rows, tile), LINK)],
            compiler_params=pltpu.CompilerParams(vmem_limit_bytes=16 << 20),
        )(scalars, trunk, head, other_head, lse)
    )
    return (
        species_loss.reshape(-1),
        head_grad,
        first_grad,
        first_bias_grad.reshape(-1),
        second_grad,
        second_bias_grad.reshape(-1),
    )


def solution(mesh):
    devices = mesh.devices.reshape(8, mesh.shape["bg"] // 16, 2, mesh.shape["sp"])
    torus = Mesh(devices, ("y", "z", "c", "x"))
    placed = (
        P(("y", "z", "c", "x"), None),
        P(),
        P(),
        P(),
        P(),
        P(),
        P(),
        P("x", None, None),
        P("x"),
        P("x", None),
    )
    return jax.shard_map(
        body,
        mesh=torus,
        in_specs=placed,
        out_specs=(P("x"), P("x", None, None), P(), P(), P(), P()),
        check_vma=False,
    )
```

```python
import functools
import math

import jax
import jax.numpy as jnp
from jax import lax
from jax.experimental import pallas as pl
from jax.experimental.pallas import tpu as pltpu
from jax.sharding import Mesh, PartitionSpec as P

BF16 = jnp.bfloat16
F32 = jnp.float32
CHUNK = 128
GROUP = 10
AT_ONCE = 4
NOWHERE = -(1 << 30)
LINK = BF16
VMEM = pl.BlockSpec(memory_space=pltpu.VMEM)
ANY = pl.BlockSpec(memory_space=pl.ANY)
SMEM = pl.BlockSpec(memory_space=pltpu.SMEM)
PARAMS = pltpu.CompilerParams(vmem_limit_bytes=58 << 20)


def dot(a, b):
    return jnp.dot(a, b, preferred_element_type=F32)


def dot_t(a, b):
    return lax.dot_general(a, b, (((1,), (1,)), ((), ())), preferred_element_type=F32)


def hits_of(presence_ref, lanes, first_row):
    shape = (CHUNK // 16, 16, lanes.size)
    rows = 16 * lax.broadcasted_iota(jnp.int32, shape, 0) + lax.broadcasted_iota(jnp.int32, shape, 1)
    rows = rows.astype(F32).astype(BF16)
    local = jnp.clip(presence_ref[:, lanes] - first_row, -1, CHUNK).astype(F32)
    one, zero = jnp.full(shape, 1.0 / presence_ref.shape[0], BF16), jnp.zeros(shape, BF16)
    hits = zero
    for record in range(presence_ref.shape[0]):
        there = jnp.broadcast_to(local[record : record + 1], shape[1:]).astype(BF16)
        hits += jnp.where(rows == there[None], one, zero)
    return hits.reshape(CHUNK, lanes.size)


def fetch(sem, *pairs):
    copies = [pltpu.make_async_copy(*pair, sem.at[i]) for i, pair in enumerate(pairs)]
    for copy in copies:
        copy.start()
    return copies


class Part:
    def __init__(self, ref, start):
        self.ref, self.start = ref, start

    def __getitem__(self, i):
        return self.ref[self.start + i]


def scalar_parts(ref, blocks, block_count):
    starts = (2, 2 + blocks, 2 + 2 * blocks, 2 + 2 * blocks + block_count, 0)
    return [Part(ref, start) for start in starts]


def widen(wide_weight, head_weight, clade):
    slab = head_weight.shape[1]
    wide_weight[...] = jnp.zeros_like(wide_weight)
    for b in range(head_weight.shape[0]):
        half = pl.ds(pl.multiple_of((clade[b] % 2) * slab, slab), slab)
        wide_weight[b, half, :] = head_weight[b]


def each_busy(busy, found, count, act):
    def note(i, n):
        found[n] = i
        return n + jnp.where(busy[i] > 0, 1, 0)

    total = lax.fori_loop(0, count, note, 0)

    def step(j, carry):
        spots = [j * AT_ONCE + u for u in range(AT_ONCE)]
        act([(jnp.where(spot < total, found[spot], 0), spot < total) for spot in spots])
        return carry

    lax.fori_loop(0, (total + AT_ONCE - 1) // AT_ONCE, step, 0)


def forward_kernel(
    scalars,
    covariates_in,
    first_weight_in,
    first_bias_in,
    second_weight_in,
    second_bias_in,
    head_weight_in,
    terms_out,
    trunk_out,
    local_lse,
    high,
    covariates,
    first_weight,
    first_bias,
    second_weight,
    second_bias,
    head_weight,
    terms,
    trunk,
    wide_weight,
    logits,
    tops,
    fetch_sem,
    term_sem,
    trunk_sem,
):
    fetched = fetch(
        fetch_sem,
        (covariates_in, covariates),
        (first_weight_in, first_weight),
        (first_bias_in, first_bias),
        (second_weight_in, second_weight),
        (second_bias_in, second_bias),
        (head_weight_in, head_weight),
    )
    first_act, features, first_slope, second_slope = (trunk.at[i] for i in range(4))
    blocks, cells, tile = features.shape
    block_count, slab, _ = head_weight.shape
    first_index, second_index, clade, _, _ = scalar_parts(scalars, blocks, block_count)

    def layer(pre, act_ref, slope_ref, o):
        sigma = 1.0 / (1.0 + jnp.exp(-pre))
        act_ref[o] = (pre * sigma).astype(BF16)
        slope_ref[o] = (sigma * (1.0 + pre * (1.0 - sigma))).astype(BF16)

    for copy in fetched[:5]:
        copy.wait()
    for o in range(blocks):
        columns = pl.ds(pl.multiple_of(first_index[o] * tile, tile), tile)
        pre = dot(covariates[:, columns], first_weight[o]) + first_bias[o : o + 1, :]
        layer(pre, first_act, first_slope, o)
    for o in range(blocks):
        pre = dot(first_act[second_index[o]], second_weight[o]) + second_bias[o : o + 1, :]
        layer(pre, features, second_slope, o)

    trunk_copy = pltpu.make_async_copy(trunk, trunk_out, trunk_sem.at[0])
    trunk_copy.start()
    fetched[5].wait()
    widen(wide_weight, head_weight, clade)

    def step(i):
        for g in range(GROUP):
            b = i * GROUP + g
            part = dot(features[clade[b] // 2], wide_weight[b])
            logits[g] = part
            tops[g] = jnp.max(part.reshape(cells // 8, 8, -1), axis=0)
        for g in range(GROUP):
            b = i * GROUP + g
            top = jnp.max(tops[g], axis=0, keepdims=True)
            part = jnp.exp(logits[g] - top)
            terms[b] = part.astype(BF16)
            lse = top + jnp.log(jnp.sum(part, axis=0, keepdims=True))
            high[b : b + 1, :] = top
            for peer in range(local_lse.shape[0]):
                local_lse[peer, b : b + 1, :] = lse

    term_copies = []
    for i in range(block_count // GROUP):
        step(i)
        part = pl.ds(i * GROUP, GROUP)
        copy = pltpu.make_async_copy(terms.at[part], terms_out.at[part], term_sem.at[i])
        copy.start()
        term_copies.append(copy)
    for copy in term_copies:
        copy.wait()
    trunk_copy.wait()


def join(parts):
    top = functools.reduce(jnp.maximum, [parts[i] for i in range(len(parts))])
    return top + jnp.log(sum(jnp.exp(parts[i] - top) for i in range(len(parts))))


def early_kernel(
    scalars,
    covariates_in,
    trunk_in,
    terms_in,
    covariates_t,
    first_act_t,
    soft_grad,
    covariates,
    layers,
    terms,
    features_t,
    product,
    fetch_sem,
    term_sem,
):
    _, blocks, cells, tile = layers.shape
    block_count, slab, _ = soft_grad.shape
    _, _, clade, _, _ = scalar_parts(scalars, blocks, block_count)
    fetched = fetch(
        fetch_sem,
        (trunk_in.at[1], layers.at[1]),
        (trunk_in.at[0], layers.at[0]),
        (covariates_in, covariates),
    )
    pieces = [pl.ds(i * GROUP, GROUP) for i in range(block_count // GROUP)]
    term_copies = fetch(term_sem, *[(terms_in.at[p], terms.at[p]) for p in pieces])
    fetched[0].wait()
    for o in range(blocks):
        features_t[o] = layers[1, o].T
    fetched[1].wait()
    for o in range(blocks):
        first_act_t[o] = layers[0, o].T
    fetched[2].wait()
    for o in range(covariates.shape[1] // tile):
        covariates_t[o] = covariates[:, o * tile : (o + 1) * tile].T
    for i, copy in enumerate(term_copies):
        copy.wait()
        for g in range(GROUP):
            b = i * GROUP + g
            product[g] = dot(features_t[clade[b] // 2], terms[b])
        for g in range(GROUP):
            b = i * GROUP + g
            half = pl.ds(pl.multiple_of((clade[b] % 2) * slab, slab), slab)
            soft_grad[b] = product[g, half, :]


def middle_kernel(
    scalars,
    presence_in,
    head_weight_in,
    trunk_in,
    hit_back,
    hit_grad,
    hit_sum,
    presence,
    head_weight,
    features,
    wide_weight,
    back,
    found,
    fetch_sem,
):
    blocks, cells, tile = features.shape
    block_count, slab, _ = head_weight.shape
    _, _, clade, busy, place = scalar_parts(scalars, blocks, block_count)
    first_cell = place[0]
    fetched = fetch(
        fetch_sem,
        (head_weight_in, head_weight),
        (presence_in, presence),
        (trunk_in.at[1], features),
    )
    hit_grad[...] = jnp.zeros_like(hit_grad)
    back[...] = jnp.zeros_like(back)
    fetched[0].wait()
    widen(wide_weight, head_weight, clade)
    for copy in fetched[1:]:
        copy.wait()

    def add_hits(chosen):
        products = []
        for i, valid in chosen:
            b, start = i // (cells // CHUNK), pl.multiple_of((i % (cells // CHUNK)) * CHUNK, CHUNK)
            lanes = pl.ds(pl.multiple_of(b * tile, tile), tile)
            rows = pl.ds(start, CHUNK)
            hits = hits_of(presence, lanes, jnp.where(valid, first_cell + start, NOWHERE))
            grad = lax.dot_general(
                features[clade[b] // 2, rows, :],
                hits,
                (((0,), (0,)), ((), ())),
                preferred_element_type=F32,
            )
            products.append((b, rows, grad, dot_t(hits, wide_weight[b])))
        for b, rows, grad, part in products:
            hit_grad[b] += grad
            back[clade[b] // 2, rows, :] += part

    each_busy(busy, found, block_count * (cells // CHUNK), add_hits)
    for b in range(block_count):
        terms = hit_grad[b] * wide_weight[b].astype(F32)
        hit_sum[b : b + 1, :] = jnp.sum(terms, axis=0, keepdims=True)
    for o in range(blocks):
        hit_back[o] = back[o].astype(BF16)


def backward_kernel(
    scalars,
    second_weight_in,
    head_weight_in,
    terms_in,
    trunk_in,
    high_in,
    lses_in,
    covariates_t_in,
    first_act_t_in,
    soft_grad_in,
    hit_back_in,
    hit_grad_in,
    hit_sum_in,
    trunk,
    keep,
    send,
    lse,
    second_weight,
    head_weight,
    terms,
    slopes,
    high,
    lses,
    covariates_t,
    first_act_t,
    soft_grad,
    hit_back,
    hit_grad,
    hit_sum,
    wide_weight,
    packed,
    bias,
    weight_cells,
    group_back,
    act_grad,
    fetch_sem,
    term_sem,
):
    first_slope, second_slope = slopes.at[0], slopes.at[1]
    blocks, cells, tile = first_slope.shape
    block_count, slab, _ = head_weight.shape
    first_index, second_index, clade, _, place = scalar_parts(scalars, blocks, block_count)
    early = fetch(
        fetch_sem,
        (lses_in, lses),
        (high_in, high),
        (head_weight_in, head_weight),
    )
    pieces = [pl.ds(i * GROUP, GROUP) for i in range(block_count // GROUP)]
    term_copies = fetch(term_sem, *[(terms_in.at[p], terms.at[p]) for p in pieces])
    late = fetch(
        fetch_sem.at[pl.ds(len(early), 8)],
        (hit_back_in, hit_back),
        (hit_grad_in, hit_grad),
        (soft_grad_in, soft_grad),
        (trunk_in.at[pl.ds(2, 2)], slopes),
        (first_act_t_in, first_act_t),
        (second_weight_in, second_weight),
        (covariates_t_in, covariates_t),
        (hit_sum_in, hit_sum),
    )
    early[0].wait()
    early[1].wait()
    lse[...] = join([lses[i] for i in range(lses.shape[0])])
    high[...] = jnp.exp(high[...] - lse[...])
    early[2].wait()
    widen(wide_weight, head_weight, clade)
    group = block_count // 2
    core = place[1]

    act_grad[...] = jnp.zeros_like(act_grad)
    for i, copy in enumerate(term_copies):
        copy.wait()
        for b in range(i * GROUP, (i + 1) * GROUP):
            weights = terms[b].astype(F32) * high[b : b + 1, :]
            weight_cells[b] = weights.astype(BF16)
    for copy in late[:3]:
        copy.wait()
    for o in range(blocks):
        group_back[o] = -hit_back[o].astype(F32)
    for i in range(block_count // GROUP):
        for g in range(GROUP):
            b = i * GROUP + g
            half = pl.ds(pl.multiple_of((clade[b] % 2) * slab, slab), slab)
            rows = slice((b % group) * slab, (b % group + 1) * slab)
            grad = soft_grad[b] * high[b : b + 1, :] - hit_grad[b, half, :]
            packed[b // group, rows, :] = grad
            group_back[clade[b] // 2] += dot_t(weight_cells[b], wide_weight[b])

    for copy in late[3:]:
        copy.wait()
    bias[...] = jnp.zeros_like(bias)
    pair = blocks // (trunk.shape[0] // 2)

    def trunk_sums(o, layer, left, dz):
        part, at = layer * (trunk.shape[0] // 2) + o // pair, o % pair
        trunk[part, at * tile : (at + 1) * tile, :] = dot(left, dz).astype(LINK)
        bias[part, at : at + 1, :] = jnp.sum(dz.astype(F32), axis=0, keepdims=True)

    for o in range(blocks):
        dz = (group_back[o] * second_slope[o].astype(F32)).astype(BF16)
        trunk_sums(o, 1, first_act_t[second_index[o]], dz)
        act_grad[second_index[o]] += dot_t(dz, second_weight[o])
    for o in range(blocks):
        dz = (act_grad[o] * first_slope[o].astype(F32)).astype(BF16)
        trunk_sums(o, 0, covariates_t[first_index[o]], dz)
    for part in range(trunk.shape[0]):
        trunk[part, pair * tile :, :] = bias[part].astype(LINK)

    tail = group * slab
    for half in range(2):
        packed[half, tail:, :] = jnp.zeros((packed.shape[1] - tail, tile), F32)
        packed[half, tail : tail + group, :] = hit_sum[half * group : (half + 1) * group, :]
    keep[...] = packed[core]
    send[...] = packed[1 - core]


def finish_kernel(
    total_cells,
    scalars,
    trunk,
    own,
    other,
    lse,
    species_loss,
    head_grad,
    first_grad,
    first_bias_grad,
    second_grad,
    second_bias_grad,
    halves,
):
    core = scalars[1]
    blocks, tile, _ = first_grad.shape
    block_count, slab, _ = head_grad.shape
    group = block_count // 2
    halves[core] = own[...]
    halves[1 - core] = other[...]
    for b in range(block_count):
        rows = slice((b % group) * slab, (b % group + 1) * slab)
        head_grad[b] = halves[b // group, rows, :].astype(F32)
    tail = group * slab
    for half in range(2):
        rows = slice(half * group, (half + 1) * group)
        hit_mean = halves[half, tail:, :].astype(F32)[:group]
        species_loss[rows, :] = lse[rows, :] - math.log(total_cells) - hit_mean
    half = trunk.shape[0] // 2
    pair = blocks // half
    for layer, (grad, bias_grad) in enumerate(
        ((first_grad, first_bias_grad), (second_grad, second_bias_grad))
    ):
        for part in range(half):
            for at in range(pair):
                rows = slice(at * tile, (at + 1) * tile)
                grad[part * pair + at] = trunk[layer * half + part, rows, :].astype(F32)
            bias = trunk[layer * half + part, pair * tile :, :].astype(F32)
            bias_grad[part * pair : (part + 1) * pair, :] = bias[:pair]


def spread(value, axis, size):
    return lax.all_to_all(jnp.broadcast_to(value[None], (size, *value.shape)), axis, 0, 0)


def forward(
    peers,
    scalars,
    covariates,
    first_weight,
    first_bias,
    second_weight,
    second_bias,
    head_weight,
):
    blocks, tile, _ = first_weight.shape
    block_count, _, species = head_weight.shape
    cells = covariates.shape[0]
    by_clade = (block_count, cells, species)
    by_layer = (4, blocks, cells, tile)
    shape = jax.ShapeDtypeStruct
    return pl.pallas_call(
        forward_kernel,
        name="forward",
        out_shape=(
            shape(by_clade, BF16),
            shape(by_layer, BF16),
            shape((peers, block_count, species), F32),
            shape((block_count, species), F32),
        ),
        in_specs=[SMEM] + [ANY] * 6,
        out_specs=[ANY] * 2 + [VMEM] * 2,
        scratch_shapes=[
            pltpu.VMEM(covariates.shape, BF16),
            pltpu.VMEM(first_weight.shape, BF16),
            pltpu.VMEM((blocks, tile), F32),
            pltpu.VMEM(second_weight.shape, BF16),
            pltpu.VMEM((blocks, tile), F32),
            pltpu.VMEM(head_weight.shape, BF16),
            pltpu.VMEM(by_clade, BF16),
            pltpu.VMEM(by_layer, BF16),
            pltpu.VMEM((block_count, tile, species), BF16),
            pltpu.VMEM((GROUP, cells, species), F32),
            pltpu.VMEM((GROUP, 8, species), F32),
            pltpu.SemaphoreType.DMA((6,)),
            pltpu.SemaphoreType.DMA((block_count // GROUP,)),
            pltpu.SemaphoreType.DMA((1,)),
        ],
        compiler_params=PARAMS,
    )(
        scalars,
        covariates,
        first_weight,
        first_bias.reshape(blocks, tile),
        second_weight,
        second_bias.reshape(blocks, tile),
        head_weight,
    )


def early(scalars, covariates, layers, terms, slab):
    _, blocks, cells, tile = layers.shape
    block_count, _, species = terms.shape
    width = covariates.shape[1]
    shape = jax.ShapeDtypeStruct
    return pl.pallas_call(
        early_kernel,
        name="early",
        out_shape=(
            shape((width // tile, tile, cells), BF16),
            shape((blocks, tile, cells), BF16),
            shape((block_count, slab, species), F32),
        ),
        in_specs=[SMEM] + [ANY] * 3,
        out_specs=[VMEM] * 3,
        scratch_shapes=[
            pltpu.VMEM(covariates.shape, BF16),
            pltpu.VMEM((2, blocks, cells, tile), BF16),
            pltpu.VMEM(terms.shape, BF16),
            pltpu.VMEM((blocks, tile, cells), BF16),
            pltpu.VMEM((GROUP, tile, species), F32),
            pltpu.SemaphoreType.DMA((3,)),
            pltpu.SemaphoreType.DMA((block_count // GROUP,)),
        ],
        compiler_params=PARAMS,
        cost_estimate=pl.CostEstimate(
            flops=2 * terms.size * tile, bytes_accessed=6 * terms.size, transcendentals=0
        ),
    )(scalars, covariates, layers, terms)


def middle(scalars, presence_t, head_weight, layers):
    _, *by_block = layers.shape
    blocks, cells, tile = by_block
    block_count, _, species = head_weight.shape
    shape = jax.ShapeDtypeStruct
    return pl.pallas_call(
        middle_kernel,
        name="middle",
        out_shape=(
            shape(by_block, BF16),
            shape((block_count, tile, species), F32),
            shape((block_count, species), F32),
        ),
        in_specs=[SMEM] + [ANY] * 3,
        out_specs=[VMEM] * 3,
        scratch_shapes=[
            pltpu.VMEM(presence_t.shape, jnp.int32),
            pltpu.VMEM(head_weight.shape, BF16),
            pltpu.VMEM(by_block, BF16),
            pltpu.VMEM((block_count, tile, species), BF16),
            pltpu.VMEM(by_block, F32),
            pltpu.SMEM((block_count * (cells // CHUNK) + AT_ONCE,), jnp.int32),
            pltpu.SemaphoreType.DMA((3,)),
        ],
        compiler_params=PARAMS,
        cost_estimate=pl.CostEstimate(
            flops=8 * block_count * cells * species * tile,
            bytes_accessed=8 * blocks * cells * tile,
            transcendentals=0,
        ),
    )(scalars, presence_t, head_weight, layers)


def backward(
    scalars, second_weight, head_weight, terms, layers, high, lses, ready, hits, nx
):
    covariates_t, first_act_t, soft_grad = ready
    hit_back, hit_grad, hit_sum = hits
    _, *by_block = layers.shape
    blocks, cells, tile = by_block
    block_count, slab, species = head_weight.shape
    shape = jax.ShapeDtypeStruct
    pair = blocks // nx
    part_rows = pair * tile + 8
    group = block_count // 2
    half_rows = group * slab + -(-group // 8) * 8
    return pl.pallas_call(
        backward_kernel,
        name="backward",
        out_shape=(
            shape((2 * nx, part_rows, tile), LINK),
            shape((half_rows, tile), F32),
            shape((half_rows, tile), F32),
            shape((block_count, species), F32),
        ),
        in_specs=[SMEM] + [ANY] * 12,
        out_specs=[VMEM] * 4,
        scratch_shapes=[
            pltpu.VMEM(second_weight.shape, BF16),
            pltpu.VMEM(head_weight.shape, BF16),
            pltpu.VMEM(terms.shape, BF16),
            pltpu.VMEM((2, *by_block), BF16),
            pltpu.VMEM(high.shape, F32),
            pltpu.VMEM(lses.shape, F32),
            pltpu.VMEM(covariates_t.shape, BF16),
            pltpu.VMEM(first_act_t.shape, BF16),
            pltpu.VMEM(soft_grad.shape, F32),
            pltpu.VMEM(by_block, BF16),
            pltpu.VMEM(hit_grad.shape, F32),
            pltpu.VMEM(hit_sum.shape, F32),
            pltpu.VMEM((block_count, tile, species), BF16),
            pltpu.VMEM((2, half_rows, tile), F32),
            pltpu.VMEM((2 * nx, 8, tile), F32),
            pltpu.VMEM(terms.shape, BF16),
            pltpu.VMEM(by_block, F32),
            pltpu.VMEM(by_block, F32),
            pltpu.SemaphoreType.DMA((11,)),
            pltpu.SemaphoreType.DMA((block_count // GROUP,)),
        ],
        compiler_params=PARAMS,
    )(
        scalars,
        second_weight,
        head_weight,
        terms,
        layers,
        high,
        lses,
        covariates_t,
        first_act_t,
        soft_grad,
        hit_back,
        hit_grad,
        hit_sum,
    )


def body(
    covariates,
    first_weight,
    first_bias,
    first_index,
    second_weight,
    second_bias,
    second_index,
    head_weight,
    clade_block,
    presence,
):
    ny, nz, nx = lax.axis_size("y"), lax.axis_size("z"), lax.axis_size("x")
    core, mine = lax.axis_index("c"), lax.axis_index("x")
    swap = [(0, 1), (1, 0)]
    blocks, tile, _ = first_weight.shape
    block_count, slab, species = head_weight.shape
    records = presence.shape[1]
    own_cells, width = covariates.shape
    cells = own_cells * nx
    first_cell = ((lax.axis_index("y") * nz + lax.axis_index("z")) * 2 + core) * cells
    total_cells = ny * nz * 2 * cells

    presence_t = presence.T
    chunk_of = lax.shift_right_arithmetic(presence_t - first_cell, int(math.log2(CHUNK)))
    chunk_of = chunk_of.reshape(records, block_count, species)
    busy = jnp.stack(
        [jnp.any(chunk_of == k, axis=(0, 2)) for k in range(cells // CHUNK)], axis=1
    )
    busy = busy.astype(jnp.int32).reshape(-1)
    place = jnp.stack([first_cell, core]).astype(jnp.int32)
    scalars = jnp.concatenate([place, first_index, second_index, clade_block, busy])

    all_covariates = spread(covariates, "x", nx).reshape(cells, width)
    terms, layers, local_lse, high = forward(
        ny,
        scalars,
        all_covariates,
        first_weight,
        first_bias,
        second_weight,
        second_bias,
        head_weight,
    )
    lses = lax.all_to_all(local_lse, "y", 0, 0)
    ready = early(scalars, all_covariates, layers, terms, slab)
    lses, ready, later = lax.optimization_barrier((join(lses), ready, scalars))
    hits = middle(later, presence_t, head_weight, layers)
    lses = spread(lses, ("z", "c"), nz * 2)
    trunk, keep, send, lse = backward(
        scalars,
        second_weight,
        head_weight,
        terms,
        layers,
        high,
        lses,
        ready,
        hits,
        nx,
    )
    pair, group = blocks // nx, block_count // 2
    head_rows = group * slab
    half_rows = keep.shape[0]

    head = keep + lax.ppermute(send, "c", swap)
    trunk = jnp.sum(lax.all_to_all(trunk, ("c", "x"), 0, 0).astype(F32), axis=0)
    peers = ny * nz
    misc = jnp.concatenate([head[head_rows : head_rows + group], trunk[pair * tile :][:pair]])
    misc = jnp.pad(misc, ((0, peers - misc.shape[0]), (0, 0)))
    trunk_cut, head_cut = pair * tile // peers, head_rows // peers
    cut = jnp.concatenate(
        [
            trunk[: pair * tile].reshape(peers, trunk_cut, tile),
            head[:head_rows].reshape(peers, head_cut, tile),
            misc[:, None],
        ],
        axis=1,
    )
    cut = jnp.pad(cut, ((0, 0), (0, -cut.shape[1] % 8), (0, 0))).astype(LINK)
    cut = jnp.sum(lax.all_to_all(cut, ("y", "z"), 0, 0).astype(F32), axis=0).astype(LINK)

    cut = spread(cut, ("y", "z"), peers)
    misc = cut[:, trunk_cut + head_cut]
    head = jnp.concatenate(
        [
            cut[:, trunk_cut : trunk_cut + head_cut].reshape(head_rows, tile),
            jnp.pad(misc[:group], ((0, -group % 8), (0, 0))),
        ]
    )
    other_head = lax.ppermute(head, "c", swap)
    trunk = jnp.concatenate(
        [
            cut[:, :trunk_cut].reshape(pair * tile, tile),
            jnp.pad(misc[group : group + pair], ((0, -pair % 8), (0, 0))),
        ]
    )
    trunk = spread(trunk, ("c", "x"), 2 * nx)
    shape = jax.ShapeDtypeStruct
    species_loss, head_grad, first_grad, first_bias_grad, second_grad, second_bias_grad = (
        pl.pallas_call(
            functools.partial(finish_kernel, total_cells),
            name="finish",
            out_shape=(
                shape((block_count, species), F32),
                shape(head_weight.shape, F32),
                shape(first_weight.shape, F32),
                shape((blocks, tile), F32),
                shape(second_weight.shape, F32),
                shape((blocks, tile), F32),
            ),
            in_specs=[SMEM] + [VMEM] * 4,
            out_specs=[VMEM] * 6,
            scratch_shapes=[pltpu.VMEM((2, half_rows, tile), LINK)],
            compiler_params=pltpu.CompilerParams(vmem_limit_bytes=16 << 20),
        )(scalars, trunk, head, other_head, lse)
    )
    return (
        species_loss.reshape(-1),
        head_grad,
        first_grad,
        first_bias_grad.reshape(-1),
        second_grad,
        second_bias_grad.reshape(-1),
    )


def solution(mesh):
    devices = mesh.devices.reshape(8, mesh.shape["bg"] // 16, 2, mesh.shape["sp"])
    torus = Mesh(devices, ("y", "z", "c", "x"))
    placed = (
        P(("y", "z", "c", "x"), None),
        P(),
        P(),
        P(),
        P(),
        P(),
        P(),
        P("x", None, None),
        P("x"),
        P("x", None),
    )
    return jax.shard_map(
        body,
        mesh=torus,
        in_specs=placed,
        out_specs=(P("x"), P("x", None, None), P(), P(), P(), P()),
        check_vma=False,
    )
```

```python
import functools
import math

import jax
import jax.numpy as jnp
from jax import lax
from jax.experimental import pallas as pl
from jax.experimental.pallas import tpu as pltpu
from jax.sharding import Mesh, PartitionSpec as P

BF16 = jnp.bfloat16
F32 = jnp.float32
CHUNK = 128
GROUP = 10
AT_ONCE = 4
NOWHERE = -(1 << 30)
LINK = BF16
VMEM = pl.BlockSpec(memory_space=pltpu.VMEM)
ANY = pl.BlockSpec(memory_space=pl.ANY)
SMEM = pl.BlockSpec(memory_space=pltpu.SMEM)
PARAMS = pltpu.CompilerParams(vmem_limit_bytes=58 << 20)


def dot(a, b):
    return jnp.dot(a, b, preferred_element_type=F32)


def dot_t(a, b):
    return lax.dot_general(a, b, (((1,), (1,)), ((), ())), preferred_element_type=F32)


def hits_of(presence_ref, lanes, first_row):
    shape = (CHUNK // 16, 16, lanes.size)
    rows = 16 * lax.broadcasted_iota(jnp.int32, shape, 0) + lax.broadcasted_iota(jnp.int32, shape, 1)
    rows = rows.astype(F32).astype(BF16)
    local = jnp.clip(presence_ref[:, lanes] - first_row, -1, CHUNK).astype(F32)
    one, zero = jnp.full(shape, 1.0 / presence_ref.shape[0], BF16), jnp.zeros(shape, BF16)
    hits = zero
    for record in range(presence_ref.shape[0]):
        there = jnp.broadcast_to(local[record : record + 1], shape[1:]).astype(BF16)
        hits += jnp.where(rows == there[None], one, zero)
    return hits.reshape(CHUNK, lanes.size)


def fetch(sem, *pairs):
    copies = [pltpu.make_async_copy(*pair, sem.at[i]) for i, pair in enumerate(pairs)]
    for copy in copies:
        copy.start()
    return copies


class Part:
    def __init__(self, ref, start):
        self.ref, self.start = ref, start

    def __getitem__(self, i):
        return self.ref[self.start + i]


def scalar_parts(ref, blocks, block_count):
    starts = (2, 2 + blocks, 2 + 2 * blocks, 2 + 2 * blocks + block_count, 0)
    return [Part(ref, start) for start in starts]


def widen(wide_weight, head_weight, clade):
    slab = head_weight.shape[1]
    wide_weight[...] = jnp.zeros_like(wide_weight)
    for b in range(head_weight.shape[0]):
        half = pl.ds(pl.multiple_of((clade[b] % 2) * slab, slab), slab)
        wide_weight[b, half, :] = head_weight[b]


def widen_pairs(pairs, head_weight, clade):
    _, slab, species = head_weight.shape
    pairs[...] = jnp.zeros_like(pairs)
    for b in range(head_weight.shape[0]):
        start = pl.multiple_of((b % 2) * 2 * slab + (clade[b] % 2) * slab, slab)
        lanes = slice((b % 2) * species, (b % 2 + 1) * species)
        pairs[b // 2, pl.ds(start, slab), lanes] = head_weight[b]


def each_busy(busy, found, count, act):
    def note(i, n):
        found[n] = i
        return n + jnp.where(busy[i] > 0, 1, 0)

    total = lax.fori_loop(0, count, note, 0)

    def step(j, carry):
        spots = [j * AT_ONCE + u for u in range(AT_ONCE)]
        act([(jnp.where(spot < total, found[spot], 0), spot < total) for spot in spots])
        return carry

    lax.fori_loop(0, (total + AT_ONCE - 1) // AT_ONCE, step, 0)


def forward_kernel(
    scalars,
    covariates_in,
    first_weight_in,
    first_bias_in,
    second_weight_in,
    second_bias_in,
    head_weight_in,
    terms_out,
    trunk_out,
    local_lse,
    high,
    covariates,
    first_weight,
    first_bias,
    second_weight,
    second_bias,
    head_weight,
    terms,
    trunk,
    pairs,
    logits,
    tops,
    fetch_sem,
    term_sem,
    trunk_sem,
):
    fetched = fetch(
        fetch_sem,
        (covariates_in, covariates),
        (first_weight_in, first_weight),
        (first_bias_in, first_bias),
        (second_weight_in, second_weight),
        (second_bias_in, second_bias),
        (head_weight_in, head_weight),
    )
    first_act, features, first_slope, second_slope = (trunk.at[i] for i in range(4))
    blocks, cells, tile = features.shape
    block_count, slab, _ = head_weight.shape
    first_index, second_index, clade, _, _ = scalar_parts(scalars, blocks, block_count)

    def layer(pre, act_ref, slope_ref, o):
        sigma = 1.0 / (1.0 + jnp.exp(-pre))
        act_ref[o] = (pre * sigma).astype(BF16)
        slope_ref[o] = (sigma * (1.0 + pre * (1.0 - sigma))).astype(BF16)

    for copy in fetched[:5]:
        copy.wait()
    for o in range(blocks):
        columns = pl.ds(pl.multiple_of(first_index[o] * tile, tile), tile)
        pre = dot(covariates[:, columns], first_weight[o]) + first_bias[o : o + 1, :]
        layer(pre, first_act, first_slope, o)
    for o in range(blocks):
        pre = dot(first_act[second_index[o]], second_weight[o]) + second_bias[o : o + 1, :]
        layer(pre, features, second_slope, o)

    trunk_copy = pltpu.make_async_copy(trunk, trunk_out, trunk_sem.at[0])
    trunk_copy.start()
    fetched[5].wait()
    widen_pairs(pairs, head_weight, clade)

    def step(i):
        for g in range(0, GROUP, 2):
            b = i * GROUP + g
            left = [features[clade[b + j] // 2] for j in range(2)]
            both = dot(jnp.concatenate(left, axis=1), pairs[b // 2])
            for j in range(2):
                part = both[:, j * tile : (j + 1) * tile]
                logits[g + j] = part
                tops[g + j] = jnp.max(part.reshape(cells // 8, 8, -1), axis=0)
        for g in range(GROUP):
            b = i * GROUP + g
            top = jnp.max(tops[g], axis=0, keepdims=True)
            part = jnp.exp(logits[g] - top)
            terms[b] = part.astype(BF16)
            lse = top + jnp.log(jnp.sum(part, axis=0, keepdims=True))
            high[b : b + 1, :] = top
            for peer in range(local_lse.shape[0]):
                local_lse[peer, b : b + 1, :] = lse

    term_copies = []
    for i in range(block_count // GROUP):
        step(i)
        part = pl.ds(i * GROUP, GROUP)
        copy = pltpu.make_async_copy(terms.at[part], terms_out.at[part], term_sem.at[i])
        copy.start()
        term_copies.append(copy)
    for copy in term_copies:
        copy.wait()
    trunk_copy.wait()


def join(parts):
    top = functools.reduce(jnp.maximum, [parts[i] for i in range(len(parts))])
    return top + jnp.log(sum(jnp.exp(parts[i] - top) for i in range(len(parts))))


def early_kernel(
    scalars,
    covariates_in,
    trunk_in,
    terms_in,
    covariates_t,
    first_act_t,
    soft_grad,
    covariates,
    layers,
    terms,
    features_t,
    product,
    fetch_sem,
    term_sem,
):
    _, blocks, cells, tile = layers.shape
    block_count, slab, _ = soft_grad.shape
    _, _, clade, _, _ = scalar_parts(scalars, blocks, block_count)
    fetched = fetch(
        fetch_sem,
        (trunk_in.at[1], layers.at[1]),
        (trunk_in.at[0], layers.at[0]),
        (covariates_in, covariates),
    )
    pieces = [pl.ds(i * GROUP, GROUP) for i in range(block_count // GROUP)]
    term_copies = fetch(term_sem, *[(terms_in.at[p], terms.at[p]) for p in pieces])
    fetched[0].wait()
    for o in range(blocks):
        features_t[o] = layers[1, o].T
    fetched[1].wait()
    for o in range(blocks):
        first_act_t[o] = layers[0, o].T
    fetched[2].wait()
    for o in range(covariates.shape[1] // tile):
        covariates_t[o] = covariates[:, o * tile : (o + 1) * tile].T
    for i, copy in enumerate(term_copies):
        copy.wait()
        for g in range(GROUP):
            b = i * GROUP + g
            product[g] = dot(features_t[clade[b] // 2], terms[b])
        for g in range(GROUP):
            b = i * GROUP + g
            half = pl.ds(pl.multiple_of((clade[b] % 2) * slab, slab), slab)
            soft_grad[b] = product[g, half, :]


def middle_kernel(
    scalars,
    presence_in,
    head_weight_in,
    trunk_in,
    hit_back,
    hit_grad,
    hit_sum,
    presence,
    head_weight,
    features,
    wide_weight,
    back,
    found,
    fetch_sem,
):
    blocks, cells, tile = features.shape
    block_count, slab, _ = head_weight.shape
    _, _, clade, busy, place = scalar_parts(scalars, blocks, block_count)
    first_cell = place[0]
    fetched = fetch(
        fetch_sem,
        (head_weight_in, head_weight),
        (presence_in, presence),
        (trunk_in.at[1], features),
    )
    hit_grad[...] = jnp.zeros_like(hit_grad)
    back[...] = jnp.zeros_like(back)
    fetched[0].wait()
    widen(wide_weight, head_weight, clade)
    for copy in fetched[1:]:
        copy.wait()

    def add_hits(chosen):
        products = []
        for i, valid in chosen:
            b, start = i // (cells // CHUNK), pl.multiple_of((i % (cells // CHUNK)) * CHUNK, CHUNK)
            lanes = pl.ds(pl.multiple_of(b * tile, tile), tile)
            rows = pl.ds(start, CHUNK)
            hits = hits_of(presence, lanes, jnp.where(valid, first_cell + start, NOWHERE))
            grad = lax.dot_general(
                features[clade[b] // 2, rows, :],
                hits,
                (((0,), (0,)), ((), ())),
                preferred_element_type=F32,
            )
            products.append((b, rows, grad, dot_t(hits, wide_weight[b])))
        for b, rows, grad, part in products:
            hit_grad[b] += grad
            back[clade[b] // 2, rows, :] += part

    each_busy(busy, found, block_count * (cells // CHUNK), add_hits)
    for b in range(block_count):
        terms = hit_grad[b] * wide_weight[b].astype(F32)
        hit_sum[b : b + 1, :] = jnp.sum(terms, axis=0, keepdims=True)
    for o in range(blocks):
        hit_back[o] = back[o].astype(BF16)


def backward_kernel(
    scalars,
    second_weight_in,
    head_weight_in,
    terms_in,
    trunk_in,
    high_in,
    lses_in,
    covariates_t_in,
    first_act_t_in,
    soft_grad_in,
    hit_back_in,
    hit_grad_in,
    hit_sum_in,
    trunk,
    keep,
    send,
    lse,
    second_weight,
    head_weight,
    terms,
    slopes,
    high,
    lses,
    covariates_t,
    first_act_t,
    soft_grad,
    hit_back,
    hit_grad,
    hit_sum,
    pairs,
    packed,
    bias,
    weight_cells,
    group_back,
    act_grad,
    fetch_sem,
    term_sem,
):
    first_slope, second_slope = slopes.at[0], slopes.at[1]
    blocks, cells, tile = first_slope.shape
    block_count, slab, _ = head_weight.shape
    first_index, second_index, clade, _, place = scalar_parts(scalars, blocks, block_count)
    early = fetch(
        fetch_sem,
        (lses_in, lses),
        (high_in, high),
        (head_weight_in, head_weight),
    )
    pieces = [pl.ds(i * GROUP, GROUP) for i in range(block_count // GROUP)]
    term_copies = fetch(term_sem, *[(terms_in.at[p], terms.at[p]) for p in pieces])
    late = fetch(
        fetch_sem.at[pl.ds(len(early), 8)],
        (hit_back_in, hit_back),
        (hit_grad_in, hit_grad),
        (soft_grad_in, soft_grad),
        (trunk_in.at[pl.ds(2, 2)], slopes),
        (first_act_t_in, first_act_t),
        (second_weight_in, second_weight),
        (covariates_t_in, covariates_t),
        (hit_sum_in, hit_sum),
    )
    early[0].wait()
    early[1].wait()
    lse[...] = join([lses[i] for i in range(lses.shape[0])])
    high[...] = jnp.exp(high[...] - lse[...])
    early[2].wait()
    widen_pairs(pairs, head_weight, clade)
    group = block_count // 2
    core = place[1]

    act_grad[...] = jnp.zeros_like(act_grad)
    for i, copy in enumerate(term_copies):
        copy.wait()
        for b in range(i * GROUP, (i + 1) * GROUP):
            weights = terms[b].astype(F32) * high[b : b + 1, :]
            weight_cells[b] = weights.astype(BF16)
    for copy in late[:3]:
        copy.wait()
    for o in range(blocks):
        group_back[o] = -hit_back[o].astype(F32)
    for i in range(block_count // GROUP):
        for g in range(GROUP):
            b = i * GROUP + g
            half = pl.ds(pl.multiple_of((clade[b] % 2) * slab, slab), slab)
            rows = slice((b % group) * slab, (b % group + 1) * slab)
            grad = soft_grad[b] * high[b : b + 1, :] - hit_grad[b, half, :]
            packed[b // group, rows, :] = grad
        for g in range(0, GROUP, 2):
            b = i * GROUP + g
            left = [weight_cells[b + j] for j in range(2)]
            both = dot_t(jnp.concatenate(left, axis=1), pairs[b // 2])
            for j in range(2):
                group_back[clade[b + j] // 2] += both[:, j * tile : (j + 1) * tile]

    for copy in late[3:]:
        copy.wait()
    bias[...] = jnp.zeros_like(bias)
    pair = blocks // (trunk.shape[0] // 2)

    def trunk_sums(o, layer, left, dz):
        part, at = layer * (trunk.shape[0] // 2) + o // pair, o % pair
        trunk[part, at * tile : (at + 1) * tile, :] = dot(left, dz).astype(LINK)
        bias[part, at : at + 1, :] = jnp.sum(dz.astype(F32), axis=0, keepdims=True)

    for o in range(blocks):
        dz = (group_back[o] * second_slope[o].astype(F32)).astype(BF16)
        trunk_sums(o, 1, first_act_t[second_index[o]], dz)
        act_grad[second_index[o]] += dot_t(dz, second_weight[o])
    for o in range(blocks):
        dz = (act_grad[o] * first_slope[o].astype(F32)).astype(BF16)
        trunk_sums(o, 0, covariates_t[first_index[o]], dz)
    for part in range(trunk.shape[0]):
        trunk[part, pair * tile :, :] = bias[part].astype(LINK)

    tail = group * slab
    for half in range(2):
        packed[half, tail:, :] = jnp.zeros((packed.shape[1] - tail, tile), F32)
        packed[half, tail : tail + group, :] = hit_sum[half * group : (half + 1) * group, :]
    keep[...] = packed[core]
    send[...] = packed[1 - core]


def finish_kernel(
    total_cells,
    scalars,
    trunk,
    own,
    other,
    lse,
    species_loss,
    head_grad,
    first_grad,
    first_bias_grad,
    second_grad,
    second_bias_grad,
    halves,
):
    core = scalars[1]
    blocks, tile, _ = first_grad.shape
    block_count, slab, _ = head_grad.shape
    group = block_count // 2
    halves[core] = own[...]
    halves[1 - core] = other[...]
    for b in range(block_count):
        rows = slice((b % group) * slab, (b % group + 1) * slab)
        head_grad[b] = halves[b // group, rows, :].astype(F32)
    tail = group * slab
    for half in range(2):
        rows = slice(half * group, (half + 1) * group)
        hit_mean = halves[half, tail:, :].astype(F32)[:group]
        species_loss[rows, :] = lse[rows, :] - math.log(total_cells) - hit_mean
    half = trunk.shape[0] // 2
    pair = blocks // half
    for layer, (grad, bias_grad) in enumerate(
        ((first_grad, first_bias_grad), (second_grad, second_bias_grad))
    ):
        for part in range(half):
            for at in range(pair):
                rows = slice(at * tile, (at + 1) * tile)
                grad[part * pair + at] = trunk[layer * half + part, rows, :].astype(F32)
            bias = trunk[layer * half + part, pair * tile :, :].astype(F32)
            bias_grad[part * pair : (part + 1) * pair, :] = bias[:pair]


def spread(value, axis, size):
    return lax.all_to_all(jnp.broadcast_to(value[None], (size, *value.shape)), axis, 0, 0)


def forward(
    peers,
    scalars,
    covariates,
    first_weight,
    first_bias,
    second_weight,
    second_bias,
    head_weight,
):
    blocks, tile, _ = first_weight.shape
    block_count, _, species = head_weight.shape
    cells = covariates.shape[0]
    by_clade = (block_count, cells, species)
    by_layer = (4, blocks, cells, tile)
    shape = jax.ShapeDtypeStruct
    return pl.pallas_call(
        forward_kernel,
        name="forward",
        out_shape=(
            shape(by_clade, BF16),
            shape(by_layer, BF16),
            shape((peers, block_count, species), F32),
            shape((block_count, species), F32),
        ),
        in_specs=[SMEM] + [ANY] * 6,
        out_specs=[ANY] * 2 + [VMEM] * 2,
        scratch_shapes=[
            pltpu.VMEM(covariates.shape, BF16),
            pltpu.VMEM(first_weight.shape, BF16),
            pltpu.VMEM((blocks, tile), F32),
            pltpu.VMEM(second_weight.shape, BF16),
            pltpu.VMEM((blocks, tile), F32),
            pltpu.VMEM(head_weight.shape, BF16),
            pltpu.VMEM(by_clade, BF16),
            pltpu.VMEM(by_layer, BF16),
            pltpu.VMEM((block_count // 2, 2 * tile, 2 * species), BF16),
            pltpu.VMEM((GROUP, cells, species), F32),
            pltpu.VMEM((GROUP, 8, species), F32),
            pltpu.SemaphoreType.DMA((6,)),
            pltpu.SemaphoreType.DMA((block_count // GROUP,)),
            pltpu.SemaphoreType.DMA((1,)),
        ],
        compiler_params=PARAMS,
    )(
        scalars,
        covariates,
        first_weight,
        first_bias.reshape(blocks, tile),
        second_weight,
        second_bias.reshape(blocks, tile),
        head_weight,
    )


def early(scalars, covariates, layers, terms, slab):
    _, blocks, cells, tile = layers.shape
    block_count, _, species = terms.shape
    width = covariates.shape[1]
    shape = jax.ShapeDtypeStruct
    return pl.pallas_call(
        early_kernel,
        name="early",
        out_shape=(
            shape((width // tile, tile, cells), BF16),
            shape((blocks, tile, cells), BF16),
            shape((block_count, slab, species), F32),
        ),
        in_specs=[SMEM] + [ANY] * 3,
        out_specs=[VMEM] * 3,
        scratch_shapes=[
            pltpu.VMEM(covariates.shape, BF16),
            pltpu.VMEM((2, blocks, cells, tile), BF16),
            pltpu.VMEM(terms.shape, BF16),
            pltpu.VMEM((blocks, tile, cells), BF16),
            pltpu.VMEM((GROUP, tile, species), F32),
            pltpu.SemaphoreType.DMA((3,)),
            pltpu.SemaphoreType.DMA((block_count // GROUP,)),
        ],
        compiler_params=PARAMS,
        cost_estimate=pl.CostEstimate(
            flops=2 * terms.size * tile, bytes_accessed=6 * terms.size, transcendentals=0
        ),
    )(scalars, covariates, layers, terms)


def middle(scalars, presence_t, head_weight, layers):
    _, *by_block = layers.shape
    blocks, cells, tile = by_block
    block_count, _, species = head_weight.shape
    shape = jax.ShapeDtypeStruct
    return pl.pallas_call(
        middle_kernel,
        name="middle",
        out_shape=(
            shape(by_block, BF16),
            shape((block_count, tile, species), F32),
            shape((block_count, species), F32),
        ),
        in_specs=[SMEM] + [ANY] * 3,
        out_specs=[VMEM] * 3,
        scratch_shapes=[
            pltpu.VMEM(presence_t.shape, jnp.int32),
            pltpu.VMEM(head_weight.shape, BF16),
            pltpu.VMEM(by_block, BF16),
            pltpu.VMEM((block_count, tile, species), BF16),
            pltpu.VMEM(by_block, F32),
            pltpu.SMEM((block_count * (cells // CHUNK) + AT_ONCE,), jnp.int32),
            pltpu.SemaphoreType.DMA((3,)),
        ],
        compiler_params=PARAMS,
        cost_estimate=pl.CostEstimate(
            flops=8 * block_count * cells * species * tile,
            bytes_accessed=8 * blocks * cells * tile,
            transcendentals=0,
        ),
    )(scalars, presence_t, head_weight, layers)


def backward(
    scalars, second_weight, head_weight, terms, layers, high, lses, ready, hits, nx
):
    covariates_t, first_act_t, soft_grad = ready
    hit_back, hit_grad, hit_sum = hits
    _, *by_block = layers.shape
    blocks, cells, tile = by_block
    block_count, slab, species = head_weight.shape
    shape = jax.ShapeDtypeStruct
    pair = blocks // nx
    part_rows = pair * tile + 8
    group = block_count // 2
    half_rows = group * slab + -(-group // 8) * 8
    return pl.pallas_call(
        backward_kernel,
        name="backward",
        out_shape=(
            shape((2 * nx, part_rows, tile), LINK),
            shape((half_rows, tile), F32),
            shape((half_rows, tile), F32),
            shape((block_count, species), F32),
        ),
        in_specs=[SMEM] + [ANY] * 12,
        out_specs=[VMEM] * 4,
        scratch_shapes=[
            pltpu.VMEM(second_weight.shape, BF16),
            pltpu.VMEM(head_weight.shape, BF16),
            pltpu.VMEM(terms.shape, BF16),
            pltpu.VMEM((2, *by_block), BF16),
            pltpu.VMEM(high.shape, F32),
            pltpu.VMEM(lses.shape, F32),
            pltpu.VMEM(covariates_t.shape, BF16),
            pltpu.VMEM(first_act_t.shape, BF16),
            pltpu.VMEM(soft_grad.shape, F32),
            pltpu.VMEM(by_block, BF16),
            pltpu.VMEM(hit_grad.shape, F32),
            pltpu.VMEM(hit_sum.shape, F32),
            pltpu.VMEM((block_count // 2, 2 * tile, 2 * species), BF16),
            pltpu.VMEM((2, half_rows, tile), F32),
            pltpu.VMEM((2 * nx, 8, tile), F32),
            pltpu.VMEM(terms.shape, BF16),
            pltpu.VMEM(by_block, F32),
            pltpu.VMEM(by_block, F32),
            pltpu.SemaphoreType.DMA((11,)),
            pltpu.SemaphoreType.DMA((block_count // GROUP,)),
        ],
        compiler_params=PARAMS,
    )(
        scalars,
        second_weight,
        head_weight,
        terms,
        layers,
        high,
        lses,
        covariates_t,
        first_act_t,
        soft_grad,
        hit_back,
        hit_grad,
        hit_sum,
    )


def body(
    covariates,
    first_weight,
    first_bias,
    first_index,
    second_weight,
    second_bias,
    second_index,
    head_weight,
    clade_block,
    presence,
):
    ny, nz, nx = lax.axis_size("y"), lax.axis_size("z"), lax.axis_size("x")
    core, mine = lax.axis_index("c"), lax.axis_index("x")
    swap = [(0, 1), (1, 0)]
    blocks, tile, _ = first_weight.shape
    block_count, slab, species = head_weight.shape
    records = presence.shape[1]
    own_cells, width = covariates.shape
    cells = own_cells * nx
    first_cell = ((lax.axis_index("y") * nz + lax.axis_index("z")) * 2 + core) * cells
    total_cells = ny * nz * 2 * cells

    presence_t = presence.T
    chunk_of = lax.shift_right_arithmetic(presence_t - first_cell, int(math.log2(CHUNK)))
    chunk_of = chunk_of.reshape(records, block_count, species)
    busy = jnp.stack(
        [jnp.any(chunk_of == k, axis=(0, 2)) for k in range(cells // CHUNK)], axis=1
    )
    busy = busy.astype(jnp.int32).reshape(-1)
    place = jnp.stack([first_cell, core]).astype(jnp.int32)
    scalars = jnp.concatenate([place, first_index, second_index, clade_block, busy])

    all_covariates = spread(covariates, "x", nx).reshape(cells, width)
    terms, layers, local_lse, high = forward(
        ny,
        scalars,
        all_covariates,
        first_weight,
        first_bias,
        second_weight,
        second_bias,
        head_weight,
    )
    lses = lax.all_to_all(local_lse, "y", 0, 0)
    ready = early(scalars, all_covariates, layers, terms, slab)
    lses, ready, later = lax.optimization_barrier((join(lses), ready, scalars))
    hits = middle(later, presence_t, head_weight, layers)
    lses = spread(lses, ("z", "c"), nz * 2)
    trunk, keep, send, lse = backward(
        scalars,
        second_weight,
        head_weight,
        terms,
        layers,
        high,
        lses,
        ready,
        hits,
        nx,
    )
    pair, group = blocks // nx, block_count // 2
    head_rows = group * slab
    half_rows = keep.shape[0]

    head = keep + lax.ppermute(send, "c", swap)
    trunk = jnp.sum(lax.all_to_all(trunk, ("c", "x"), 0, 0).astype(F32), axis=0)
    peers = ny * nz
    misc = jnp.concatenate([head[head_rows : head_rows + group], trunk[pair * tile :][:pair]])
    misc = jnp.pad(misc, ((0, peers - misc.shape[0]), (0, 0)))
    trunk_cut, head_cut = pair * tile // peers, head_rows // peers
    cut = jnp.concatenate(
        [
            trunk[: pair * tile].reshape(peers, trunk_cut, tile),
            head[:head_rows].reshape(peers, head_cut, tile),
            misc[:, None],
        ],
        axis=1,
    )
    cut = jnp.pad(cut, ((0, 0), (0, -cut.shape[1] % 8), (0, 0))).astype(LINK)
    cut = jnp.sum(lax.all_to_all(cut, ("y", "z"), 0, 0).astype(F32), axis=0).astype(LINK)

    cut = spread(cut, ("y", "z"), peers)
    misc = cut[:, trunk_cut + head_cut]
    head = jnp.concatenate(
        [
            cut[:, trunk_cut : trunk_cut + head_cut].reshape(head_rows, tile),
            jnp.pad(misc[:group], ((0, -group % 8), (0, 0))),
        ]
    )
    other_head = lax.ppermute(head, "c", swap)
    trunk = jnp.concatenate(
        [
            cut[:, :trunk_cut].reshape(pair * tile, tile),
            jnp.pad(misc[group : group + pair], ((0, -pair % 8), (0, 0))),
        ]
    )
    trunk = spread(trunk, ("c", "x"), 2 * nx)
    shape = jax.ShapeDtypeStruct
    species_loss, head_grad, first_grad, first_bias_grad, second_grad, second_bias_grad = (
        pl.pallas_call(
            functools.partial(finish_kernel, total_cells),
            name="finish",
            out_shape=(
                shape((block_count, species), F32),
                shape(head_weight.shape, F32),
                shape(first_weight.shape, F32),
                shape((blocks, tile), F32),
                shape(second_weight.shape, F32),
                shape((blocks, tile), F32),
            ),
            in_specs=[SMEM] + [VMEM] * 4,
            out_specs=[VMEM] * 6,
            scratch_shapes=[pltpu.VMEM((2, half_rows, tile), LINK)],
            compiler_params=pltpu.CompilerParams(vmem_limit_bytes=16 << 20),
        )(scalars, trunk, head, other_head, lse)
    )
    return (
        species_loss.reshape(-1),
        head_grad,
        first_grad,
        first_bias_grad.reshape(-1),
        second_grad,
        second_bias_grad.reshape(-1),
    )


def solution(mesh):
    devices = mesh.devices.reshape(8, mesh.shape["bg"] // 16, 2, mesh.shape["sp"])
    torus = Mesh(devices, ("y", "z", "c", "x"))
    placed = (
        P(("y", "z", "c", "x"), None),
        P(),
        P(),
        P(),
        P(),
        P(),
        P(),
        P("x", None, None),
        P("x"),
        P("x", None),
    )
    return jax.shard_map(
        body,
        mesh=torus,
        in_specs=placed,
        out_specs=(P("x"), P("x", None, None), P(), P(), P(), P()),
        check_vma=False,
    )
```

```python
import functools
import math

import jax
import jax.numpy as jnp
from jax import lax
from jax.experimental import pallas as pl
from jax.experimental.pallas import tpu as pltpu
from jax.sharding import Mesh, PartitionSpec as P

BF16 = jnp.bfloat16
F32 = jnp.float32
CHUNK = 128
GROUP = 10
AT_ONCE = 4
NOWHERE = -(1 << 30)
LINK = BF16
VMEM = pl.BlockSpec(memory_space=pltpu.VMEM)
ANY = pl.BlockSpec(memory_space=pl.ANY)
SMEM = pl.BlockSpec(memory_space=pltpu.SMEM)
PARAMS = pltpu.CompilerParams(vmem_limit_bytes=58 << 20)


def dot(a, b):
    return jnp.dot(a, b, preferred_element_type=F32)


def dot_t(a, b):
    return lax.dot_general(a, b, (((1,), (1,)), ((), ())), preferred_element_type=F32)


def hits_of(presence_ref, lanes, first_row):
    shape = (CHUNK // 16, 16, lanes.size)
    rows = 16 * lax.broadcasted_iota(jnp.int32, shape, 0) + lax.broadcasted_iota(jnp.int32, shape, 1)
    rows = rows.astype(F32).astype(BF16)
    local = jnp.clip(presence_ref[:, lanes] - first_row, -1, CHUNK).astype(F32)
    one, zero = jnp.full(shape, 1.0 / presence_ref.shape[0], BF16), jnp.zeros(shape, BF16)
    hits = zero
    for record in range(presence_ref.shape[0]):
        there = jnp.broadcast_to(local[record : record + 1], shape[1:]).astype(BF16)
        hits += jnp.where(rows == there[None], one, zero)
    return hits.reshape(CHUNK, lanes.size)


def fetch(sem, *pairs):
    copies = [pltpu.make_async_copy(*pair, sem.at[i]) for i, pair in enumerate(pairs)]
    for copy in copies:
        copy.start()
    return copies


class Part:
    def __init__(self, ref, start):
        self.ref, self.start = ref, start

    def __getitem__(self, i):
        return self.ref[self.start + i]


def scalar_parts(ref, blocks, block_count):
    starts = (2, 2 + blocks, 2 + 2 * blocks, 2 + 2 * blocks + block_count, 0)
    return [Part(ref, start) for start in starts]


def widen(wide_weight, head_weight, clade):
    slab = head_weight.shape[1]
    wide_weight[...] = jnp.zeros_like(wide_weight)
    for b in range(head_weight.shape[0]):
        half = pl.ds(pl.multiple_of((clade[b] % 2) * slab, slab), slab)
        wide_weight[b, half, :] = head_weight[b]


def each_busy(busy, found, count, act):
    def note(i, n):
        found[n] = i
        return n + jnp.where(busy[i] > 0, 1, 0)

    total = lax.fori_loop(0, count, note, 0)

    def step(j, carry):
        spots = [j * AT_ONCE + u for u in range(AT_ONCE)]
        act([(jnp.where(spot < total, found[spot], 0), spot < total) for spot in spots])
        return carry

    lax.fori_loop(0, (total + AT_ONCE - 1) // AT_ONCE, step, 0)


def forward_kernel(
    scalars,
    covariates_in,
    first_weight_in,
    first_bias_in,
    second_weight_in,
    second_bias_in,
    head_weight_in,
    terms_out,
    trunk_out,
    local_lse,
    high,
    covariates,
    first_weight,
    first_bias,
    second_weight,
    second_bias,
    head_weight,
    terms,
    trunk,
    wide_weight,
    logits,
    tops,
    fetch_sem,
    term_sem,
    trunk_sem,
):
    fetched = fetch(
        fetch_sem,
        (covariates_in, covariates),
        (first_weight_in, first_weight),
        (first_bias_in, first_bias),
        (second_weight_in, second_weight),
        (second_bias_in, second_bias),
        (head_weight_in, head_weight),
    )
    first_act, features, first_slope, second_slope = (trunk.at[i] for i in range(4))
    blocks, cells, tile = features.shape
    block_count, slab, _ = head_weight.shape
    first_index, second_index, clade, _, _ = scalar_parts(scalars, blocks, block_count)

    def layer(pre, act_ref, slope_ref, o):
        sigma = 1.0 / (1.0 + jnp.exp(-pre))
        act_ref[o] = (pre * sigma).astype(BF16)
        slope_ref[o] = (sigma * (1.0 + pre * (1.0 - sigma))).astype(BF16)

    for copy in fetched[:5]:
        copy.wait()
    for o in range(blocks):
        columns = pl.ds(pl.multiple_of(first_index[o] * tile, tile), tile)
        pre = dot(covariates[:, columns], first_weight[o]) + first_bias[o : o + 1, :]
        layer(pre, first_act, first_slope, o)
    for o in range(blocks):
        pre = dot(first_act[second_index[o]], second_weight[o]) + second_bias[o : o + 1, :]
        layer(pre, features, second_slope, o)

    trunk_copy = pltpu.make_async_copy(trunk, trunk_out, trunk_sem.at[0])
    trunk_copy.start()
    fetched[5].wait()
    widen(wide_weight, head_weight, clade)

    def step(i):
        for g in range(GROUP):
            b = i * GROUP + g
            part = dot(features[clade[b] // 2], wide_weight[b])
            logits[g] = part
            tops[g] = jnp.max(part.reshape(cells // 8, 8, -1), axis=0)
        for g in range(GROUP):
            b = i * GROUP + g
            top = jnp.max(tops[g], axis=0, keepdims=True)
            part = jnp.exp(logits[g] - top)
            terms[b] = part.astype(BF16)
            lse = top + jnp.log(jnp.sum(part, axis=0, keepdims=True))
            high[b : b + 1, :] = top
            for peer in range(local_lse.shape[0]):
                local_lse[peer, b : b + 1, :] = lse

    term_copies = []
    for i in range(block_count // GROUP):
        step(i)
        part = pl.ds(i * GROUP, GROUP)
        copy = pltpu.make_async_copy(terms.at[part], terms_out.at[part], term_sem.at[i])
        copy.start()
        term_copies.append(copy)
    for copy in term_copies:
        copy.wait()
    trunk_copy.wait()


def join(parts):
    top = functools.reduce(jnp.maximum, [parts[i] for i in range(len(parts))])
    return top + jnp.log(sum(jnp.exp(parts[i] - top) for i in range(len(parts))))


def early_kernel(
    scalars,
    covariates_in,
    trunk_in,
    terms_in,
    covariates_t,
    first_act_t,
    soft_grad,
    covariates,
    layers,
    terms,
    features_t,
    product,
    fetch_sem,
    term_sem,
):
    _, blocks, cells, tile = layers.shape
    block_count, slab, _ = soft_grad.shape
    _, _, clade, _, _ = scalar_parts(scalars, blocks, block_count)
    fetched = fetch(
        fetch_sem,
        (trunk_in.at[1], layers.at[1]),
        (trunk_in.at[0], layers.at[0]),
        (covariates_in, covariates),
    )
    pieces = [pl.ds(i * GROUP, GROUP) for i in range(block_count // GROUP)]
    term_copies = fetch(term_sem, *[(terms_in.at[p], terms.at[p]) for p in pieces])
    fetched[0].wait()
    for o in range(blocks):
        features_t[o] = layers[1, o].T
    fetched[1].wait()
    for o in range(blocks):
        first_act_t[o] = layers[0, o].T
    fetched[2].wait()
    for o in range(covariates.shape[1] // tile):
        covariates_t[o] = covariates[:, o * tile : (o + 1) * tile].T
    for i, copy in enumerate(term_copies):
        copy.wait()
        for g in range(GROUP):
            b = i * GROUP + g
            product[g] = dot(features_t[clade[b] // 2], terms[b])
        for g in range(GROUP):
            b = i * GROUP + g
            half = pl.ds(pl.multiple_of((clade[b] % 2) * slab, slab), slab)
            soft_grad[b] = product[g, half, :]


def middle_kernel(
    scalars,
    presence_in,
    head_weight_in,
    trunk_in,
    hit_back,
    hit_grad,
    hit_sum,
    presence,
    head_weight,
    features,
    wide_weight,
    back,
    found,
    fetch_sem,
):
    blocks, cells, tile = features.shape
    block_count, slab, _ = head_weight.shape
    _, _, clade, busy, place = scalar_parts(scalars, blocks, block_count)
    first_cell = place[0]
    fetched = fetch(
        fetch_sem,
        (head_weight_in, head_weight),
        (presence_in, presence),
        (trunk_in.at[1], features),
    )
    hit_grad[...] = jnp.zeros_like(hit_grad)
    back[...] = jnp.zeros_like(back)
    fetched[0].wait()
    widen(wide_weight, head_weight, clade)
    for copy in fetched[1:]:
        copy.wait()

    def add_hits(chosen):
        products = []
        for i, valid in chosen:
            b, start = i // (cells // CHUNK), pl.multiple_of((i % (cells // CHUNK)) * CHUNK, CHUNK)
            lanes = pl.ds(pl.multiple_of(b * tile, tile), tile)
            rows = pl.ds(start, CHUNK)
            hits = hits_of(presence, lanes, jnp.where(valid, first_cell + start, NOWHERE))
            grad = lax.dot_general(
                features[clade[b] // 2, rows, :],
                hits,
                (((0,), (0,)), ((), ())),
                preferred_element_type=F32,
            )
            products.append((b, rows, grad, dot_t(hits, wide_weight[b])))
        for b, rows, grad, part in products:
            hit_grad[b] += grad
            back[clade[b] // 2, rows, :] += part

    each_busy(busy, found, block_count * (cells // CHUNK), add_hits)
    for b in range(block_count):
        terms = hit_grad[b] * wide_weight[b].astype(F32)
        hit_sum[b : b + 1, :] = jnp.sum(terms, axis=0, keepdims=True)
    for o in range(blocks):
        hit_back[o] = back[o].astype(BF16)


def backward_kernel(
    scalars,
    second_weight_in,
    head_weight_in,
    terms_in,
    trunk_in,
    high_in,
    lses_in,
    covariates_t_in,
    first_act_t_in,
    soft_grad_in,
    hit_back_in,
    hit_grad_in,
    hit_sum_in,
    trunk,
    keep,
    send,
    lse,
    second_weight,
    head_weight,
    terms,
    slopes,
    high,
    lses,
    covariates_t,
    first_act_t,
    soft_grad,
    hit_back,
    hit_grad,
    hit_sum,
    wide_weight,
    packed,
    bias,
    weight_cells,
    group_back,
    act_grad,
    fetch_sem,
    term_sem,
):
    first_slope, second_slope = slopes.at[0], slopes.at[1]
    blocks, cells, tile = first_slope.shape
    block_count, slab, _ = head_weight.shape
    first_index, second_index, clade, _, place = scalar_parts(scalars, blocks, block_count)
    early = fetch(
        fetch_sem,
        (lses_in, lses),
        (high_in, high),
        (head_weight_in, head_weight),
    )
    pieces = [pl.ds(i * GROUP, GROUP) for i in range(block_count // GROUP)]
    term_copies = fetch(term_sem, *[(terms_in.at[p], terms.at[p]) for p in pieces])
    early[0].wait()
    early[1].wait()
    lse[...] = join([lses[i] for i in range(lses.shape[0])])
    high[...] = jnp.exp(high[...] - lse[...])
    early[2].wait()
    widen(wide_weight, head_weight, clade)
    group = block_count // 2
    core = place[1]

    act_grad[...] = jnp.zeros_like(act_grad)
    term_copies[0].wait()
    late = fetch(
        fetch_sem.at[pl.ds(len(early), 8)],
        (hit_back_in, hit_back),
        (hit_grad_in, hit_grad),
        (soft_grad_in, soft_grad),
        (trunk_in.at[pl.ds(2, 2)], slopes),
        (first_act_t_in, first_act_t),
        (second_weight_in, second_weight),
        (covariates_t_in, covariates_t),
        (hit_sum_in, hit_sum),
    )
    for i, copy in enumerate(term_copies):
        if i > 0:
            copy.wait()
        for b in range(i * GROUP, (i + 1) * GROUP):
            weights = terms[b].astype(F32) * high[b : b + 1, :]
            weight_cells[b] = weights.astype(BF16)
    for copy in late[:3]:
        copy.wait()
    for o in range(blocks):
        group_back[o] = -hit_back[o].astype(F32)
    for i in range(block_count // GROUP):
        for g in range(GROUP):
            b = i * GROUP + g
            half = pl.ds(pl.multiple_of((clade[b] % 2) * slab, slab), slab)
            rows = slice((b % group) * slab, (b % group + 1) * slab)
            grad = soft_grad[b] * high[b : b + 1, :] - hit_grad[b, half, :]
            packed[b // group, rows, :] = grad
            group_back[clade[b] // 2] += dot_t(weight_cells[b], wide_weight[b])

    for copy in late[3:]:
        copy.wait()
    bias[...] = jnp.zeros_like(bias)
    pair = blocks // (trunk.shape[0] // 2)

    def trunk_sums(o, layer, left, dz):
        part, at = layer * (trunk.shape[0] // 2) + o // pair, o % pair
        trunk[part, at * tile : (at + 1) * tile, :] = dot(left, dz).astype(LINK)
        bias[part, at : at + 1, :] = jnp.sum(dz.astype(F32), axis=0, keepdims=True)

    for o in range(blocks):
        dz = (group_back[o] * second_slope[o].astype(F32)).astype(BF16)
        trunk_sums(o, 1, first_act_t[second_index[o]], dz)
        act_grad[second_index[o]] += dot_t(dz, second_weight[o])
    for o in range(blocks):
        dz = (act_grad[o] * first_slope[o].astype(F32)).astype(BF16)
        trunk_sums(o, 0, covariates_t[first_index[o]], dz)
    for part in range(trunk.shape[0]):
        trunk[part, pair * tile :, :] = bias[part].astype(LINK)

    tail = group * slab
    for half in range(2):
        packed[half, tail:, :] = jnp.zeros((packed.shape[1] - tail, tile), F32)
        packed[half, tail : tail + group, :] = hit_sum[half * group : (half + 1) * group, :]
    keep[...] = packed[core]
    send[...] = packed[1 - core]


def finish_kernel(
    total_cells,
    scalars,
    trunk,
    own,
    other,
    lse,
    species_loss,
    head_grad,
    first_grad,
    first_bias_grad,
    second_grad,
    second_bias_grad,
    halves,
):
    core = scalars[1]
    blocks, tile, _ = first_grad.shape
    block_count, slab, _ = head_grad.shape
    group = block_count // 2
    halves[core] = own[...]
    halves[1 - core] = other[...]
    for b in range(block_count):
        rows = slice((b % group) * slab, (b % group + 1) * slab)
        head_grad[b] = halves[b // group, rows, :].astype(F32)
    tail = group * slab
    for half in range(2):
        rows = slice(half * group, (half + 1) * group)
        hit_mean = halves[half, tail:, :].astype(F32)[:group]
        species_loss[rows, :] = lse[rows, :] - math.log(total_cells) - hit_mean
    half = trunk.shape[0] // 2
    pair = blocks // half
    for layer, (grad, bias_grad) in enumerate(
        ((first_grad, first_bias_grad), (second_grad, second_bias_grad))
    ):
        for part in range(half):
            for at in range(pair):
                rows = slice(at * tile, (at + 1) * tile)
                grad[part * pair + at] = trunk[layer * half + part, rows, :].astype(F32)
            bias = trunk[layer * half + part, pair * tile :, :].astype(F32)
            bias_grad[part * pair : (part + 1) * pair, :] = bias[:pair]


def spread(value, axis, size):
    return lax.all_to_all(jnp.broadcast_to(value[None], (size, *value.shape)), axis, 0, 0)


def forward(
    peers,
    scalars,
    covariates,
    first_weight,
    first_bias,
    second_weight,
    second_bias,
    head_weight,
):
    blocks, tile, _ = first_weight.shape
    block_count, _, species = head_weight.shape
    cells = covariates.shape[0]
    by_clade = (block_count, cells, species)
    by_layer = (4, blocks, cells, tile)
    shape = jax.ShapeDtypeStruct
    return pl.pallas_call(
        forward_kernel,
        name="forward",
        out_shape=(
            shape(by_clade, BF16),
            shape(by_layer, BF16),
            shape((peers, block_count, species), F32),
            shape((block_count, species), F32),
        ),
        in_specs=[SMEM] + [ANY] * 6,
        out_specs=[ANY] * 2 + [VMEM] * 2,
        scratch_shapes=[
            pltpu.VMEM(covariates.shape, BF16),
            pltpu.VMEM(first_weight.shape, BF16),
            pltpu.VMEM((blocks, tile), F32),
            pltpu.VMEM(second_weight.shape, BF16),
            pltpu.VMEM((blocks, tile), F32),
            pltpu.VMEM(head_weight.shape, BF16),
            pltpu.VMEM(by_clade, BF16),
            pltpu.VMEM(by_layer, BF16),
            pltpu.VMEM((block_count, tile, species), BF16),
            pltpu.VMEM((GROUP, cells, species), F32),
            pltpu.VMEM((GROUP, 8, species), F32),
            pltpu.SemaphoreType.DMA((6,)),
            pltpu.SemaphoreType.DMA((block_count // GROUP,)),
            pltpu.SemaphoreType.DMA((1,)),
        ],
        compiler_params=PARAMS,
    )(
        scalars,
        covariates,
        first_weight,
        first_bias.reshape(blocks, tile),
        second_weight,
        second_bias.reshape(blocks, tile),
        head_weight,
    )


def early(scalars, covariates, layers, terms, slab):
    _, blocks, cells, tile = layers.shape
    block_count, _, species = terms.shape
    width = covariates.shape[1]
    shape = jax.ShapeDtypeStruct
    return pl.pallas_call(
        early_kernel,
        name="early",
        out_shape=(
            shape((width // tile, tile, cells), BF16),
            shape((blocks, tile, cells), BF16),
            shape((block_count, slab, species), F32),
        ),
        in_specs=[SMEM] + [ANY] * 3,
        out_specs=[VMEM] * 3,
        scratch_shapes=[
            pltpu.VMEM(covariates.shape, BF16),
            pltpu.VMEM((2, blocks, cells, tile), BF16),
            pltpu.VMEM(terms.shape, BF16),
            pltpu.VMEM((blocks, tile, cells), BF16),
            pltpu.VMEM((GROUP, tile, species), F32),
            pltpu.SemaphoreType.DMA((3,)),
            pltpu.SemaphoreType.DMA((block_count // GROUP,)),
        ],
        compiler_params=PARAMS,
        cost_estimate=pl.CostEstimate(
            flops=2 * terms.size * tile, bytes_accessed=6 * terms.size, transcendentals=0
        ),
    )(scalars, covariates, layers, terms)


def middle(scalars, presence_t, head_weight, layers):
    _, *by_block = layers.shape
    blocks, cells, tile = by_block
    block_count, _, species = head_weight.shape
    shape = jax.ShapeDtypeStruct
    return pl.pallas_call(
        middle_kernel,
        name="middle",
        out_shape=(
            shape(by_block, BF16),
            shape((block_count, tile, species), F32),
            shape((block_count, species), F32),
        ),
        in_specs=[SMEM] + [ANY] * 3,
        out_specs=[VMEM] * 3,
        scratch_shapes=[
            pltpu.VMEM(presence_t.shape, jnp.int32),
            pltpu.VMEM(head_weight.shape, BF16),
            pltpu.VMEM(by_block, BF16),
            pltpu.VMEM((block_count, tile, species), BF16),
            pltpu.VMEM(by_block, F32),
            pltpu.SMEM((block_count * (cells // CHUNK) + AT_ONCE,), jnp.int32),
            pltpu.SemaphoreType.DMA((3,)),
        ],
        compiler_params=PARAMS,
        cost_estimate=pl.CostEstimate(
            flops=8 * block_count * cells * species * tile,
            bytes_accessed=8 * blocks * cells * tile,
            transcendentals=0,
        ),
    )(scalars, presence_t, head_weight, layers)


def backward(
    scalars, second_weight, head_weight, terms, layers, high, lses, ready, hits, nx
):
    covariates_t, first_act_t, soft_grad = ready
    hit_back, hit_grad, hit_sum = hits
    _, *by_block = layers.shape
    blocks, cells, tile = by_block
    block_count, slab, species = head_weight.shape
    shape = jax.ShapeDtypeStruct
    pair = blocks // nx
    part_rows = pair * tile + 8
    group = block_count // 2
    half_rows = group * slab + -(-group // 8) * 8
    return pl.pallas_call(
        backward_kernel,
        name="backward",
        out_shape=(
            shape((2 * nx, part_rows, tile), LINK),
            shape((half_rows, tile), F32),
            shape((half_rows, tile), F32),
            shape((block_count, species), F32),
        ),
        in_specs=[SMEM] + [ANY] * 12,
        out_specs=[VMEM] * 4,
        scratch_shapes=[
            pltpu.VMEM(second_weight.shape, BF16),
            pltpu.VMEM(head_weight.shape, BF16),
            pltpu.VMEM(terms.shape, BF16),
            pltpu.VMEM((2, *by_block), BF16),
            pltpu.VMEM(high.shape, F32),
            pltpu.VMEM(lses.shape, F32),
            pltpu.VMEM(covariates_t.shape, BF16),
            pltpu.VMEM(first_act_t.shape, BF16),
            pltpu.VMEM(soft_grad.shape, F32),
            pltpu.VMEM(by_block, BF16),
            pltpu.VMEM(hit_grad.shape, F32),
            pltpu.VMEM(hit_sum.shape, F32),
            pltpu.VMEM((block_count, tile, species), BF16),
            pltpu.VMEM((2, half_rows, tile), F32),
            pltpu.VMEM((2 * nx, 8, tile), F32),
            pltpu.VMEM(terms.shape, BF16),
            pltpu.VMEM(by_block, F32),
            pltpu.VMEM(by_block, F32),
            pltpu.SemaphoreType.DMA((11,)),
            pltpu.SemaphoreType.DMA((block_count // GROUP,)),
        ],
        compiler_params=PARAMS,
    )(
        scalars,
        second_weight,
        head_weight,
        terms,
        layers,
        high,
        lses,
        covariates_t,
        first_act_t,
        soft_grad,
        hit_back,
        hit_grad,
        hit_sum,
    )


def body(
    covariates,
    first_weight,
    first_bias,
    first_index,
    second_weight,
    second_bias,
    second_index,
    head_weight,
    clade_block,
    presence,
):
    ny, nz, nx = lax.axis_size("y"), lax.axis_size("z"), lax.axis_size("x")
    core, mine = lax.axis_index("c"), lax.axis_index("x")
    swap = [(0, 1), (1, 0)]
    blocks, tile, _ = first_weight.shape
    block_count, slab, species = head_weight.shape
    records = presence.shape[1]
    own_cells, width = covariates.shape
    cells = own_cells * nx
    first_cell = ((lax.axis_index("y") * nz + lax.axis_index("z")) * 2 + core) * cells
    total_cells = ny * nz * 2 * cells

    presence_t = presence.T
    chunk_of = lax.shift_right_arithmetic(presence_t - first_cell, int(math.log2(CHUNK)))
    chunk_of = chunk_of.reshape(records, block_count, species)
    busy = jnp.stack(
        [jnp.any(chunk_of == k, axis=(0, 2)) for k in range(cells // CHUNK)], axis=1
    )
    busy = busy.astype(jnp.int32).reshape(-1)
    place = jnp.stack([first_cell, core]).astype(jnp.int32)
    scalars = jnp.concatenate([place, first_index, second_index, clade_block, busy])

    all_covariates = spread(covariates, "x", nx).reshape(cells, width)
    terms, layers, local_lse, high = forward(
        ny,
        scalars,
        all_covariates,
        first_weight,
        first_bias,
        second_weight,
        second_bias,
        head_weight,
    )
    lses = lax.all_to_all(local_lse, "y", 0, 0)
    ready = early(scalars, all_covariates, layers, terms, slab)
    lses, ready, later = lax.optimization_barrier((join(lses), ready, scalars))
    hits = middle(later, presence_t, head_weight, layers)
    lses = spread(lses, ("z", "c"), nz * 2)
    trunk, keep, send, lse = backward(
        scalars,
        second_weight,
        head_weight,
        terms,
        layers,
        high,
        lses,
        ready,
        hits,
        nx,
    )
    pair, group = blocks // nx, block_count // 2
    head_rows = group * slab
    half_rows = keep.shape[0]

    head = keep + lax.ppermute(send, "c", swap)
    trunk = jnp.sum(lax.all_to_all(trunk, ("c", "x"), 0, 0).astype(F32), axis=0)
    peers = ny * nz
    misc = jnp.concatenate([head[head_rows : head_rows + group], trunk[pair * tile :][:pair]])
    misc = jnp.pad(misc, ((0, peers - misc.shape[0]), (0, 0)))
    trunk_cut, head_cut = pair * tile // peers, head_rows // peers
    cut = jnp.concatenate(
        [
            trunk[: pair * tile].reshape(peers, trunk_cut, tile),
            head[:head_rows].reshape(peers, head_cut, tile),
            misc[:, None],
        ],
        axis=1,
    )
    cut = jnp.pad(cut, ((0, 0), (0, -cut.shape[1] % 8), (0, 0))).astype(LINK)
    cut = jnp.sum(lax.all_to_all(cut, ("y", "z"), 0, 0).astype(F32), axis=0).astype(LINK)

    cut = spread(cut, ("y", "z"), peers)
    misc = cut[:, trunk_cut + head_cut]
    head = jnp.concatenate(
        [
            cut[:, trunk_cut : trunk_cut + head_cut].reshape(head_rows, tile),
            jnp.pad(misc[:group], ((0, -group % 8), (0, 0))),
        ]
    )
    other_head = lax.ppermute(head, "c", swap)
    trunk = jnp.concatenate(
        [
            cut[:, :trunk_cut].reshape(pair * tile, tile),
            jnp.pad(misc[group : group + pair], ((0, -pair % 8), (0, 0))),
        ]
    )
    trunk = spread(trunk, ("c", "x"), 2 * nx)
    shape = jax.ShapeDtypeStruct
    species_loss, head_grad, first_grad, first_bias_grad, second_grad, second_bias_grad = (
        pl.pallas_call(
            functools.partial(finish_kernel, total_cells),
            name="finish",
            out_shape=(
                shape((block_count, species), F32),
                shape(head_weight.shape, F32),
                shape(first_weight.shape, F32),
                shape((blocks, tile), F32),
                shape(second_weight.shape, F32),
                shape((blocks, tile), F32),
            ),
            in_specs=[SMEM] + [VMEM] * 4,
            out_specs=[VMEM] * 6,
            scratch_shapes=[pltpu.VMEM((2, half_rows, tile), LINK)],
            compiler_params=pltpu.CompilerParams(vmem_limit_bytes=16 << 20),
        )(scalars, trunk, head, other_head, lse)
    )
    return (
        species_loss.reshape(-1),
        head_grad,
        first_grad,
        first_bias_grad.reshape(-1),
        second_grad,
        second_bias_grad.reshape(-1),
    )


def solution(mesh):
    devices = mesh.devices.reshape(8, mesh.shape["bg"] // 16, 2, mesh.shape["sp"])
    torus = Mesh(devices, ("y", "z", "c", "x"))
    placed = (
        P(("y", "z", "c", "x"), None),
        P(),
        P(),
        P(),
        P(),
        P(),
        P(),
        P("x", None, None),
        P("x"),
        P("x", None),
    )
    return jax.shard_map(
        body,
        mesh=torus,
        in_specs=placed,
        out_specs=(P("x"), P("x", None, None), P(), P(), P(), P()),
        check_vma=False,
    )
```
